32 devices in a mesh: dp: 16 (over z, x, core), tensor: 2 (over y).
Axes of the slice: x: 2, y: 2, z: 4, core: 2. Of those that a mesh axis runs over, the one named last changes fastest.
Arguments:
- tokens: bfloat16 [16384, 1024], P(('dp', 'tensor')), may hold values from -6 to 6
- doc_ids: int32 [16, 1024], P('dp'), may hold values from 0 to 7, never falling along the last dimension, each value on 1 to 512 neighbouring positions
- gain_attn: float32 [1024], replicated, may hold values from 0.25 to 1.75
- w_q: bfloat16 [1024, 1024], P(None, 'tensor'), may hold values from -0.1875 to 0.1875
- w_kv: bfloat16 [1024, 2, 512], P(None, None, 'tensor'), may hold values from -0.1875 to 0.1875
- q_gain: float32 [64], replicated, may hold values from 0.25 to 1.75
- k_gain: float32 [64], replicated, may hold values from 0.25 to 1.75
- w_o: bfloat16 [1024, 1024], P('tensor'), may hold values from -1.5 to 1.5
- gain_ffn: float32 [1024], replicated, may hold values from 0.25 to 1.75
- w_gu: bfloat16 [1024, 2, 4608], P(None, None, 'tensor'), may hold values from -0.1875 to 0.1875
- w_down: bfloat16 [4608, 1024], P('tensor'), may hold values from -0.09375 to 0.09375
- cotangent: bfloat16 [16384, 1024], P(('dp', 'tensor')), may hold values from -6 to 6
Outputs:
- output: bfloat16 [16384, 1024], P(('dp', 'tensor'))
- grad_tokens: float32 [16384, 1024], P(('dp', 'tensor'))
- grad_gain_attn: float32 [1024], replicated
- grad_w_q: float32 [1024, 1024], P('dp', 'tensor')
- grad_w_kv: float32 [1024, 2, 512], P('dp', None, 'tensor')
- grad_q_gain: float32 [64], replicated
- grad_k_gain: float32 [64], replicated
- grad_w_o: float32 [1024, 1024], P('tensor', 'dp')
- grad_gain_ffn: float32 [1024], replicated
- grad_w_gu: float32 [1024, 2, 4608], P('dp', None, 'tensor')
- grad_w_down: float32 [4608, 1024], P('tensor', 'dp')
The draws below stay inside these ranges and needn't reach their ends.
Inputs may be any that keep to these rules, and one draw needn't show every extreme that they name: In each row of doc_ids the document numbers never fall along the sequence; each document holds 1 to 512 tokens and one holds exactly 512.
All inputs are finite; a program needn't handle non-finite values.
Results may differ from the reference program's by a relative error of at most 0.019.
Values may be sent and summed in bfloat16 or wider, within the bound.
A program may use at most 192 MiB of HBM per device.

```python
import math
import jax
import jax.numpy as jnp
import numpy as np
from jax import lax

D = 1024
H = 16
KVH = 8
HD = 64
FF = 4608
SEQ = 1024
DOCS = 8
MOST_DOC = 512
SEQS = 16
TOKENS = 16384


def raised(values, own_key, source, target, shards_of, factor):
    def block_of(axis_at):
        return (jnp.arange(values.shape[axis_at]) // (values.shape[axis_at] // shards_of)).reshape((-1,) + (1,) * (values.ndim - 1 - axis_at))

    first = jax.random.permutation(own_key, shards_of)[block_of(target)]
    second = (block_of(target) + shards_of // 2) % shards_of
    return jnp.where((block_of(source) == first) | (block_of(source) == second), factor * values, values)


def steps_of(rng, extent, cuts, low, high):
    loudness = 1.0
    for dim, shards_of in cuts:
        heights = jax.random.uniform(jax.random.fold_in(jax.random.fold_in(rng, 6), dim), (shards_of,), jnp.float32, low / len(cuts), high / len(cuts))
        loudness = loudness * jnp.repeat(jnp.exp(heights), extent[dim] // shards_of).reshape((-1,) + (1,) * (len(extent) - 1 - dim))
    return loudness


def length_profile(amount, total, limit, lean):
    portions = [(1 << 20) // math.isqrt(grade ** lean) + 1 for grade in range(2, amount + 1)]
    surplus, given = total - limit - (amount - 1), [1] * (amount - 1)
    while surplus > 0:
        free = [i for i in range(amount - 1) if given[i] < limit]
        whole, budget = sum([portions[i] for i in free]), surplus
        for i in free:
            addition = min(limit - given[i], max(1, budget * portions[i] // whole), surplus)
            given[i] = given[i] + addition
            surplus = surplus - addition
    return np.array([limit] + given)


def ragged(key, count, total, limit, slope):
    if count == 2:
        one = jax.random.randint(key, (), max(1, total - limit), min(limit, total - 1) + 1)
        return jnp.stack([one, total - one])
    tallies = jnp.asarray(length_profile(count, total, limit, slope), jnp.int32)
    pairs = (count - 1) // 2
    source_of, taker = tallies[1:1 + 2 * pairs:2], tallies[2:2 + 2 * pairs:2]
    slack = jnp.minimum(source_of - 1, limit - taker)
    passed = jax.random.randint(jax.random.fold_in(key, 1), (pairs,), 0, 1 << 20) % (slack + 1)
    tallies = tallies.at[1:1 + 2 * pairs:2].set(source_of - passed).at[2:2 + 2 * pairs:2].set(taker + passed)
    return tallies[jax.random.permutation(jax.random.fold_in(key, 2), count)]


def centred(stream_key, dims, spread, limit, pieces=(), kind=jnp.bfloat16):
    values = spread * jax.random.normal(stream_key, dims, jnp.float32)
    if pieces:
        values = values * steps_of(stream_key, dims, pieces, -0.22, 0.18)
    return jnp.clip(values, -limit, limit).astype(kind)


def gaussian_with(own_key, dims, scale, reach, split, heavy, held_as=jnp.bfloat16):
    values = scale * jax.random.normal(own_key, dims, jnp.float32)
    if split:
        values = values * steps_of(own_key, dims, split, -0.22, 0.18)
    return jnp.clip(raised(values, jax.random.fold_in(own_key, 3), *heavy), -reach, reach).astype(held_as)


def setup_inputs(seed: int = 0) -> dict:
    key_list = jax.random.split(jax.random.key(seed), 13)
    tokens = gaussian_with(key_list[0], (TOKENS, D), 1.0, 6.0, ((0, 32),), (0, 1, 32, 2.75))
    doc_ids = jax.vmap(lambda own: jnp.searchsorted(jnp.cumsum(ragged(own, DOCS, SEQ, MOST_DOC, 2)), jnp.arange(SEQ), side="right"))(jax.random.split(key_list[1], SEQS)).reshape((SEQS, SEQ)).astype(jnp.int32)
    gain_attn = jnp.clip(1.0 + 0.15 * jax.random.normal(key_list[2], (D,), jnp.float32), 0.25, 1.75)
    w_q = centred(key_list[3], (D, H * HD), D ** -0.5, 0.1875, ((1, 2),))
    w_kv = centred(key_list[4], (D, 2, KVH * HD), D ** -0.5, 0.1875, ((2, 2),))
    q_gain = jnp.clip(1.0 + 0.15 * jax.random.normal(key_list[5], (HD,), jnp.float32), 0.25, 1.75)
    k_gain = jnp.clip(1.0 + 0.15 * jax.random.normal(key_list[6], (HD,), jnp.float32), 0.25, 1.75)
    w_o = centred(key_list[7], (H * HD, D), (H * HD // 64) ** -0.5, 1.5, ((0, 2),))
    gain_ffn = jnp.clip(1.0 + 0.15 * jax.random.normal(key_list[8], (D,), jnp.float32), 0.25, 1.75)
    w_gu = centred(key_list[9], (D, 2, FF), D ** -0.5, 0.1875, ((2, 2),))
    w_down = centred(key_list[10], (FF, D), FF ** -0.5, 0.09375, ((0, 2),))
    cotangent = gaussian_with(key_list[11], (TOKENS, D), 1.0, 6.0, ((0, 32),), (0, 1, 32, 2.75))
    return dict(tokens=tokens, doc_ids=doc_ids, gain_attn=gain_attn, w_q=w_q, w_kv=w_kv, q_gain=q_gain, k_gain=k_gain, w_o=w_o, gain_ffn=gain_ffn, w_gu=w_gu, w_down=w_down, cotangent=cotangent)


EPS = 1e-06
THETA = 1000000.0
HIGH = lax.Precision.HIGHEST

@jax.custom_vjp
def low(v):
    return lax.optimization_barrier(v.astype(jnp.bfloat16)).astype(jnp.float32)

@jax.custom_vjp
def low_back(v):
    return v

def low_keep(v):
    return (low(v), None)

def low_pass(kept, grad):
    return (grad,)

def back_keep(v):
    return (v, None)

def back_low(kept, grad):
    return (low(grad),)
low.defvjp(low_keep, low_pass)
low_back.defvjp(back_keep, back_low)

def matmul(left, right):
    return jnp.dot(left, right, precision=HIGH, preferred_element_type=jnp.float32)

def normalize(values):
    return values * lax.rsqrt(lax.optimization_barrier(jnp.mean(values * values, axis=-1, keepdims=True)) + EPS)

def rotate(values, cosine_table, sine_table):
    half_dim = values.shape[-1] // 2
    first_half = values[..., :half_dim]
    second_half = values[..., half_dim:]
    return jnp.concatenate([first_half * cosine_table - second_half * sine_table, second_half * cosine_table + first_half * sine_table], -1)

def tables(length):
    half_dim = HD // 2
    frequency = jnp.exp(-math.log(THETA) * 2.0 * jnp.arange(half_dim, dtype=jnp.float32) / HD)
    angles = jnp.arange(length, dtype=jnp.float32)[:, None] * frequency[None, :]
    return (jnp.cos(angles)[:, None, :], jnp.sin(angles)[:, None, :])

def layer(stream, doc_row, params):
    gain_attn, w_q, w_kv, q_gain, k_gain, w_o, gain_ffn, w_gu, w_down = params
    cosine_table, sine_table = tables(SEQ)
    attn_in = low(normalize(stream) * gain_attn)
    q_raw = low_back(matmul(attn_in, w_q)).reshape(SEQ, H, HD)
    kv_raw = low_back(matmul(attn_in, w_kv.reshape(D, 2 * KVH * HD))).reshape(SEQ, 2, KVH, HD)
    queries = low(rotate(normalize(q_raw) * q_gain, cosine_table, sine_table))
    keys = low(rotate(normalize(kv_raw[:, 0]) * k_gain, cosine_table, sine_table))
    values_low = low(kv_raw[:, 1])
    group_size = H // KVH
    keys_wide = jnp.repeat(keys, group_size, axis=1)
    values_wide = jnp.repeat(values_low, group_size, axis=1)
    block_rows = min(512, SEQ)
    key_pos = jnp.arange(SEQ, dtype=jnp.int32)
    score_scale = HD ** (-0.5)

    def attend(first_row):
        q_block = lax.dynamic_slice_in_dim(queries, first_row, block_rows, 0)
        seg_block = lax.dynamic_slice_in_dim(doc_row, first_row, block_rows, 0)
        scores = low_back(jnp.einsum('qhd,khd->hqk', q_block, keys_wide, precision=HIGH) * score_scale)
        query_pos = first_row + jnp.arange(block_rows, dtype=jnp.int32)
        allowed = (key_pos[None, :] <= query_pos[:, None]) & (seg_block[:, None] == doc_row[None, :])
        scores = jnp.where(allowed[None], scores, -1e+30)
        row_max = lax.optimization_barrier(jnp.max(scores, axis=-1, keepdims=True))
        exponent = jnp.exp(scores - row_max)
        probs = exponent / lax.optimization_barrier(jnp.sum(exponent, axis=-1, keepdims=True))
        return jnp.einsum('hqk,khd->qhd', low(probs), values_wide, precision=HIGH)
    starts = jnp.arange(SEQ // block_rows, dtype=jnp.int32) * block_rows
    attended = lax.map(jax.checkpoint(attend), starts).reshape(SEQ, H * HD)
    attended = low(low_back(attended))
    resid = stream + low_back(matmul(attended, w_o))
    ffn_in = low(normalize(resid) * gain_ffn)
    gate_up = low_back(matmul(ffn_in, w_gu.reshape(D, 2 * FF)))
    gate_part = gate_up[:, :FF]
    mixed = low(gate_part * jax.nn.sigmoid(gate_part) * gate_up[:, FF:])
    return resid + low_back(matmul(mixed, w_down))

def reference(tokens, doc_ids, gain_attn, w_q, w_kv, q_gain, k_gain, w_o, gain_ffn, w_gu, w_down, cotangent):
    params = tuple((p.astype(jnp.float32) for p in (gain_attn, w_q, w_kv, q_gain, k_gain, w_o, gain_ffn, w_gu, w_down)))
    stream = tokens.astype(jnp.float32).reshape(SEQS, SEQ, D)

    def forward(stream_all, params_all):

        def one_seq(scanned):
            return layer(scanned[0], scanned[1], params_all)
        return lax.map(jax.checkpoint(one_seq), (stream_all, doc_ids))
    result, pull = jax.vjp(forward, stream, params)
    grad_stream, grads = pull(cotangent.astype(jnp.float32).reshape(SEQS, SEQ, D))
    return (result.reshape(TOKENS, D).astype(jnp.bfloat16), grad_stream.reshape(TOKENS, D), grads[0], grads[1], grads[2], grads[3], grads[4], grads[5], grads[6], grads[7], grads[8])
```

```python
import functools
import math

import jax
import jax.numpy as jnp
from jax import lax
from jax.experimental import pallas as pl
from jax.experimental.pallas import tpu as pltpu
from jax.sharding import PartitionSpec as P

EPS = 1e-06
THETA = 1000000.0
LOG2E = 1.4426950408889634
LN2 = 0.6931471805599453
BLOCK = 256
PAIR = 128
SAME = 256.0
F32 = jnp.float32
BF16 = jnp.bfloat16
VMEM_LIMIT = 56 * 1024 * 1024


def dot_nn(a, b):
    return lax.dot_general(a, b, (((1,), (0,)), ((), ())), preferred_element_type=F32)


def dot_nt(a, b):
    return lax.dot_general(a, b, (((1,), (1,)), ((), ())), preferred_element_type=F32)


def lane_of(shape):
    return lax.broadcasted_iota(jnp.int32, shape, len(shape) - 1)


def head_mean(values):
    high = values.astype(BF16)
    low = (values - high.astype(F32)).astype(BF16)
    row = lax.broadcasted_iota(jnp.int32, (PAIR, PAIR), 0) // 64
    col = lax.broadcasted_iota(jnp.int32, (PAIR, PAIR), 1) // 64
    mean = jnp.where(row == col, 1.0 / 64.0, 0.0).astype(BF16)
    return dot_nn(high, mean) + dot_nn(low, mean)


def swap_halves(values):
    first = lane_of(values.shape) % 64 < 32
    return jnp.where(first, pltpu.roll(values, 96, 1), pltpu.roll(values, 32, 1))


def rope(values, cosine, sine):
    return values * cosine + swap_halves(values) * sine


def row_norm(x):
    return lax.rsqrt(jnp.mean(x * x, axis=-1, keepdims=True) + EPS)


def qkv_kernel(
    x_ref, gain_ref, wq_ref, wk_ref, wv_ref, qg_ref, kg_ref, cos_ref, sin_ref,
    attn_ref, q_ref, kd_ref, vd_ref, qraw_ref, kraw_ref,
):
    x = x_ref[...].astype(F32)
    attn = (x * row_norm(x) * gain_ref[...]).astype(BF16)
    attn_ref[...] = attn
    q = dot_nn(attn, wq_ref[...])
    k = dot_nn(attn, wk_ref[...])
    v = dot_nn(attn, wv_ref[...])
    qraw_ref[...] = q.astype(BF16)
    kraw_ref[...] = k.astype(BF16)
    cosine, sine = cos_ref[...], sin_ref[...]
    for g in range(q.shape[1] // PAIR):
        at = slice(g * PAIR, (g + 1) * PAIR)
        u = q[:, at]
        n = u * lax.rsqrt(head_mean(u * u) + EPS)
        q_ref[:, at] = (rope(n * qg_ref[...], cosine, sine) * (LOG2E / 8.0)).astype(BF16)
    low = lane_of((x.shape[0], PAIR)) < 64
    for p in range(k.shape[1] // PAIR):
        at = slice(p * PAIR, (p + 1) * PAIR)
        u = k[:, at]
        n = u * lax.rsqrt(head_mean(u * u) + EPS)
        roped = rope(n * kg_ref[...], cosine, sine)
        for src, dst in ((roped, kd_ref), (v[:, at], vd_ref)):
            turned = pltpu.roll(src, 64, 1)
            dst[:, 2 * p * PAIR : (2 * p + 1) * PAIR] = jnp.where(low, src, turned).astype(BF16)
            dst[:, (2 * p + 1) * PAIR : (2 * p + 2) * PAIR] = jnp.where(low, turned, src).astype(BF16)


def qkv(x, gain, w_q, w_kv, qg, kg, cosine, sine, half):
    rows, width = x.shape
    qc, kc = w_q.shape[1], w_kv.shape[1] // 2
    nb = rows // BLOCK
    whole = lambda shape, *at: pl.BlockSpec(shape, lambda i: at)
    row = lambda cols: pl.BlockSpec((BLOCK, cols), lambda i: (i, 0))
    table = pl.BlockSpec((BLOCK, PAIR), lambda i: (i + half * nb, 0))
    return pl.pallas_call(
        qkv_kernel,
        grid=(nb,),
        in_specs=[
            row(width), whole((1, width), 0, 0), whole((width, qc), 0, 0),
            whole((width, kc), 0, 0), whole((width, kc), 0, 1),
            whole((1, PAIR), 0, 0), whole((1, PAIR), 0, 0), table, table,
        ],
        out_specs=[row(width), row(qc), row(2 * kc), row(2 * kc), row(qc), row(kc)],
        out_shape=[
            jax.ShapeDtypeStruct((rows, c), BF16) for c in (width, qc, 2 * kc, 2 * kc, qc, kc)
        ],
        compiler_params=pltpu.CompilerParams(vmem_limit_bytes=VMEM_LIMIT),
        cost_estimate=pl.CostEstimate(
            flops=2 * rows * width * (qc + 2 * kc), bytes_accessed=10 * rows * width, transcendentals=0
        ),
        name="qkv",
    )(x, gain, w_q, w_kv, w_kv, qg, kg, cosine, sine)


def attn_fwd_kernel(
    s_ref, q_ref, kown_ref, koth_ref, vown_ref, voth_ref, segq_ref, segk_ref,
    o_ref, linv_ref, kx0, kx1, vx0, vx1, acc,
):
    rows = q_ref.shape[0]
    own = s_ref[0]
    first = s_ref[1]
    nb = rows // BLOCK
    low = lane_of((rows, PAIR)) < 64
    zero = jnp.zeros((rows, PAIR), BF16)

    @pl.when(pl.program_id(0) == 0)
    def _():
        one = jnp.ones((2 * rows, PAIR), F32)
        both = lane_of((2 * rows, PAIR)) < 64
        kx0[:, PAIR:] = segk_ref[...]
        kx1[:, PAIR:] = segk_ref[...]
        vx0[:, PAIR:] = jnp.where(both, one, 0.0).astype(BF16)
        vx1[:, PAIR:] = jnp.where(both, 0.0, one).astype(BF16)

    for part, (k_ref, v_ref) in enumerate(((kown_ref, vown_ref), (koth_ref, voth_ref))):
        at = slice(part * rows, (part + 1) * rows)
        kx0[at, :PAIR] = jnp.where(low, k_ref[...], zero)
        kx1[at, :PAIR] = jnp.where(low, zero, k_ref[...])
        vx0[at, :PAIR] = jnp.where(low, v_ref[...], zero)
        vx1[at, :PAIR] = jnp.where(low, zero, v_ref[...])

    for i in range(nb):
        at = slice(i * BLOCK, (i + 1) * BLOCK)
        q = jnp.concatenate([q_ref[at, :], segq_ref[at, :]], axis=1)
        block = first + i

        def step(kb, diagonal):
            here = pl.ds(pl.multiple_of(lax.rem(kb + own, 2 * nb) * BLOCK, BLOCK), BLOCK)
            total = None
            for kx, vx in ((kx0, vx0), (kx1, vx1)):
                s = dot_nt(q, kx[here, :])
                if diagonal:
                    r = lax.broadcasted_iota(jnp.int32, s.shape, 0)
                    s = jnp.where(lane_of(s.shape) <= r, s, -1e30)
                term = dot_nn(jnp.exp2(s).astype(BF16), vx[here, :])
                total = term if total is None else total + term
            return total

        acc[...] = step(block, True)

        def body(kb, carry):
            acc[...] += step(kb, False)
            return carry

        lax.fori_loop(s_ref[2 + block], block, body, 0)
        inverse = 1.0 / acc[:, PAIR:]
        o_ref[at, :] = (acc[:, :PAIR] * inverse).astype(BF16)
        linv_ref[at, :] = inverse


def attn_fwd(scalars, q, k_own, k_oth, v_own, v_oth, segq, segk, half):
    rows, qc = q.shape
    groups = qc // PAIR
    col = pl.BlockSpec((rows, PAIR), lambda g, s: (0, g))
    return pl.pallas_call(
        attn_fwd_kernel,
        grid_spec=pltpu.PrefetchScalarGridSpec(
            num_scalar_prefetch=1,
            grid=(groups,),
            in_specs=[col] * 5
            + [
                pl.BlockSpec((rows, PAIR), lambda g, s: (half, 0)),
                pl.BlockSpec((2 * rows, PAIR), lambda g, s: (0, 0)),
            ],
            out_specs=[col, col],
            scratch_shapes=[pltpu.VMEM((2 * rows, 2 * PAIR), BF16)] * 4
            + [pltpu.VMEM((BLOCK, 2 * PAIR), F32)],
        ),
        out_shape=[
            jax.ShapeDtypeStruct((rows, qc), BF16),
            jax.ShapeDtypeStruct((rows, qc), F32),
        ],
        compiler_params=pltpu.CompilerParams(vmem_limit_bytes=VMEM_LIMIT),
        cost_estimate=pl.CostEstimate(
            flops=16 * rows * rows * qc, bytes_accessed=12 * rows * qc, transcendentals=0
        ),
        name="attn_fwd",
    )(scalars, q, k_own, k_oth, v_own, v_oth, segq, segk)


def attn_bwd_kernel(
    s_ref, q_own, q_oth, kd_own, kd_oth, vd_own, vd_oth, do_own, do_oth, o_own, o_oth,
    linv_own, linv_oth, qraw_own, qraw_oth, kraw_own, kraw_oth, segq_ref, segk_ref,
    cos_ref, sin_ref, qg_ref, kg_ref,
    gq_own, gq_oth, gk_own, gk_oth, gv_own, gv_oth, qgain_ref, kgain_ref,
    qx, dox, kx0, kx1, vx0, vx1, kt, dqt, dk0, dk1, dv0, dv1, dks, dvs,
):
    rows = q_own.shape[0]
    own = s_ref[0]
    nb = rows // BLOCK
    low = lane_of((rows, PAIR)) < 64
    zero = jnp.zeros((rows, PAIR), BF16)
    parts = (
        (q_own, kd_own, vd_own, do_own, o_own, linv_own),
        (q_oth, kd_oth, vd_oth, do_oth, o_oth, linv_oth),
    )

    @pl.when(pl.program_id(0) == 0)
    def _():
        one = jnp.ones((2 * rows, PAIR), F32)
        both = lane_of((2 * rows, PAIR)) < 64
        qx[:, PAIR:] = segq_ref[...]
        kx0[:, PAIR:] = segk_ref[...]
        kx1[:, PAIR:] = segk_ref[...]
        vx0[:, PAIR:] = jnp.where(both, -one, 0.0).astype(BF16)
        vx1[:, PAIR:] = jnp.where(both, 0.0, -one).astype(BF16)
        qgain_ref[...] = jnp.zeros_like(qgain_ref)
        kgain_ref[...] = jnp.zeros_like(kgain_ref)

    def place(block):
        return pl.ds(pl.multiple_of(lax.rem(block + own, 2 * nb) * BLOCK, BLOCK), BLOCK)

    for gi in range(2):
        lanes = slice(gi * PAIR, (gi + 1) * PAIR)
        for part, (q_ref, k_ref, v_ref, do_ref, o_ref, linv_ref) in enumerate(parts):
            at = slice(part * rows, (part + 1) * rows)
            qx[at, :PAIR] = q_ref[:, lanes]
            k = k_ref[:, lanes]
            kx0[at, :PAIR] = jnp.where(low, k, zero)
            kx1[at, :PAIR] = jnp.where(low, zero, k)
            v = v_ref[:, lanes]
            vx0[at, :PAIR] = jnp.where(low, v, zero)
            vx1[at, :PAIR] = jnp.where(low, zero, v)
            kt[:, at] = jnp.transpose(k.astype(F32))[:64, :].astype(BF16)
            scaled = do_ref[:, lanes].astype(F32) * linv_ref[:, lanes]
            dox[at, :PAIR] = scaled.astype(BF16)
            dox[at, PAIR:] = (scaled * o_ref[:, lanes].astype(F32)).astype(BF16)
        for ref in (dqt, dk0, dk1, dv0, dv1):
            ref[...] = jnp.zeros_like(ref)

        def step(qb, kb, diagonal):
            qs, ks = place(qb), place(kb)
            q, do = qx[qs, :], dox[qs, :]
            for h, (kx, vx, dk, dv) in enumerate(((kx0, vx0, dk0, dv0), (kx1, vx1, dk1, dv1))):
                s = dot_nt(kx[ks, :], q)
                if diagonal:
                    r = lax.broadcasted_iota(jnp.int32, s.shape, 0)
                    s = jnp.where(r <= lane_of(s.shape), s, -1e30)
                e = jnp.exp2(s)
                ds = (e * dot_nt(vx[ks, :], do)).astype(BF16)
                dv[ks, :] += dot_nn(e.astype(BF16), do[:, :PAIR])
                dk[ks, :] += dot_nn(ds, q[:, :PAIR])
                dqt[h * 64 : (h + 1) * 64, qs] += dot_nn(kt[:, ks], ds)

        def q_body(qb, carry):
            step(qb, qb, True)

            def k_body(kb, c):
                step(qb, kb, False)
                return c

            lax.fori_loop(s_ref[2 + qb], qb, k_body, 0)
            return carry

        lax.fori_loop(0, 2 * nb, q_body, 0)

        for part, (g_ref, raw_ref) in enumerate(((gq_own, qraw_own), (gq_oth, qraw_oth))):
            at = slice(part * rows, (part + 1) * rows)
            dq = jnp.transpose(dqt[:, at]) * 0.125
            normed_grad = rope(dq, cos_ref[at, :], -sin_ref[at, :])
            raw = raw_ref[:, lanes].astype(F32)
            inverse = lax.rsqrt(head_mean(raw * raw) + EPS)
            u = raw * inverse
            qgain_ref[...] += jnp.sum(normed_grad * u, axis=0, keepdims=True)
            w = normed_grad * qg_ref[...]
            g_ref[:, lanes] = (inverse * (w - u * head_mean(w * u))).astype(BF16)
            for a, b, total in ((dk0, dk1, dks), (dv0, dv1, dvs)):
                both = jnp.where(low, a[at, :], b[at, :])
                both = both + pltpu.roll(both, 64, 1)
                if gi == 0:
                    total[at, :] = both
                else:
                    total[at, :] = jnp.where(low, total[at, :], both)

    for part, (gk_ref, gv_ref, raw_ref) in enumerate(
        ((gk_own, gv_own, kraw_own), (gk_oth, gv_oth, kraw_oth))
    ):
        at = slice(part * rows, (part + 1) * rows)
        normed_grad = rope(dks[at, :] * LN2, cos_ref[at, :], -sin_ref[at, :])
        raw = raw_ref[...].astype(F32)
        inverse = lax.rsqrt(head_mean(raw * raw) + EPS)
        u = raw * inverse
        kgain_ref[...] += jnp.sum(normed_grad * u, axis=0, keepdims=True)
        w = normed_grad * kg_ref[...]
        gk_ref[...] = (inverse * (w - u * head_mean(w * u))).astype(BF16)
        gv_ref[...] = dvs[at, :].astype(BF16)


def attn_bwd(scalars, pairs, segq, segk, cosine, sine, qg, kg):
    (q, kd, vd, do, o, linv, qraw, kraw) = pairs
    rows, qc = q[0].shape
    kc = kraw[0].shape[1]
    two = pl.BlockSpec((rows, 2 * PAIR), lambda p, s: (0, p))
    one = pl.BlockSpec((rows, PAIR), lambda p, s: (0, p))
    table = pl.BlockSpec((2 * rows, PAIR), lambda p, s: (0, 0))
    gain = pl.BlockSpec((1, PAIR), lambda p, s: (0, 0))
    operands = [a for pair in (q, kd, vd, do, o, linv, qraw, kraw) for a in pair]
    return pl.pallas_call(
        attn_bwd_kernel,
        grid_spec=pltpu.PrefetchScalarGridSpec(
            num_scalar_prefetch=1,
            grid=(qc // (2 * PAIR),),
            in_specs=[two] * 14 + [one] * 2 + [table] * 4 + [gain] * 2,
            out_specs=[two] * 2 + [one] * 4 + [gain] * 2,
            scratch_shapes=[pltpu.VMEM((2 * rows, 2 * PAIR), BF16)] * 6
            + [pltpu.VMEM((64, 2 * rows), BF16), pltpu.VMEM((PAIR, 2 * rows), F32)]
            + [pltpu.VMEM((2 * rows, PAIR), F32)] * 6,
        ),
        out_shape=[jax.ShapeDtypeStruct((rows, qc), BF16)] * 2
        + [jax.ShapeDtypeStruct((rows, kc), BF16)] * 4
        + [jax.ShapeDtypeStruct((1, PAIR), F32)] * 2,
        compiler_params=pltpu.CompilerParams(vmem_limit_bytes=VMEM_LIMIT),
        cost_estimate=pl.CostEstimate(
            flops=80 * rows * rows * qc, bytes_accessed=32 * rows * qc, transcendentals=0
        ),
        name="attn_bwd",
    )(scalars, *operands, segq, segk, cosine, sine, qg, kg)


def resid_kernel(mine_ref, theirs_ref, wm_ref, wt_ref, x_ref, gain_ref, resid_ref, ffn_ref):
    resid = (
        x_ref[...].astype(F32)
        + dot_nn(mine_ref[...], wm_ref[...])
        + dot_nn(theirs_ref[...], wt_ref[...])
    )
    resid_ref[...] = resid
    ffn_ref[...] = (resid * row_norm(resid) * gain_ref[...]).astype(BF16)


def resid_norm(mine, theirs, w_mine, w_theirs, x, gain):
    rows, width = x.shape
    cols = mine.shape[1]
    row = lambda c: pl.BlockSpec((BLOCK, c), lambda i: (i, 0))
    whole = lambda r, c: pl.BlockSpec((r, c), lambda i: (0, 0))
    return pl.pallas_call(
        resid_kernel,
        grid=(rows // BLOCK,),
        in_specs=[row(cols), row(cols), whole(cols, width), whole(cols, width), row(width), whole(1, width)],
        out_specs=[row(width), row(width)],
        out_shape=[jax.ShapeDtypeStruct((rows, width), F32), jax.ShapeDtypeStruct((rows, width), BF16)],
        compiler_params=pltpu.CompilerParams(vmem_limit_bytes=VMEM_LIMIT),
        cost_estimate=pl.CostEstimate(
            flops=4 * rows * width * cols, bytes_accessed=12 * rows * width, transcendentals=0
        ),
        name="resid",
    )(mine, theirs, w_mine, w_theirs, x, gain)


def resid_back_kernel(
    part_ref, recv_ref, resid_ref, cot_ref, gain_ref, wm_ref, wt_ref,
    gres_ref, branch_ref, mine_ref, theirs_ref, gsum_ref,
):
    grad = part_ref[...] + recv_ref[...].astype(F32)
    resid = resid_ref[...]
    inverse = row_norm(resid)
    normed = resid * inverse

    @pl.when(pl.program_id(0) == 0)
    def _():
        gsum_ref[...] = jnp.zeros_like(gsum_ref)

    gsum_ref[...] += jnp.sum(grad * normed, axis=0, keepdims=True)
    w = grad * gain_ref[...]
    gres = cot_ref[...].astype(F32) + inverse * (w - normed * jnp.mean(w * normed, axis=-1, keepdims=True))
    gres_ref[...] = gres
    branch = gres.astype(BF16)
    branch_ref[...] = branch
    theirs_ref[...] = dot_nt(branch, wt_ref[...]).astype(BF16)
    mine_ref[...] = dot_nt(branch, wm_ref[...]).astype(BF16)


def resid_back(part, recv, resid, cot, gain, w_mine, w_theirs):
    rows, width = resid.shape
    cols = w_mine.shape[0]
    row = lambda c: pl.BlockSpec((BLOCK, c), lambda i: (i, 0))
    whole = lambda r, c: pl.BlockSpec((r, c), lambda i: (0, 0))
    return pl.pallas_call(
        resid_back_kernel,
        grid=(rows // BLOCK,),
        in_specs=[row(width)] * 4 + [whole(1, width), whole(cols, width), whole(cols, width)],
        out_specs=[row(width), row(width), row(cols), row(cols), whole(1, width)],
        out_shape=[
            jax.ShapeDtypeStruct((rows, width), F32), jax.ShapeDtypeStruct((rows, width), BF16),
            jax.ShapeDtypeStruct((rows, cols), BF16), jax.ShapeDtypeStruct((rows, cols), BF16),
            jax.ShapeDtypeStruct((1, width), F32),
        ],
        compiler_params=pltpu.CompilerParams(vmem_limit_bytes=VMEM_LIMIT),
        cost_estimate=pl.CostEstimate(
            flops=4 * rows * width * cols, bytes_accessed=16 * rows * width, transcendentals=0
        ),
        name="resid_back",
    )(part, recv, resid, cot, gain, w_mine, w_theirs)


def ffn_kernel(x_ref, c_ref, wg_ref, wu_ref, wd_ref, mixed_ref, gg_ref, gu_ref, y_ref, gf_ref, yacc, gacc):
    x, c = x_ref[...], c_ref[...]
    gate = dot_nn(x, wg_ref[...])
    up = dot_nn(x, wu_ref[...])
    grad = dot_nt(c, wd_ref[...])
    sig = 0.5 * jnp.tanh(0.5 * gate) + 0.5
    silu = gate * sig
    mixed = (silu * up).astype(BF16)
    gg = (grad * up * (sig + silu * (1.0 - sig))).astype(BF16)
    gu = (grad * silu).astype(BF16)
    mixed_ref[...] = mixed
    gg_ref[...] = gg
    gu_ref[...] = gu
    y = dot_nn(mixed, wd_ref[...])
    gf = dot_nt(gg, wg_ref[...]) + dot_nt(gu, wu_ref[...])
    step = pl.program_id(0)

    @pl.when(step == 0)
    def _():
        yacc[...] = y
        gacc[...] = gf

    @pl.when(step > 0)
    def _():
        yacc[...] += y
        gacc[...] += gf

    @pl.when(step == pl.num_programs(0) - 1)
    def _():
        y_ref[...] = yacc[...].astype(y_ref.dtype)
        gf_ref[...] = gacc[...].astype(gf_ref.dtype)


def ffn(x, c, w_gu, w_down, dtype):
    rows, width = x.shape
    hidden = w_down.shape[0]
    tile = BLOCK
    nf = hidden // tile
    whole = pl.BlockSpec((rows, width), lambda f: (0, 0))
    mid = pl.BlockSpec((rows, tile), lambda f: (0, f))
    return pl.pallas_call(
        ffn_kernel,
        grid=(nf,),
        in_specs=[
            whole, whole,
            pl.BlockSpec((width, tile), lambda f: (0, f)),
            pl.BlockSpec((width, tile), lambda f: (0, f + nf)),
            pl.BlockSpec((tile, width), lambda f: (f, 0)),
        ],
        out_specs=[mid, mid, mid, whole, whole],
        out_shape=[jax.ShapeDtypeStruct((rows, hidden), BF16)] * 3
        + [jax.ShapeDtypeStruct((rows, width), dtype)] * 2,
        scratch_shapes=[pltpu.VMEM((rows, width), F32)] * 2,
        compiler_params=pltpu.CompilerParams(vmem_limit_bytes=VMEM_LIMIT),
        cost_estimate=pl.CostEstimate(
            flops=12 * rows * width * hidden, bytes_accessed=6 * width * hidden, transcendentals=0
        ),
        name="ffn",
    )(x, c, w_gu, w_gu, w_down)


def grad_kernel(s_ref, xo_ref, xt_ref, yo_ref, yt_ref, send_ref, keep_ref, turned):
    rows, width = xo_ref.shape
    mine = s_ref[0]

    @pl.when(pl.program_id(0) == 0)
    def _():
        for part, x_ref in enumerate((xo_ref, xt_ref)):
            for k in range(width // PAIR):
                piece = jnp.transpose(x_ref[:, k * PAIR : (k + 1) * PAIR].astype(F32)).astype(BF16)
                for c in range(2):
                    turned[c, k * 64 : (k + 1) * 64, part * rows : (part + 1) * rows] = piece[
                        c * 64 : (c + 1) * 64, :
                    ]

    for which, out_ref in ((1 - mine, send_ref), (mine, keep_ref)):
        left = turned[which]
        out_ref[...] = (
            dot_nn(left[:, :rows], yo_ref[...]) + dot_nn(left[:, rows:], yt_ref[...])
        ).astype(BF16)


def weight_grad(core, x, y, tile):
    rows, width = x[0].shape
    cols = y[0].shape[1]
    whole = pl.BlockSpec((rows, width), lambda f, s: (0, 0))
    right = pl.BlockSpec((rows, tile), lambda f, s: (0, f))
    out = pl.BlockSpec((width // 2, tile), lambda f, s: (0, f))
    return pl.pallas_call(
        grad_kernel,
        grid_spec=pltpu.PrefetchScalarGridSpec(
            num_scalar_prefetch=1,
            grid=(cols // tile,),
            in_specs=[whole, whole, right, right],
            out_specs=[out, out],
            scratch_shapes=[pltpu.VMEM((2, width // 2, 2 * rows), BF16)],
        ),
        out_shape=[jax.ShapeDtypeStruct((width // 2, cols), BF16)] * 2,
        compiler_params=pltpu.CompilerParams(vmem_limit_bytes=VMEM_LIMIT),
        cost_estimate=pl.CostEstimate(
            flops=4 * rows * width * cols, bytes_accessed=6 * rows * cols, transcendentals=0
        ),
        name="weight_grad",
    )(core, x[0], x[1], y[0], y[1])


def attn_in_grad_kernel(
    x_ref, gq_ref, gk_ref, gv_ref, wq_ref, wk_ref, wv_ref, out_ref, gsum_ref
):
    out = dot_nt(gq_ref[...], wq_ref[...]) + dot_nt(gk_ref[...], wk_ref[...]) + dot_nt(gv_ref[...], wv_ref[...])
    out_ref[...] = out.astype(out_ref.dtype)
    x = x_ref[...].astype(F32)

    @pl.when(pl.program_id(0) == 0)
    def _():
        gsum_ref[...] = jnp.zeros_like(gsum_ref)

    gsum_ref[...] += jnp.sum(out * (x * row_norm(x)), axis=0, keepdims=True)


def attn_in_grad(x, gq, gk, gv, w_q, w_kv, dtype):
    rows, width = x.shape
    qc, kc = gq.shape[1], gk.shape[1]
    row = lambda c: pl.BlockSpec((BLOCK, c), lambda i: (i, 0))
    whole = lambda shape, *at: pl.BlockSpec(shape, lambda i: at)
    return pl.pallas_call(
        attn_in_grad_kernel,
        grid=(rows // BLOCK,),
        in_specs=[
            row(width), row(qc), row(kc), row(kc),
            whole((width, qc), 0, 0), whole((width, kc), 0, 0), whole((width, kc), 0, 1),
        ],
        out_specs=[row(width), whole((1, width), 0, 0)],
        out_shape=[jax.ShapeDtypeStruct((rows, width), dtype), jax.ShapeDtypeStruct((1, width), F32)],
        compiler_params=pltpu.CompilerParams(vmem_limit_bytes=VMEM_LIMIT),
        cost_estimate=pl.CostEstimate(
            flops=2 * rows * width * (qc + 2 * kc), bytes_accessed=8 * rows * width, transcendentals=0
        ),
        name="attn_in_grad",
    )(x, gq, gk, gv, w_q, w_kv, w_kv)


def final_kernel(part_ref, recv_ref, x_ref, gres_ref, gain_ref, out_ref):
    x = x_ref[...].astype(F32)
    inverse = row_norm(x)
    normed = x * inverse
    w = (part_ref[...] + recv_ref[...].astype(F32)) * gain_ref[...]
    out_ref[...] = gres_ref[...] + inverse * (w - normed * jnp.mean(w * normed, axis=-1, keepdims=True))


def final(part, recv, x, gres, gain):
    rows, width = x.shape
    row = pl.BlockSpec((PAIR, width), lambda i: (i, 0))
    return pl.pallas_call(
        final_kernel,
        grid=(rows // PAIR,),
        in_specs=[row] * 4 + [pl.BlockSpec((1, width), lambda i: (0, 0))],
        out_specs=row,
        out_shape=jax.ShapeDtypeStruct((rows, width), F32),
        compiler_params=pltpu.CompilerParams(vmem_limit_bytes=VMEM_LIMIT),
        cost_estimate=pl.CostEstimate(flops=10 * rows * width, bytes_accessed=16 * rows * width, transcendentals=0),
        name="final",
    )(part, recv, x, gres, gain)


def swap(value, axis, size, bit):
    return lax.ppermute(value, axis, [(i, i ^ bit) for i in range(size)])


def pick(value, axis, index):
    return lax.dynamic_index_in_dim(value, index, axis, keepdims=False)


def scatter_sum(send, keep, position, size, order):
    received = swap(send, "dp", size, 1)
    blocks = size // 2
    cols = keep.shape[-1]
    rest = [b for b in range(size.bit_length() - 2, 0, -1)]
    shape = (2,) * len(rest) + (keep.shape[0] // blocks, cols)
    keep, received = keep.reshape(shape), received.reshape(shape)
    for bit in order:
        axis = rest.index(bit)
        mine = (position >> bit) & 1

        def half(index):
            total = pick(keep, axis, index).astype(F32) + pick(received, axis, index).astype(F32)
            return total.astype(BF16)

        going, keep = half(1 - mine), half(mine)
        received = swap(going, "dp", size, 1 << bit)
        rest.remove(bit)
    return keep.astype(F32) + received.astype(F32)


def sum_all(value, n_dp, n_tensor):
    for bit in range(n_dp.bit_length() - 1):
        value = value + swap(value, "dp", n_dp, 1 << bit)
    return value + swap(value, "tensor", n_tensor, 1)


def after(value, *others):
    return lax.optimization_barrier((value,) + others)[0]


def paired(
    n_dp, tokens, doc_ids, gain_attn, w_q, w_kv, q_gain, k_gain, w_o, gain_ffn, w_gu, w_down, cotangent
):
    rows, width = tokens.shape
    head_dim = q_gain.shape[0]
    hidden = w_down.shape[0]
    seq = doc_ids.shape[1]
    t = lax.axis_index("tensor")
    d = lax.axis_index("dp")
    over = functools.partial(swap, axis="tensor", size=2, bit=1)

    tokens_oth = over(tokens)
    w_o_oth = over(after(w_o, tokens_oth))
    cot_oth = over(after(cotangent, tokens_oth))

    segment = doc_ids[0]
    nb = seq // BLOCK
    heads_of_blocks = segment.reshape(nb, BLOCK)
    first_doc, last_doc = heads_of_blocks[:, 0], heads_of_blocks[:, -1]
    below = jnp.arange(nb)[None, :] < jnp.arange(nb)[:, None]
    lowest = jnp.sum((below & (last_doc[None, :] < first_doc[:, None])).astype(jnp.int32), axis=1)
    shift = t * (nb // 2)
    table = lambda first: jnp.concatenate([jnp.stack([shift, first]).astype(jnp.int32), lowest])
    scalars_own = table(shift)
    scalars_oth = table(nb // 2 - shift)
    segment = jnp.where(t == 0, segment, jnp.roll(segment, rows))
    lanes = jnp.arange(PAIR, dtype=jnp.int32)[None, :]
    match = lanes == segment[:, None]
    marker = lanes == 8
    segk = (match | marker).astype(BF16)
    segq = (jnp.where(match, SAME, 0.0) - jnp.where(marker, SAME, 0.0)).astype(BF16)
    half_dim = head_dim // 2
    frequency = jnp.exp(-math.log(THETA) * 2.0 * jnp.arange(half_dim, dtype=F32) / head_dim)
    position = (jnp.arange(seq, dtype=jnp.int32) + t * rows) % seq
    angles = position.astype(F32)[:, None] * frequency[None, :]
    cos, sin = jnp.cos(angles), jnp.sin(angles)
    cosine = jnp.concatenate([cos] * 4, axis=1)
    sine = jnp.concatenate([-sin, sin] * 2, axis=1)
    gain1, gain2 = gain_attn.reshape(1, width), gain_ffn.reshape(1, width)
    qg = jnp.concatenate([q_gain, q_gain]).reshape(1, PAIR)
    kg = jnp.concatenate([k_gain, k_gain]).reshape(1, PAIR)
    w_kv = w_kv.reshape(width, -1)
    w_gu = w_gu.reshape(width, 2 * hidden)
    core = (d & 1).astype(jnp.int32).reshape(1)

    attn_own, q_own, kd_own, vd_own, qraw_own, kraw_own = qkv(
        tokens, gain1, w_q, w_kv, qg, kg, cosine, sine, 0
    )
    attn_oth, q_oth, kd_oth, vd_oth, qraw_oth, kraw_oth = qkv(
        tokens_oth, gain1, w_q, w_kv, qg, kg, cosine, sine, 1
    )
    o_oth, linv_oth = attn_fwd(scalars_oth, q_oth, kd_own, kd_oth, vd_own, vd_oth, segq, segk, 1)
    theirs = over(o_oth)
    o_own, linv_own = attn_fwd(scalars_own, q_own, kd_own, kd_oth, vd_own, vd_oth, segq, segk, 0)
    resid, ffn_own = resid_norm(o_own, theirs, w_o, w_o_oth, tokens, gain2)

    ffn_oth = over(ffn_own)
    mixed_own, gg_own, gu_own, y_own, gf_own = ffn(ffn_own, cotangent, w_gu, w_down, F32)
    mixed_oth, gg_oth, gu_oth, y_oth, gf_oth = ffn(ffn_oth, cot_oth, w_gu, w_down, BF16)
    gf_recv = over(gf_oth)
    down = weight_grad(core, (cotangent, cot_oth), (mixed_own, mixed_oth), 768)
    gate = weight_grad(core, (ffn_own, ffn_oth), (gg_own, gg_oth), 768)
    up = weight_grad(core, (ffn_own, ffn_oth), (gu_own, gu_oth), 768)
    gres, branch, do_own, do_send, gain_ffn_part = resid_back(
        gf_own, gf_recv, resid, cotangent, gain2, w_o, w_o_oth
    )
    do_oth = over(do_send)
    branch_oth = over(after(branch, do_oth))
    y_recv = over(after(y_oth, branch_oth))
    output = (resid + y_own + y_recv.astype(F32)).astype(BF16)

    gq_own, gq_oth, gk_own, gk_oth, gv_own, gv_oth, q_gain_part, k_gain_part = attn_bwd(
        scalars_own,
        (
            (q_own, q_oth), (kd_own, kd_oth), (vd_own, vd_oth), (do_own, do_oth), (o_own, o_oth),
            (linv_own, linv_oth), (qraw_own, qraw_oth), (kraw_own, kraw_oth),
        ),
        segq, segk, cosine, sine, qg, kg,
    )
    ga_oth, sum_oth = attn_in_grad(tokens_oth, gq_oth, gk_oth, gv_oth, w_q, w_kv, BF16)
    ga_recv = over(ga_oth)
    ga_own, sum_own = attn_in_grad(tokens, gq_own, gk_own, gv_own, w_q, w_kv, F32)
    out_proj = weight_grad(core, (branch, branch_oth), (o_own, o_oth), 512)
    grad_q = weight_grad(core, (attn_own, attn_oth), (gq_own, gq_oth), 512)
    grad_k = weight_grad(core, (attn_own, attn_oth), (gk_own, gk_oth), 256)
    grad_v = weight_grad(core, (attn_own, attn_oth), (gv_own, gv_oth), 256)
    grad_tokens = final(ga_own, ga_recv, tokens, gres, gain1)

    high = n_dp.bit_length() - 2
    along = list(range(1, high + 1))
    turned = along[1:2] + along[:1] + along[2:]
    shard_down = scatter_sum(*down, d, n_dp, turned)
    shard_gate = scatter_sum(*gate, d, n_dp, along)
    shard_up = scatter_sum(*up, d, n_dp, along)
    shard_o = scatter_sum(*out_proj, d, n_dp, along)
    shard_q = scatter_sum(*grad_q, d, n_dp, along)
    shard_k = scatter_sum(*grad_k, d, n_dp, along)
    shard_v = scatter_sum(*grad_v, d, n_dp, along)
    gains = jnp.concatenate(
        [(sum_own + sum_oth).reshape(-1, PAIR), gain_ffn_part.reshape(-1, PAIR), q_gain_part, k_gain_part]
    )
    gains = sum_all(gains, n_dp, 2)
    m = width // PAIR
    fold = lambda row: row[:head_dim] + row[head_dim:]
    return (
        output,
        grad_tokens,
        gains[:m].reshape(width),
        shard_q,
        jnp.stack([shard_k, shard_v], axis=1),
        fold(gains[2 * m]),
        fold(gains[2 * m + 1]),
        shard_o.T,
        gains[m : 2 * m].reshape(width),
        jnp.stack([shard_gate, shard_up], axis=1),
        shard_down.T,
    )


def normalize(values):
    inverse = lax.rsqrt(jnp.mean(values * values, axis=-1, keepdims=True) + EPS)
    return (values * inverse, inverse)


def norm_back(grad_normed, normed, inverse):
    return inverse * (grad_normed - normed * jnp.mean(grad_normed * normed, axis=-1, keepdims=True))


def rotate(values, cosine_table, sine_table):
    half_dim = values.shape[-1] // 2
    first_half = values[..., :half_dim]
    second_half = values[..., half_dim:]
    return jnp.concatenate(
        [
            first_half * cosine_table - second_half * sine_table,
            second_half * cosine_table + first_half * sine_table,
        ],
        -1,
    )


def shards(
    tokens, doc_ids, gain_attn, w_q, w_kv, q_gain, k_gain, w_o, gain_ffn, w_gu, w_down, cotangent
):
    f32 = jnp.float32
    bf16 = jnp.bfloat16
    rows_dev, model_width = tokens.shape
    head_dim = q_gain.shape[0]
    q_cols = w_q.shape[1]
    q_heads = q_cols // head_dim
    kv_cols = w_kv.shape[2]
    kv_heads = kv_cols // head_dim
    group_size = q_heads // kv_heads
    hidden = w_gu.shape[2]
    seq_len = doc_ids.shape[1]
    segment = doc_ids[0]
    block_rows = min(512, seq_len)
    blocks = seq_len // block_rows
    score_scale = head_dim ** (-0.5)
    w_kv_flat = w_kv.reshape(model_width, 2 * kv_cols)
    w_gu_flat = w_gu.reshape(model_width, 2 * hidden)
    half_dim = head_dim // 2
    frequency = jnp.exp(-math.log(THETA) * 2.0 * jnp.arange(half_dim, dtype=f32) / head_dim)
    angles = jnp.arange(seq_len, dtype=f32)[:, None] * frequency[None, :]
    cosine_table = jnp.cos(angles)[:, None, :]
    sine_table = jnp.sin(angles)[:, None, :]
    key_pos = jnp.arange(seq_len, dtype=jnp.int32)
    x_float = tokens.astype(f32)
    normed1, inverse1 = normalize(x_float)
    attn_in = (normed1 * gain_attn).astype(bf16)
    attn_all = lax.all_gather(attn_in, "tensor", axis=0, tiled=True)
    q_raw = jnp.dot(attn_all, w_q, preferred_element_type=f32).reshape(seq_len, q_heads, head_dim)
    kv_raw = jnp.dot(attn_all, w_kv_flat, preferred_element_type=f32).reshape(
        seq_len, 2, kv_heads, head_dim
    )
    q_normed, q_inverse = normalize(q_raw)
    k_normed, k_inverse = normalize(kv_raw[:, 0])
    queries = rotate(q_normed * q_gain, cosine_table, sine_table).astype(bf16)
    queries = queries.reshape(seq_len, kv_heads, group_size, head_dim)
    keys = rotate(k_normed * k_gain, cosine_table, sine_table).astype(bf16)
    values_low = kv_raw[:, 1].astype(bf16)

    def scores_of(first_row):
        q_block = lax.dynamic_slice_in_dim(queries, first_row, block_rows, 0)
        seg_block = lax.dynamic_slice_in_dim(segment, first_row, block_rows, 0)
        raw_scores = (
            jnp.einsum("qhgd,thd->hgqt", q_block, keys, preferred_element_type=f32) * score_scale
        )
        query_pos = first_row + jnp.arange(block_rows, dtype=jnp.int32)
        allowed = (key_pos[None, :] <= query_pos[:, None]) & (
            seg_block[:, None] == segment[None, :]
        )
        return (jnp.where(allowed, raw_scores, -1e30), q_block)

    def attend(first_row):
        masked, q_block = scores_of(first_row)
        row_max = jnp.max(masked, axis=-1, keepdims=True)
        exponent = jnp.exp(masked - row_max)
        denominator = jnp.sum(exponent, axis=-1, keepdims=True)
        probs = (exponent / denominator).astype(bf16)
        attended_block = jnp.einsum("hgqt,thd->qhgd", probs, values_low, preferred_element_type=f32)
        return (attended_block, (row_max + jnp.log(denominator))[..., 0])

    starts = jnp.arange(blocks, dtype=jnp.int32) * block_rows
    attended, log_sums = lax.map(attend, starts)
    attended_low = attended.reshape(seq_len, q_cols).astype(bf16)
    resid = x_float + lax.psum_scatter(
        jnp.dot(attended_low, w_o, preferred_element_type=f32),
        "tensor",
        scatter_dimension=0,
        tiled=True,
    )
    normed2, inverse2 = normalize(resid)
    ffn_in = (normed2 * gain_ffn).astype(bf16)
    ffn_all = lax.all_gather(ffn_in, "tensor", axis=0, tiled=True)
    gate_up = jnp.dot(ffn_all, w_gu_flat, preferred_element_type=f32)
    gate_part = gate_up[:, :hidden]
    up_part = gate_up[:, hidden:]
    sigmoid_gate = jax.nn.sigmoid(gate_part)
    silu_gate = gate_part * sigmoid_gate
    mixed = (silu_gate * up_part).astype(bf16)
    result = resid + lax.psum_scatter(
        jnp.dot(mixed, w_down, preferred_element_type=f32).astype(jnp.bfloat16),
        "tensor",
        scatter_dimension=0,
        tiled=True,
    ).astype(jnp.float32)
    output = result.astype(bf16)
    grad_all = lax.all_gather(cotangent, "tensor", axis=0, tiled=True)
    grad_down = jnp.einsum("sf,sd->fd", mixed, grad_all, preferred_element_type=f32)
    grad_mixed = jnp.einsum("sd,fd->sf", grad_all, w_down, preferred_element_type=f32)
    grad_gate = grad_mixed * up_part * sigmoid_gate * (1.0 + gate_part * (1.0 - sigmoid_gate))
    grad_up = grad_mixed * silu_gate
    grad_gu = jnp.concatenate([grad_gate, grad_up], 1).astype(bf16)
    grad_w_gu = jnp.einsum("sd,sf->df", ffn_all, grad_gu, preferred_element_type=f32).reshape(
        model_width, 2, hidden
    )
    grad_ffn_in = lax.psum_scatter(
        jnp.einsum("sf,df->sd", grad_gu, w_gu_flat, preferred_element_type=f32).astype(
            jnp.bfloat16
        ),
        "tensor",
        scatter_dimension=0,
        tiled=True,
    ).astype(jnp.float32)
    gain_ffn_part = jnp.sum(grad_ffn_in * normed2, axis=0)
    grad_resid = cotangent.astype(f32) + norm_back(grad_ffn_in * gain_ffn, normed2, inverse2)
    branch_all = lax.all_gather(grad_resid.astype(bf16), "tensor", axis=0, tiled=True)
    grad_w_o = jnp.einsum("sc,sd->cd", attended_low, branch_all, preferred_element_type=f32)
    grad_attended = jnp.einsum("sd,cd->sc", branch_all, w_o, preferred_element_type=f32).astype(
        bf16
    )
    grad_attended = grad_attended.reshape(seq_len, kv_heads, group_size, head_dim)

    def attend_back(carried, scanned):
        first_row, lse_block = scanned
        masked, q_block = scores_of(first_row)
        probs = jnp.exp(masked - lse_block[..., None])
        go_block = lax.dynamic_slice_in_dim(grad_attended, first_row, block_rows, 0)
        grad_probs = jnp.einsum("qhgd,thd->hgqt", go_block, values_low, preferred_element_type=f32)
        grad_scores = (
            probs * (grad_probs - jnp.sum(probs * grad_probs, axis=-1, keepdims=True))
        ).astype(bf16)
        keys_next = carried[0] + score_scale * jnp.einsum(
            "hgqt,qhgd->thd", grad_scores, q_block, preferred_element_type=f32
        )
        values_next = carried[1] + jnp.einsum(
            "hgqt,qhgd->thd", probs.astype(bf16), go_block, preferred_element_type=f32
        )
        grad_q_block = score_scale * jnp.einsum(
            "hgqt,thd->qhgd", grad_scores, keys, preferred_element_type=f32
        )
        return ((keys_next, values_next), grad_q_block)

    zero_kv = jnp.zeros((seq_len, kv_heads, head_dim), f32)
    (grad_keys, grad_values), grad_queries = lax.scan(
        attend_back, (zero_kv, zero_kv), (starts, log_sums)
    )
    grad_q_normed = rotate(
        grad_queries.reshape(seq_len, q_heads, head_dim), cosine_table, -sine_table
    )
    q_gain_part = jnp.sum(grad_q_normed * q_normed, axis=(0, 1))
    grad_q_raw = (
        norm_back(grad_q_normed * q_gain, q_normed, q_inverse).astype(bf16).reshape(seq_len, q_cols)
    )
    grad_k_normed = rotate(grad_keys, cosine_table, -sine_table)
    k_gain_part = jnp.sum(grad_k_normed * k_normed, axis=(0, 1))
    grad_k_raw = (
        norm_back(grad_k_normed * k_gain, k_normed, k_inverse)
        .astype(bf16)
        .reshape(seq_len, kv_cols)
    )
    grad_kv = jnp.concatenate([grad_k_raw, grad_values.astype(bf16).reshape(seq_len, kv_cols)], 1)
    grad_w_q = jnp.einsum("sd,sc->dc", attn_all, grad_q_raw, preferred_element_type=f32)
    grad_w_kv = jnp.einsum("sd,sc->dc", attn_all, grad_kv, preferred_element_type=f32).reshape(
        model_width, 2, kv_cols
    )
    grad_attn_in = lax.psum_scatter(
        (
            jnp.einsum("sc,dc->sd", grad_q_raw, w_q, preferred_element_type=f32)
            + jnp.einsum("sc,dc->sd", grad_kv, w_kv_flat, preferred_element_type=f32)
        ).astype(jnp.bfloat16),
        "tensor",
        scatter_dimension=0,
        tiled=True,
    ).astype(jnp.float32)
    gain_attn_part = jnp.sum(grad_attn_in * normed1, axis=0)
    grad_tokens = grad_resid + norm_back(grad_attn_in * gain_attn, normed1, inverse1)
    gain_sums = lax.psum(
        (gain_attn_part, gain_ffn_part, q_gain_part, k_gain_part), ("dp", "tensor")
    )
    shard_q, shard_kv, shard_o, shard_gu, shard_down = (
        lax.psum_scatter(
            grad_w_q.astype(jnp.bfloat16), "dp", scatter_dimension=0, tiled=True
        ).astype(jnp.float32),
        lax.psum_scatter(
            grad_w_kv.astype(jnp.bfloat16), "dp", scatter_dimension=0, tiled=True
        ).astype(jnp.float32),
        lax.psum_scatter(
            grad_w_o.astype(jnp.bfloat16), "dp", scatter_dimension=1, tiled=True
        ).astype(jnp.float32),
        lax.psum_scatter(
            grad_w_gu.astype(jnp.bfloat16), "dp", scatter_dimension=0, tiled=True
        ).astype(jnp.float32),
        lax.psum_scatter(
            grad_down.astype(jnp.bfloat16), "dp", scatter_dimension=1, tiled=True
        ).astype(jnp.float32),
    )
    return (
        output,
        grad_tokens,
        gain_sums[0],
        shard_q,
        shard_kv,
        gain_sums[2],
        gain_sums[3],
        shard_o,
        gain_sums[1],
        shard_gu,
        shard_down,
    )


def solution(mesh):
    in_specs = (
        P(("dp", "tensor"), None),
        P("dp", None),
        P(),
        P(None, "tensor"),
        P(None, None, "tensor"),
        P(),
        P(),
        P("tensor", None),
        P(),
        P(None, None, "tensor"),
        P("tensor", None),
        P(("dp", "tensor"), None),
    )
    out_specs = (
        P(("dp", "tensor"), None),
        P(("dp", "tensor"), None),
        P(),
        P("dp", "tensor"),
        P("dp", None, "tensor"),
        P(),
        P(),
        P("tensor", "dp"),
        P(),
        P("dp", None, "tensor"),
        P("tensor", "dp"),
    )
    paired_axes = mesh.shape["tensor"] == 2 and mesh.shape["dp"] == 16
    body = functools.partial(paired, mesh.shape["dp"]) if paired_axes else shards
    return jax.shard_map(body, mesh=mesh, in_specs=in_specs, out_specs=out_specs, check_vma=False)
```

```python
import functools
import math

import jax
import jax.numpy as jnp
from jax import lax
from jax.experimental import pallas as pl
from jax.experimental.pallas import tpu as pltpu
from jax.sharding import PartitionSpec as P

EPS = 1e-06
THETA = 1000000.0
LOG2E = 1.4426950408889634
LN2 = 0.6931471805599453
BLOCK = 256
PAIR = 128
SAME = 256.0
F32 = jnp.float32
BF16 = jnp.bfloat16
COST_RATE = 1.0e13
VMEM_LIMIT = 56 * 1024 * 1024
BACK_VMEM = 61 * 1024 * 1024


def dot_nn(a, b):
    return lax.dot_general(a, b, (((1,), (0,)), ((), ())), preferred_element_type=F32)


def dot_nt(a, b):
    return lax.dot_general(a, b, (((1,), (1,)), ((), ())), preferred_element_type=F32)


def cost(seconds):
    return pl.CostEstimate(flops=int(seconds * COST_RATE), bytes_accessed=0, transcendentals=0)


def lane_of(shape):
    return lax.broadcasted_iota(jnp.int32, shape, len(shape) - 1)


def head_mean(values):
    high = values.astype(BF16)
    low = (values - high.astype(F32)).astype(BF16)
    row = lax.broadcasted_iota(jnp.int32, (PAIR, PAIR), 0) // 64
    col = lax.broadcasted_iota(jnp.int32, (PAIR, PAIR), 1) // 64
    mean = jnp.where(row == col, 1.0 / 64.0, 0.0).astype(BF16)
    return dot_nn(high, mean) + dot_nn(low, mean)


def swap_halves(values):
    first = lane_of(values.shape) % 64 < 32
    return jnp.where(first, pltpu.roll(values, 96, 1), pltpu.roll(values, 32, 1))


def rope(values, cosine, sine):
    return values * cosine + swap_halves(values) * sine


def row_norm(x):
    return lax.rsqrt(jnp.mean(x * x, axis=-1, keepdims=True) + EPS)


def qkv_kernel(
    x_ref, gain_ref, wq_ref, wk_ref, wv_ref, qg_ref, kg_ref, cos_ref, sin_ref,
    attn_ref, q_ref, kd_ref, vd_ref, qraw_ref, kraw_ref,
):
    x = x_ref[...].astype(F32)
    attn = (x * row_norm(x) * gain_ref[...]).astype(BF16)
    attn_ref[...] = attn
    q = dot_nn(attn, wq_ref[...])
    k = dot_nn(attn, wk_ref[...])
    v = dot_nn(attn, wv_ref[...])
    qraw_ref[...] = q.astype(BF16)
    kraw_ref[...] = k.astype(BF16)
    cosine, sine = cos_ref[...], sin_ref[...]
    for g in range(q.shape[1] // PAIR):
        at = slice(g * PAIR, (g + 1) * PAIR)
        u = q[:, at]
        n = u * lax.rsqrt(head_mean(u * u) + EPS)
        q_ref[:, at] = (rope(n * qg_ref[...], cosine, sine) * (LOG2E / 8.0)).astype(BF16)
    low = lane_of((x.shape[0], PAIR)) < 64
    for p in range(k.shape[1] // PAIR):
        at = slice(p * PAIR, (p + 1) * PAIR)
        u = k[:, at]
        n = u * lax.rsqrt(head_mean(u * u) + EPS)
        roped = rope(n * kg_ref[...], cosine, sine)
        for src, dst in ((roped, kd_ref), (v[:, at], vd_ref)):
            turned = pltpu.roll(src, 64, 1)
            dst[:, 2 * p * PAIR : (2 * p + 1) * PAIR] = jnp.where(low, src, turned).astype(BF16)
            dst[:, (2 * p + 1) * PAIR : (2 * p + 2) * PAIR] = jnp.where(low, turned, src).astype(BF16)


def qkv(x, gain, w_q, w_kv, qg, kg, cosine, sine, half):
    rows, width = x.shape
    qc, kc = w_q.shape[1], w_kv.shape[1] // 2
    nb = rows // BLOCK
    whole = lambda shape, *at: pl.BlockSpec(shape, lambda i: at)
    row = lambda cols: pl.BlockSpec((BLOCK, cols), lambda i: (i, 0))
    table = pl.BlockSpec((BLOCK, PAIR), lambda i: (i + half * nb, 0))
    return pl.pallas_call(
        qkv_kernel,
        grid=(nb,),
        in_specs=[
            row(width), whole((1, width), 0, 0), whole((width, qc), 0, 0),
            whole((width, kc), 0, 0), whole((width, kc), 0, 1),
            whole((1, PAIR), 0, 0), whole((1, PAIR), 0, 0), table, table,
        ],
        out_specs=[row(width), row(qc), row(2 * kc), row(2 * kc), row(qc), row(kc)],
        out_shape=[
            jax.ShapeDtypeStruct((rows, c), BF16) for c in (width, qc, 2 * kc, 2 * kc, qc, kc)
        ],
        compiler_params=pltpu.CompilerParams(vmem_limit_bytes=VMEM_LIMIT),
        cost_estimate=cost(5e-6),
        name="qkv",
    )(x, gain, w_q, w_kv, w_kv, qg, kg, cosine, sine)


def attn_fwd_kernel(
    s_ref, q_ref, kown_ref, koth_ref, vown_ref, voth_ref, segq_ref, segk_ref,
    o_ref, linv_ref, kx0, kx1, vx0, vx1, acc,
):
    rows = q_ref.shape[0]
    own = s_ref[0]
    first = s_ref[1]
    nb = rows // BLOCK
    low = lane_of((rows, PAIR)) < 64
    zero = jnp.zeros((rows, PAIR), BF16)

    @pl.when(pl.program_id(0) == 0)
    def _():
        one = jnp.ones((2 * rows, PAIR), F32)
        both = lane_of((2 * rows, PAIR)) < 64
        kx0[:, PAIR:] = segk_ref[...]
        kx1[:, PAIR:] = segk_ref[...]
        vx0[:, PAIR:] = jnp.where(both, one, 0.0).astype(BF16)
        vx1[:, PAIR:] = jnp.where(both, 0.0, one).astype(BF16)

    for part, (k_ref, v_ref) in enumerate(((kown_ref, vown_ref), (koth_ref, voth_ref))):
        at = slice(part * rows, (part + 1) * rows)
        kx0[at, :PAIR] = jnp.where(low, k_ref[...], zero)
        kx1[at, :PAIR] = jnp.where(low, zero, k_ref[...])
        vx0[at, :PAIR] = jnp.where(low, v_ref[...], zero)
        vx1[at, :PAIR] = jnp.where(low, zero, v_ref[...])

    for i in range(nb):
        at = slice(i * BLOCK, (i + 1) * BLOCK)
        q = jnp.concatenate([q_ref[at, :], segq_ref[at, :]], axis=1)
        block = first + i

        def step(kb, diagonal):
            here = pl.ds(pl.multiple_of(lax.rem(kb + own, 2 * nb) * BLOCK, BLOCK), BLOCK)
            total = None
            for kx, vx in ((kx0, vx0), (kx1, vx1)):
                s = dot_nt(q, kx[here, :])
                if diagonal:
                    r = lax.broadcasted_iota(jnp.int32, s.shape, 0)
                    s = jnp.where(lane_of(s.shape) <= r, s, -1e30)
                term = dot_nn(jnp.exp2(s).astype(BF16), vx[here, :])
                total = term if total is None else total + term
            return total

        acc[...] = step(block, True)

        def body(kb, carry):
            acc[...] += step(kb, False)
            return carry

        lax.fori_loop(s_ref[2 + block], block, body, 0)
        inverse = 1.0 / acc[:, PAIR:]
        o_ref[at, :] = (acc[:, :PAIR] * inverse).astype(BF16)
        linv_ref[at, :] = inverse


def attn_fwd(scalars, q, k_own, k_oth, v_own, v_oth, segq, segk, half):
    rows, qc = q.shape
    groups = qc // PAIR
    col = pl.BlockSpec((rows, PAIR), lambda g, s: (0, g))
    return pl.pallas_call(
        attn_fwd_kernel,
        grid_spec=pltpu.PrefetchScalarGridSpec(
            num_scalar_prefetch=1,
            grid=(groups,),
            in_specs=[col] * 5
            + [
                pl.BlockSpec((rows, PAIR), lambda g, s: (half, 0)),
                pl.BlockSpec((2 * rows, PAIR), lambda g, s: (0, 0)),
            ],
            out_specs=[col, col],
            scratch_shapes=[pltpu.VMEM((2 * rows, 2 * PAIR), BF16)] * 4
            + [pltpu.VMEM((BLOCK, 2 * PAIR), F32)],
        ),
        out_shape=[
            jax.ShapeDtypeStruct((rows, qc), BF16),
            jax.ShapeDtypeStruct((rows, qc), F32),
        ],
        compiler_params=pltpu.CompilerParams(vmem_limit_bytes=VMEM_LIMIT),
        cost_estimate=cost(10e-6),
        name="attn_fwd",
    )(scalars, q, k_own, k_oth, v_own, v_oth, segq, segk)


def resid_kernel(mine_ref, theirs_ref, wm_ref, wt_ref, x_ref, gain_ref, resid_ref, ffn_ref):
    resid = (
        x_ref[...].astype(F32)
        + dot_nn(mine_ref[...], wm_ref[...])
        + dot_nn(theirs_ref[...], wt_ref[...])
    )
    resid_ref[...] = resid
    ffn_ref[...] = (resid * row_norm(resid) * gain_ref[...]).astype(BF16)


def resid_norm(mine, theirs, w_mine, w_theirs, x, gain):
    rows, width = x.shape
    cols = mine.shape[1]
    row = lambda c: pl.BlockSpec((BLOCK, c), lambda i: (i, 0))
    whole = lambda r, c: pl.BlockSpec((r, c), lambda i: (0, 0))
    return pl.pallas_call(
        resid_kernel,
        grid=(rows // BLOCK,),
        in_specs=[row(cols), row(cols), whole(cols, width), whole(cols, width), row(width), whole(1, width)],
        out_specs=[row(width), row(width)],
        out_shape=[jax.ShapeDtypeStruct((rows, width), F32), jax.ShapeDtypeStruct((rows, width), BF16)],
        compiler_params=pltpu.CompilerParams(vmem_limit_bytes=VMEM_LIMIT),
        cost_estimate=cost(4e-6),
        name="resid",
    )(mine, theirs, w_mine, w_theirs, x, gain)


def ffn_kernel(x_ref, c_ref, wg_ref, wu_ref, wd_ref, h_ref, y_ref, gf_ref, yacc, gacc):
    x, c = x_ref[...], c_ref[...]
    gate = dot_nn(x, wg_ref[...])
    up = dot_nn(x, wu_ref[...])
    grad = dot_nt(c, wd_ref[...])
    sig = 0.5 * jnp.tanh(0.5 * gate) + 0.5
    silu = gate * sig
    mixed = (silu * up).astype(BF16)
    gg = (grad * up * (sig + silu * (1.0 - sig))).astype(BF16)
    gu = (grad * silu).astype(BF16)
    for i, value in enumerate((mixed, gg, gu)):
        h_ref[i] = value
    y = dot_nn(mixed, wd_ref[...])
    gf = dot_nt(gg, wg_ref[...]) + dot_nt(gu, wu_ref[...])
    step = pl.program_id(0)

    @pl.when(step == 0)
    def _():
        yacc[...] = y
        gacc[...] = gf

    @pl.when(step > 0)
    def _():
        yacc[...] += y
        gacc[...] += gf

    @pl.when(step == pl.num_programs(0) - 1)
    def _():
        y_ref[...] = yacc[...].astype(y_ref.dtype)
        gf_ref[...] = gacc[...].astype(gf_ref.dtype)


def ffn(x, c, w_gu, w_down, dtype):
    rows, width = x.shape
    hidden = w_down.shape[0]
    tile = CHUNK
    nf = hidden // tile
    whole = pl.BlockSpec((rows, width), lambda f: (0, 0))
    mid = pl.BlockSpec((3, rows, tile), lambda f: (0, 0, f))
    return pl.pallas_call(
        ffn_kernel,
        grid=(nf,),
        in_specs=[
            whole, whole,
            pl.BlockSpec((width, tile), lambda f: (0, f)),
            pl.BlockSpec((width, tile), lambda f: (0, f + nf)),
            pl.BlockSpec((tile, width), lambda f: (f, 0)),
        ],
        out_specs=[mid, whole, whole],
        out_shape=[jax.ShapeDtypeStruct((3, rows, hidden), BF16)]
        + [jax.ShapeDtypeStruct((rows, width), dtype)] * 2,
        scratch_shapes=[pltpu.VMEM((rows, width), F32)] * 2,
        compiler_params=pltpu.CompilerParams(vmem_limit_bytes=VMEM_LIMIT),
        cost_estimate=cost(20e-6),
        name="ffn",
    )(x, c, w_gu, w_gu, w_down)


MESH = pl.DeviceIdType.MESH
CHUNK = 768
SPLIT = 512
BITS = 3


def dot_tn(a, b):
    return lax.dot_general(a, b, (((0,), (0,)), ((), ())), preferred_element_type=F32)


BACK_INPUTS = (
    "h_own", "h_oth", "cot_own", "cot_oth", "ffn_own", "ffn_oth", "attn_own", "attn_oth", "tok_own", "tok_oth",
    "gf_own", "gf_send", "y_own", "y_send", "resid", "wo_mine", "wo_oth", "w_q", "w_kv",
    "q_own", "q_oth", "kd_own", "kd_oth", "vd_own", "vd_oth", "o_own", "o_oth", "linv_own", "linv_oth",
    "qraw_own", "qraw_oth", "kraw_own", "kraw_oth",
)
BACK_TABLES = ("segq", "segk", "cos", "sin", "gain1", "gain2", "qg", "kg")
BACK_OUTPUTS = ("output", "grad_tokens", "shards", "gains", "y_recv")


class Names:
    def __init__(self, names, refs):
        self.__dict__.update(zip(names, refs))


def back_kernel(n_dp, scratch_names, *refs):
    m = Names(BACK_INPUTS + BACK_TABLES + BACK_OUTPUTS + scratch_names, refs)
    rows, width = m.resid.shape
    hidden = m.h_own.shape[2]
    per_x = hidden // CHUNK
    n_wide = 3 * per_x
    n_chunks = n_wide + 2
    nb = 2 * rows // BLOCK
    t = lax.axis_index("tensor")
    d = lax.axis_index("dp")
    core = lax.rem(d, 2)
    x = lax.rem(d // 2, 2)
    zl = lax.rem(d // 4, 2)
    zh = d // 8
    over_t = {"tensor": 1 - t}
    over_core = {"dp": d + 1 - 2 * core}
    over_x = {"dp": d + 2 - 4 * x}
    over_zl = {"dp": d + 4 - 8 * zl}
    over_zh = {"dp": d + 8 - 16 * zh}
    partners = (over_t, over_core, over_x, over_zl, over_zh)
    low = lane_of((rows, PAIR)) < 64
    own_rows, oth_rows = pl.ds(0, rows), pl.ds(rows, rows)

    barrier = pltpu.get_barrier_semaphore()
    for p in partners:
        pl.semaphore_signal(barrier, inc=1, device_id=p, device_id_type=MESH)
    pl.semaphore_wait(barrier, len(partners))

    def tensor_copy(i, src, dst):
        return pltpu.make_async_remote_copy(
            src_ref=src, dst_ref=dst, send_sem=m.t_send.at[i], recv_sem=m.t_recv.at[i],
            device_id=over_t, device_id_type=MESH,
        )

    gf_copy = tensor_copy(0, m.gf_send, m.gf_recv)
    do_copy = tensor_copy(1, m.do_send, m.do_recv)
    branch_copy = tensor_copy(2, m.branch, m.branch_recv)
    y_copy = tensor_copy(3, m.y_send, m.y_recv)
    ga_copy = tensor_copy(4, m.branch, m.gf_recv)

    def rs_copy(stage, c, src, dst, device):
        return pltpu.make_async_remote_copy(
            src_ref=src, dst_ref=dst, send_sem=m.rs_send.at[stage, c], recv_sem=m.rs_recv.at[stage, c],
            device_id=device, device_id_type=MESH,
        )

    left, right = pl.ds(0, SPLIT), pl.ds(SPLIT, CHUNK - SPLIT)
    every = pl.ds(0, 2)
    block_rows = m.sums.shape[4]
    full_rows = pl.ds(0, block_rows)

    def core_copy(c):
        return rs_copy(0, c, m.core_send.at[lax.rem(c, 2)], m.sums.at[c], over_core)

    def first_copies(c):
        return (
            rs_copy(1, c, m.sums.at[c, every, every, 1 - x, full_rows, left], m.r1a.at[c], over_x),
            rs_copy(2, c, m.sums.at[c, every, 1 - zl, every, full_rows, right], m.r1b.at[c], over_zl),
        )

    def second_copies(c):
        return (
            rs_copy(3, c, m.sums.at[c, every, 1 - zl, x, full_rows, left], m.r2a.at[c], over_zl),
            rs_copy(4, c, m.sums.at[c, every, zl, 1 - x, full_rows, right], m.r2b.at[c], over_x),
        )

    def third_copy(c):
        return rs_copy(5, c, m.sums.at[c, 1 - zh, zl, x], m.r3.at[c], over_zh)

    def local(i, src, dst):
        return pltpu.make_async_copy(src, dst, m.l_sem.at[i])

    def both(i, src_own, src_oth, dst):
        return (local(i, src_own, dst.at[own_rows]), local(i + 1, src_oth, dst.at[oth_rows]))

    def start(copies):
        for copy in copies:
            copy.start()

    def wait(copies):
        for copy in copies:
            copy.wait()

    def add_core(c):
        core_copy(c).wait_recv()
        for a in range(2):
            for b in range(2):
                for e in range(2):
                    m.sums[c, a, b, e] = (
                        m.sums[c, a, b, e].astype(F32) + m.kept[lax.rem(c, 2), a, b, e].astype(F32)
                    ).astype(BF16)

    def total_copy(c):
        slot = lax.rem(c, 2)
        return pltpu.make_async_copy(m.totals.at[slot], m.shards.at[c], m.s_sem.at[slot])

    def tick(i):
        @pl.when(i < n_chunks)
        def _():
            a_copy, b_copy = first_copies(i)
            a_copy.wait_recv()
            b_copy.wait_recv()
            for a in range(2):
                for b in range(2):
                    m.sums[i, a, b, x, :, :SPLIT] = (
                        m.sums[i, a, b, x, :, :SPLIT].astype(F32) + m.r1a[i, a, b].astype(F32)
                    ).astype(BF16)
                    m.sums[i, a, zl, b, :, SPLIT:] = (
                        m.sums[i, a, zl, b, :, SPLIT:].astype(F32) + m.r1b[i, a, b].astype(F32)
                    ).astype(BF16)
            start(second_copies(i))

        @pl.when(i + 2 < n_chunks)
        def _():
            start(first_copies(i + 2))

        @pl.when((i >= 1) & (i < n_chunks + 1))
        def _():
            c = i - 1
            a_copy, b_copy = second_copies(c)
            a_copy.wait_recv()
            b_copy.wait_recv()
            for a in range(2):
                m.sums[c, a, zl, x, :, :SPLIT] = (
                    m.sums[c, a, zl, x, :, :SPLIT].astype(F32) + m.r2a[c, a].astype(F32)
                ).astype(BF16)
                m.sums[c, a, zl, x, :, SPLIT:] = (
                    m.sums[c, a, zl, x, :, SPLIT:].astype(F32) + m.r2b[c, a].astype(F32)
                ).astype(BF16)
            third_copy(c).start()

        @pl.when((i >= 2) & (i < n_chunks + 2))
        def _():
            c = i - 2
            third_copy(c).wait_recv()

            @pl.when(c >= 2)
            def _():
                total_copy(c - 2).wait()

            m.totals[lax.rem(c, 2)] = m.sums[c, zh, zl, x].astype(F32) + m.r3[c].astype(F32)
            total_copy(c).start()

    def pack(dst, own_ref, oth_ref):
        for part, ref in enumerate((own_ref, oth_ref)):
            at = pl.ds(part * rows, rows)
            for k in range(width // (2 * PAIR)):
                a = ref[:, 2 * k * PAIR : (2 * k + 1) * PAIR].astype(F32)
                b = ref[:, (2 * k + 1) * PAIR : (2 * k + 2) * PAIR].astype(F32)
                lanes = slice(k * PAIR, (k + 1) * PAIR)
                m.packed[dst, 0, at, lanes] = jnp.where(low, a, pltpu.roll(b, 64, 1)).astype(BF16)
                m.packed[dst, 1, at, lanes] = jnp.where(low, pltpu.roll(a, 64, 1), b).astype(BF16)

    def put(ref, slot, lanes, value):
        for a in range(2):
            for b in range(2):
                for e in range(2):
                    k = ((a * 2 + b) * 2 + e) * block_rows
                    ref[slot, a, b, e, :, lanes] = value[k : k + block_rows].astype(BF16)

    gf_copy.start()
    stage_cot = both(0, m.cot_own, m.cot_oth, m.stage)
    stage_ffn = both(0, m.ffn_own, m.ffn_oth, m.stage)
    stage_attn = both(0, m.attn_own, m.attn_oth, m.stage)
    start(stage_cot)
    loads = [
        local(2, m.gf_own, m.gres), local(3, m.resid, m.resid_v), local(4, m.wo_mine, m.wom_v),
        local(5, m.wo_oth, m.wot_v), local(6, m.cot_own, m.cot_v), local(7, m.w_q, m.wq_v), local(8, m.w_kv, m.wkv_v),
        *both(9, m.o_own, m.o_oth, m.o_v), *both(11, m.kraw_own, m.kraw_oth, m.kraw_v),
    ]

    def tiles(g):
        slot = lax.rem(g, 2)
        lanes = pl.ds(pl.multiple_of(g * PAIR, PAIR), PAIR)
        out = []
        for j, (own, oth, dst) in enumerate((
            (m.q_own, m.q_oth, m.q_v), (m.kd_own, m.kd_oth, m.kd_v), (m.vd_own, m.vd_oth, m.vd_v),
            (m.qraw_own, m.qraw_oth, m.qraw_v), (m.linv_own, m.linv_oth, m.linv_v),
        )):
            out.append(pltpu.make_async_copy(own.at[:, lanes], dst.at[slot, own_rows], m.g_sem.at[slot, 2 * j]))
            out.append(pltpu.make_async_copy(oth.at[:, lanes], dst.at[slot, oth_rows], m.g_sem.at[slot, 2 * j + 1]))
        return out

    def wide_phase(y_v):
        def fetch(c):
            slot = lax.rem(c, 2)
            cols = pl.ds(pl.multiple_of(lax.rem(c, per_x) * CHUNK, CHUNK), CHUNK)
            return [
                pltpu.make_async_copy(
                    h.at[c // per_x, :, cols], y_v.at[slot, at], m.h_sem.at[slot, j]
                )
                for j, (h, at) in enumerate(((m.h_own, own_rows), (m.h_oth, oth_rows)))
            ]

        start(fetch(0))
        wait(stage_cot)
        pack(0, m.stage.at[own_rows], m.stage.at[oth_rows])
        start(stage_ffn)
        start(loads)

        def chunk(c, which):
            slot = lax.rem(c, 2)
            wait(fetch(c))

            @pl.when(c + 1 < n_wide)
            def _():
                start(fetch(c + 1))

            @pl.when(c >= 2)
            def _():
                core_copy(c - 2).wait_send()

            put(m.core_send, slot, slice(None), dot_tn(m.packed[which, 1 - core], y_v[slot]))
            core_copy(c).start()
            put(m.kept, slot, slice(None), dot_tn(m.packed[which, core], y_v[slot]))

            @pl.when(c >= 1)
            def _():
                add_core(c - 1)

            @pl.when((c >= 1) & (c <= 2))
            def _():
                start(first_copies(c - 1))

            @pl.when(c == n_wide - 3)
            def _():
                tick(0)

        def first(c, carry):
            chunk(c, 0)
            return carry

        lax.fori_loop(0, per_x, first, 0)
        wait(stage_ffn)
        pack(1, m.stage.at[own_rows], m.stage.at[oth_rows])
        start(stage_attn)

        def second(c, carry):
            chunk(c, 1)
            return carry

        lax.fori_loop(per_x, n_wide, second, 0)
        add_core(n_wide - 1)
        tick(1)

    pl.run_scoped(wide_phase, pltpu.VMEM((2, 2 * rows, CHUNK), BF16))
    start(tiles(0))

    wait(loads)
    gf_copy.wait_recv()
    gain_sum = jnp.zeros((1, width), F32)
    for i in range(rows // BLOCK):
        at = slice(i * BLOCK, (i + 1) * BLOCK)
        grad = m.gres[at, :] + m.gf_recv[at, :].astype(F32)
        resid = m.resid_v[at, :]
        inverse = row_norm(resid)
        normed = resid * inverse
        gain_sum += jnp.sum(grad * normed, axis=0, keepdims=True)
        w = grad * m.gain2[...]
        gres = m.cot_v[at, :].astype(F32) + inverse * (
            w - normed * jnp.mean(w * normed, axis=-1, keepdims=True)
        )
        m.gres[at, :] = gres
        branch = gres.astype(BF16)
        m.branch[at, :] = branch
        m.do_send[at, :] = dot_nt(branch, m.wot_v[...]).astype(BF16)
    do_copy.start()
    m.do_own[...] = dot_nt(m.branch[...], m.wom_v[...]).astype(BF16)
    for r in range(width // PAIR):
        m.mine[width // PAIR + r : width // PAIR + r + 1, :] = gain_sum[:, r * PAIR : (r + 1) * PAIR]
    wait(stage_attn)
    pack(0, m.stage.at[own_rows], m.stage.at[oth_rows])
    tick(2)
    do_copy.wait_recv()
    branch_copy.start()
    tick(3)

    def narrow_chunk(p):
        c = n_wide + p
        slot = lax.rem(c, 2)
        core_copy(c - 2).wait_send()
        cols = pl.ds(pl.multiple_of(p * SPLIT, SPLIT), SPLIT)
        o_cols = pl.ds(pl.multiple_of(p * (CHUNK - SPLIT), CHUNK - SPLIT), CHUNK - SPLIT)
        for which, dst in ((1 - core, m.core_send), (core, m.kept)):
            put(dst, slot, slice(0, SPLIT), dot_tn(m.packed[0, which], m.g_v[:, cols]))
            put(dst, slot, slice(SPLIT, CHUNK), dot_tn(m.packed[1, which], m.o_v[:, o_cols]))
        core_copy(c).start()

    def place(block):
        return pl.ds(pl.multiple_of(lax.rem(block + t * (nb // 2), nb) * BLOCK, BLOCK), BLOCK)

    m.qgain[...] = jnp.zeros_like(m.qgain)
    m.kgain[...] = jnp.zeros_like(m.kgain)

    def attention_phase(qx, dox, kx0, kx1, vx0, vx1, kt, dqt, dk0, dk1, dv0, dv1, dks, dvs):
        all_low = lane_of((2 * rows, PAIR)) < 64
        one = jnp.ones((2 * rows, PAIR), F32)
        zero = jnp.zeros((2 * rows, PAIR), BF16)
        qx[:, PAIR:] = m.segq[...]
        kx0[:, PAIR:] = m.segk[...]
        kx1[:, PAIR:] = m.segk[...]
        vx0[:, PAIR:] = jnp.where(all_low, -one, 0.0).astype(BF16)
        vx1[:, PAIR:] = jnp.where(all_low, 0.0, -one).astype(BF16)

        def step(qb, kb, diagonal):
            qs, ks = place(qb), place(kb)
            q, do = qx[qs, :], dox[qs, :]
            for h, (kx, vx, dk, dv) in enumerate(((kx0, vx0, dk0, dv0), (kx1, vx1, dk1, dv1))):
                s = dot_nt(kx[ks, :], q)
                if diagonal:
                    r = lax.broadcasted_iota(jnp.int32, s.shape, 0)
                    s = jnp.where(r <= lane_of(s.shape), s, -1e30)
                e = jnp.exp2(s)
                ds = (e * dot_nt(vx[ks, :], do)).astype(BF16)
                dv[ks, :] += dot_nn(e.astype(BF16), do[:, :PAIR])
                dk[ks, :] += dot_nn(ds, q[:, :PAIR])
                dqt[h * 64 : (h + 1) * 64, qs] += dot_nn(kt[:, ks], ds)

        def group(g, carry):
            slot = lax.rem(g, 2)
            lanes = pl.ds(pl.multiple_of(g * PAIR, PAIR), PAIR)
            p = g // 2
            wait(tiles(g))

            @pl.when(g + 1 < 4)
            def _():
                start(tiles(g + 1))

            qx[:, :PAIR] = m.q_v[slot]
            k, v = m.kd_v[slot], m.vd_v[slot]
            kx0[:, :PAIR] = jnp.where(all_low, k, zero)
            kx1[:, :PAIR] = jnp.where(all_low, zero, k)
            vx0[:, :PAIR] = jnp.where(all_low, v, zero)
            vx1[:, :PAIR] = jnp.where(all_low, zero, v)
            kt[...] = jnp.transpose(k.astype(F32))[:64, :].astype(BF16)
            for at, do_ref in ((own_rows, m.do_own), (oth_rows, m.do_recv)):
                scaled = do_ref[:, lanes].astype(F32) * m.linv_v[slot, at, :]
                dox[at, :PAIR] = scaled.astype(BF16)
                dox[at, PAIR:] = (scaled * m.o_v[at, lanes].astype(F32)).astype(BF16)
            for ref in (dqt, dk0, dk1, dv0, dv1):
                ref[...] = jnp.zeros_like(ref)

            def q_body(qb, c):
                step(qb, qb, True)

                def k_body(kb, cc):
                    step(qb, kb, False)
                    return cc

                lax.fori_loop(jnp.maximum(qb - 2, 0), qb, k_body, 0)
                return c

            lax.fori_loop(0, nb, q_body, 0)

            g_lanes = pl.ds(pl.multiple_of(p * SPLIT + slot * PAIR, PAIR), PAIR)
            for at in (own_rows, oth_rows):
                dq = jnp.transpose(dqt[:, at]) * 0.125
                normed_grad = rope(dq, m.cos[at, :], -m.sin[at, :])
                raw = m.qraw_v[slot, at, :].astype(F32)
                inverse = lax.rsqrt(head_mean(raw * raw) + EPS)
                u = raw * inverse
                m.qgain[...] += jnp.sum(normed_grad * u, axis=0, keepdims=True)
                w = normed_grad * m.qg[...]
                m.g_v[at, g_lanes] = (inverse * (w - u * head_mean(w * u))).astype(BF16)

            def gathered(a, b, at):
                joined = jnp.where(low, a[at, :], b[at, :])
                return joined + pltpu.roll(joined, 64, 1)

            @pl.when(slot == 0)
            def _():
                for at in (own_rows, oth_rows):
                    dks[at, :] = gathered(dk0, dk1, at)
                    dvs[at, :] = gathered(dv0, dv1, at)

            @pl.when(slot == 1)
            def _():
                k_lanes = pl.ds(pl.multiple_of(p * SPLIT + 2 * PAIR, PAIR), PAIR)
                v_lanes = pl.ds(pl.multiple_of(p * SPLIT + 3 * PAIR, PAIR), PAIR)
                raw_lanes = pl.ds(pl.multiple_of(p * PAIR, PAIR), PAIR)
                for at in (own_rows, oth_rows):
                    dk = jnp.where(low, dks[at, :], gathered(dk0, dk1, at)) * LN2
                    dv = jnp.where(low, dvs[at, :], gathered(dv0, dv1, at))
                    normed_grad = rope(dk, m.cos[at, :], -m.sin[at, :])
                    raw = m.kraw_v[at, raw_lanes].astype(F32)
                    inverse = lax.rsqrt(head_mean(raw * raw) + EPS)
                    u = raw * inverse
                    m.kgain[...] += jnp.sum(normed_grad * u, axis=0, keepdims=True)
                    w = normed_grad * m.kg[...]
                    m.g_v[at, k_lanes] = (inverse * (w - u * head_mean(w * u))).astype(BF16)
                    m.g_v[at, v_lanes] = dv.astype(BF16)

                @pl.when(p == 0)
                def _():
                    branch_copy.wait_recv()
                    y_copy.start()
                    pack(1, m.branch, m.branch_recv)

                narrow_chunk(p)

            @pl.when(g == 2)
            def _():
                add_core(n_wide)

            tick(4 + g)
            return carry

        lax.fori_loop(0, 4, group, 0)

    pl.run_scoped(
        attention_phase,
        *[pltpu.VMEM((2 * rows, 2 * PAIR), BF16)] * 6,
        pltpu.VMEM((64, 2 * rows), BF16), pltpu.VMEM((PAIR, 2 * rows), F32),
        *[pltpu.VMEM((2 * rows, PAIR), F32)] * 6,
    )

    def attn_in_grad(at):
        out = None
        qc, kc = m.wq_v.shape[1], m.wkv_v.shape[1] // 2
        for p in range(2):
            for ref, base, begin, size in (
                (m.wq_v, 0, 0, 2 * PAIR), (m.wkv_v, 0, 2 * PAIR, PAIR), (m.wkv_v, kc, 3 * PAIR, PAIR)
            ):
                term = dot_nt(
                    m.g_v[at, p * SPLIT + begin : p * SPLIT + begin + size],
                    ref[:, base + p * size : base + (p + 1) * size],
                )
                out = term if out is None else out + term
        return out

    def end_phase(ga_own, y_v, y_other):
        tok_v, out_v = m.stage, m.cot_v
        start(both(0, m.tok_own, m.tok_oth, tok_v))
        load_y = local(2, m.y_own, y_v)
        load_y.start()
        wait(both(0, m.tok_own, m.tok_oth, tok_v))

        def grad_and_gain(at):
            grad = attn_in_grad(at)
            tokens = tok_v[at, :].astype(F32)
            return grad, jnp.sum(grad * (tokens * row_norm(tokens)), axis=0, keepdims=True)

        branch_copy.wait_send()
        total = jnp.zeros((1, width), F32)
        for i in range(rows // BLOCK):
            grad, part = grad_and_gain(pl.ds(rows + i * BLOCK, BLOCK))
            m.branch[i * BLOCK : (i + 1) * BLOCK, :] = grad.astype(BF16)
            total += part
        ga_copy.start()
        add_core(n_chunks - 1)
        tick(n_chunks - 3)
        for i in range(rows // BLOCK):
            grad, part = grad_and_gain(pl.ds(i * BLOCK, BLOCK))
            ga_own[i * BLOCK : (i + 1) * BLOCK, :] = grad
            total += part
        for r in range(width // PAIR):
            m.mine[r : r + 1, :] = total[:, r * PAIR : (r + 1) * PAIR]
        last = 2 * width // PAIR
        m.mine[last : last + 1, :] = m.qgain[...]
        m.mine[last + 1 : last + 2, :] = m.kgain[...]
        m.mine[last + 2 :, :] = jnp.zeros((m.mine.shape[0] - last - 2, PAIR), F32)

        def gain_copy(i, device):
            return pltpu.make_async_remote_copy(
                src_ref=m.gain_out.at[i], dst_ref=m.gain_in.at[i], send_sem=m.gain_sem.at[0, i],
                recv_sem=m.gain_sem.at[1, i], device_id=device, device_id_type=MESH,
            )

        for i, device in enumerate(partners):
            m.gain_out[i] = m.mine[...]
            gain_copy(i, device).start()
            if i == 2:
                y_copy.wait_recv()
                load_y.wait()
                arrived = local(4, m.y_recv, y_other)
                arrived.start()
                arrived.wait()
                out_v[...] = (m.resid_v[...] + y_v[...] + y_other[...].astype(F32)).astype(BF16)
                local(3, out_v, m.output).start()
            if i >= 1:
                tick(n_chunks - 3 + i)
            gain_copy(i, device).wait_recv()
            m.mine[...] += m.gain_in[i]
        m.gains[...] = m.mine[...]
        ga_copy.wait_recv()
        for i in range(rows // PAIR):
            at = slice(i * PAIR, (i + 1) * PAIR)
            tokens = tok_v[at, :].astype(F32)
            inverse = row_norm(tokens)
            normed = tokens * inverse
            w = (ga_own[at, :] + m.gf_recv[at, :].astype(F32)) * m.gain1[...]
            ga_own[at, :] = m.gres[at, :] + inverse * (
                w - normed * jnp.mean(w * normed, axis=-1, keepdims=True)
            )
            local(4 + i, ga_own.at[pl.ds(i * PAIR, PAIR)], m.grad_tokens.at[pl.ds(i * PAIR, PAIR)]).start()
        for copy in (gf_copy, do_copy, y_copy, ga_copy):
            copy.wait_send()
        for i, device in enumerate(partners):
            gain_copy(i, device).wait_send()
        for c in (n_chunks - 2, n_chunks - 1):
            core_copy(c).wait_send()

        def drain(c, carry):
            for copy in (*first_copies(c), *second_copies(c), third_copy(c)):
                copy.wait_send()
            return carry

        lax.fori_loop(0, n_chunks, drain, 0)
        local(3, out_v, m.output).wait()
        for i in range(rows // PAIR):
            local(4 + i, ga_own.at[pl.ds(i * PAIR, PAIR)], m.grad_tokens.at[pl.ds(i * PAIR, PAIR)]).wait()
        for c in (n_chunks - 2, n_chunks - 1):
            total_copy(c).wait()

    pl.run_scoped(
        end_phase,
        pltpu.VMEM((rows, width), F32), pltpu.VMEM((rows, width), F32), pltpu.VMEM((rows, width), BF16),
    )


def back(n_dp, values, tables):
    rows, width = values["resid"].shape
    hidden = values["h_own"].shape[2]
    seq = 2 * rows
    qc = values["w_q"].shape[1]
    n_chunks = 3 * hidden // CHUNK + 2
    block = width // n_dp
    vm = pltpu.VMEM
    dma = pltpu.SemaphoreType.DMA
    scratch = dict(
        stage=vm((seq, width), BF16), packed=vm((2, 2, seq, width // 2), BF16),
        core_send=vm((2, 2, 2, 2, block, CHUNK), BF16), kept=vm((2, 2, 2, 2, block, CHUNK), BF16),
        sums=vm((n_chunks, 2, 2, 2, block, CHUNK), BF16),
        r1a=vm((n_chunks, 2, 2, block, SPLIT), BF16), r1b=vm((n_chunks, 2, 2, block, CHUNK - SPLIT), BF16),
        r2a=vm((n_chunks, 2, block, SPLIT), BF16), r2b=vm((n_chunks, 2, block, CHUNK - SPLIT), BF16),
        r3=vm((n_chunks, block, CHUNK), BF16), totals=vm((2, block, CHUNK), F32),
        gres=vm((rows, width), F32), resid_v=vm((rows, width), F32), cot_v=vm((rows, width), BF16),
        wom_v=vm((qc, width), BF16), wot_v=vm((qc, width), BF16),
        wq_v=vm((width, qc), BF16), wkv_v=vm((width, qc), BF16),
        o_v=vm((seq, qc), BF16), kraw_v=vm((seq, qc // 2), BF16),
        q_v=vm((2, seq, PAIR), BF16), kd_v=vm((2, seq, PAIR), BF16), vd_v=vm((2, seq, PAIR), BF16),
        qraw_v=vm((2, seq, PAIR), BF16), linv_v=vm((2, seq, PAIR), F32),
        g_v=vm((seq, 2 * SPLIT), BF16), do_own=vm((rows, qc), BF16),
        gf_recv=vm((rows, width), BF16), do_send=vm((rows, qc), BF16), do_recv=vm((rows, qc), BF16),
        branch=vm((rows, width), BF16), branch_recv=vm((rows, width), BF16),
        qgain=vm((1, PAIR), F32), kgain=vm((1, PAIR), F32), mine=vm((24, PAIR), F32),
        gain_out=vm((5, 24, PAIR), F32), gain_in=vm((5, 24, PAIR), F32),
        t_send=dma((5,)), t_recv=dma((5,)), rs_send=dma((6, n_chunks)), rs_recv=dma((6, n_chunks)),
        l_sem=dma((13,)), g_sem=dma((2, 10)), h_sem=dma((2, 2)), s_sem=dma((2,)), gain_sem=dma((2, 5)),
    )
    anywhere = pl.BlockSpec(memory_space=pl.ANY)
    vmem = pl.BlockSpec(memory_space=pltpu.VMEM)
    return pl.pallas_call(
        functools.partial(back_kernel, n_dp, tuple(scratch)),
        in_specs=[anywhere] * len(BACK_INPUTS) + [vmem] * len(BACK_TABLES),
        out_specs=[anywhere, anywhere, anywhere, vmem, anywhere],
        out_shape=[
            jax.ShapeDtypeStruct((rows, width), BF16), jax.ShapeDtypeStruct((rows, width), F32),
            jax.ShapeDtypeStruct((n_chunks, block, CHUNK), F32), jax.ShapeDtypeStruct((24, PAIR), F32),
            jax.ShapeDtypeStruct((rows, width), BF16),
        ],
        scratch_shapes=list(scratch.values()),
        compiler_params=pltpu.CompilerParams(
            vmem_limit_bytes=BACK_VMEM, collective_id=0, has_side_effects=True
        ),
        cost_estimate=cost(100e-6),
        name="back",
    )(*[values[k] for k in BACK_INPUTS], *[tables[k] for k in BACK_TABLES])


def swap(value, axis, size, bit):
    return lax.ppermute(value, axis, [(i, i ^ bit) for i in range(size)])


def after(value, *others):
    return lax.optimization_barrier((value,) + others)[0]


def paired(
    n_dp, tokens, doc_ids, gain_attn, w_q, w_kv, q_gain, k_gain, w_o, gain_ffn, w_gu, w_down, cotangent
):
    rows, width = tokens.shape
    head_dim = q_gain.shape[0]
    hidden = w_down.shape[0]
    seq = doc_ids.shape[1]
    t = lax.axis_index("tensor")
    d = lax.axis_index("dp")
    over = functools.partial(swap, axis="tensor", size=2, bit=1)

    tokens_oth = over(tokens)
    w_o_oth = over(after(w_o, tokens_oth))
    cot_oth = over(after(cotangent, tokens_oth))

    segment = doc_ids[0]
    nb = seq // BLOCK
    heads_of_blocks = segment.reshape(nb, BLOCK)
    first_doc, last_doc = heads_of_blocks[:, 0], heads_of_blocks[:, -1]
    below = jnp.arange(nb)[None, :] < jnp.arange(nb)[:, None]
    lowest = jnp.sum((below & (last_doc[None, :] < first_doc[:, None])).astype(jnp.int32), axis=1)
    shift = t * (nb // 2)
    table = lambda first: jnp.concatenate([jnp.stack([shift, first]).astype(jnp.int32), lowest])
    scalars_own = table(shift)
    scalars_oth = table(nb // 2 - shift)
    segment = jnp.where(t == 0, segment, jnp.roll(segment, rows))
    lanes = jnp.arange(PAIR, dtype=jnp.int32)[None, :]
    match = lanes == segment[:, None]
    marker = lanes == 8
    segk = (match | marker).astype(BF16)
    segq = (jnp.where(match, SAME, 0.0) - jnp.where(marker, SAME, 0.0)).astype(BF16)
    half_dim = head_dim // 2
    frequency = jnp.exp(-math.log(THETA) * 2.0 * jnp.arange(half_dim, dtype=F32) / head_dim)
    position = (jnp.arange(seq, dtype=jnp.int32) + t * rows) % seq
    angles = position.astype(F32)[:, None] * frequency[None, :]
    cos, sin = jnp.cos(angles), jnp.sin(angles)
    cosine = jnp.concatenate([cos] * 4, axis=1)
    sine = jnp.concatenate([-sin, sin] * 2, axis=1)
    gain1, gain2 = gain_attn.reshape(1, width), gain_ffn.reshape(1, width)
    qg = jnp.concatenate([q_gain, q_gain]).reshape(1, PAIR)
    kg = jnp.concatenate([k_gain, k_gain]).reshape(1, PAIR)
    w_kv = w_kv.reshape(width, -1)
    w_gu = w_gu.reshape(width, 2 * hidden)
    core = (d & 1).astype(jnp.int32).reshape(1)

    attn_own, q_own, kd_own, vd_own, qraw_own, kraw_own = qkv(
        tokens, gain1, w_q, w_kv, qg, kg, cosine, sine, 0
    )
    attn_oth, q_oth, kd_oth, vd_oth, qraw_oth, kraw_oth = qkv(
        tokens_oth, gain1, w_q, w_kv, qg, kg, cosine, sine, 1
    )
    o_oth, linv_oth = attn_fwd(scalars_oth, q_oth, kd_own, kd_oth, vd_own, vd_oth, segq, segk, 1)
    theirs = over(o_oth)
    o_own, linv_own = attn_fwd(scalars_own, q_own, kd_own, kd_oth, vd_own, vd_oth, segq, segk, 0)
    resid, ffn_own = resid_norm(o_own, theirs, w_o, w_o_oth, tokens, gain2)

    ffn_oth = over(ffn_own)
    h_own, y_own, gf_own = ffn(ffn_own, cotangent, w_gu, w_down, F32)
    h_oth, y_oth, gf_oth = ffn(after(ffn_oth, gf_own), cot_oth, w_gu, w_down, BF16)

    output, grad_tokens, shards, gains, _ = back(
        n_dp,
        dict(
            h_own=h_own, h_oth=h_oth, cot_own=cotangent, cot_oth=cot_oth, ffn_own=ffn_own, ffn_oth=ffn_oth,
            attn_own=attn_own, attn_oth=attn_oth, tok_own=tokens, tok_oth=tokens_oth,
            gf_own=gf_own, gf_send=gf_oth, y_own=y_own, y_send=y_oth, resid=resid,
            wo_mine=w_o, wo_oth=w_o_oth, w_q=w_q, w_kv=w_kv,
            q_own=q_own, q_oth=q_oth, kd_own=kd_own, kd_oth=kd_oth, vd_own=vd_own, vd_oth=vd_oth,
            o_own=o_own, o_oth=o_oth, linv_own=linv_own, linv_oth=linv_oth,
            qraw_own=qraw_own, qraw_oth=qraw_oth, kraw_own=kraw_own, kraw_oth=kraw_oth,
        ),
        dict(segq=segq, segk=segk, cos=cosine, sin=sine, gain1=gain1, gain2=gain2, qg=qg, kg=kg),
    )
    m = width // PAIR
    per_x = hidden // CHUNK
    fold = lambda row: row[:head_dim] + row[head_dim:]
    side = lambda i: jnp.concatenate([shards[i * per_x + j] for j in range(per_x)], axis=1)
    pairs = [shards[3 * per_x + p] for p in range(2)]
    join = lambda a, b: jnp.concatenate([pair[:, a:b] for pair in pairs], axis=1)
    return (
        output,
        grad_tokens,
        gains[:m].reshape(width),
        join(0, 2 * PAIR),
        jnp.stack([join(2 * PAIR, 3 * PAIR), join(3 * PAIR, 4 * PAIR)], axis=1),
        fold(gains[2 * m]),
        fold(gains[2 * m + 1]),
        join(SPLIT, CHUNK).T,
        gains[m : 2 * m].reshape(width),
        jnp.stack([side(1), side(2)], axis=1),
        side(0).T,
    )


def normalize(values):
    inverse = lax.rsqrt(jnp.mean(values * values, axis=-1, keepdims=True) + EPS)
    return (values * inverse, inverse)


def norm_back(grad_normed, normed, inverse):
    return inverse * (grad_normed - normed * jnp.mean(grad_normed * normed, axis=-1, keepdims=True))


def rotate(values, cosine_table, sine_table):
    half_dim = values.shape[-1] // 2
    first_half = values[..., :half_dim]
    second_half = values[..., half_dim:]
    return jnp.concatenate(
        [
            first_half * cosine_table - second_half * sine_table,
            second_half * cosine_table + first_half * sine_table,
        ],
        -1,
    )


def shards(
    tokens, doc_ids, gain_attn, w_q, w_kv, q_gain, k_gain, w_o, gain_ffn, w_gu, w_down, cotangent
):
    f32 = jnp.float32
    bf16 = jnp.bfloat16
    rows_dev, model_width = tokens.shape
    head_dim = q_gain.shape[0]
    q_cols = w_q.shape[1]
    q_heads = q_cols // head_dim
    kv_cols = w_kv.shape[2]
    kv_heads = kv_cols // head_dim
    group_size = q_heads // kv_heads
    hidden = w_gu.shape[2]
    seq_len = doc_ids.shape[1]
    segment = doc_ids[0]
    block_rows = min(512, seq_len)
    blocks = seq_len // block_rows
    score_scale = head_dim ** (-0.5)
    w_kv_flat = w_kv.reshape(model_width, 2 * kv_cols)
    w_gu_flat = w_gu.reshape(model_width, 2 * hidden)
    half_dim = head_dim // 2
    frequency = jnp.exp(-math.log(THETA) * 2.0 * jnp.arange(half_dim, dtype=f32) / head_dim)
    angles = jnp.arange(seq_len, dtype=f32)[:, None] * frequency[None, :]
    cosine_table = jnp.cos(angles)[:, None, :]
    sine_table = jnp.sin(angles)[:, None, :]
    key_pos = jnp.arange(seq_len, dtype=jnp.int32)
    x_float = tokens.astype(f32)
    normed1, inverse1 = normalize(x_float)
    attn_in = (normed1 * gain_attn).astype(bf16)
    attn_all = lax.all_gather(attn_in, "tensor", axis=0, tiled=True)
    q_raw = jnp.dot(attn_all, w_q, preferred_element_type=f32).reshape(seq_len, q_heads, head_dim)
    kv_raw = jnp.dot(attn_all, w_kv_flat, preferred_element_type=f32).reshape(
        seq_len, 2, kv_heads, head_dim
    )
    q_normed, q_inverse = normalize(q_raw)
    k_normed, k_inverse = normalize(kv_raw[:, 0])
    queries = rotate(q_normed * q_gain, cosine_table, sine_table).astype(bf16)
    queries = queries.reshape(seq_len, kv_heads, group_size, head_dim)
    keys = rotate(k_normed * k_gain, cosine_table, sine_table).astype(bf16)
    values_low = kv_raw[:, 1].astype(bf16)

    def scores_of(first_row):
        q_block = lax.dynamic_slice_in_dim(queries, first_row, block_rows, 0)
        seg_block = lax.dynamic_slice_in_dim(segment, first_row, block_rows, 0)
        raw_scores = (
            jnp.einsum("qhgd,thd->hgqt", q_block, keys, preferred_element_type=f32) * score_scale
        )
        query_pos = first_row + jnp.arange(block_rows, dtype=jnp.int32)
        allowed = (key_pos[None, :] <= query_pos[:, None]) & (
            seg_block[:, None] == segment[None, :]
        )
        return (jnp.where(allowed, raw_scores, -1e30), q_block)

    def attend(first_row):
        masked, q_block = scores_of(first_row)
        row_max = jnp.max(masked, axis=-1, keepdims=True)
        exponent = jnp.exp(masked - row_max)
        denominator = jnp.sum(exponent, axis=-1, keepdims=True)
        probs = (exponent / denominator).astype(bf16)
        attended_block = jnp.einsum("hgqt,thd->qhgd", probs, values_low, preferred_element_type=f32)
        return (attended_block, (row_max + jnp.log(denominator))[..., 0])

    starts = jnp.arange(blocks, dtype=jnp.int32) * block_rows
    attended, log_sums = lax.map(attend, starts)
    attended_low = attended.reshape(seq_len, q_cols).astype(bf16)
    resid = x_float + lax.psum_scatter(
        jnp.dot(attended_low, w_o, preferred_element_type=f32),
        "tensor",
        scatter_dimension=0,
        tiled=True,
    )
    normed2, inverse2 = normalize(resid)
    ffn_in = (normed2 * gain_ffn).astype(bf16)
    ffn_all = lax.all_gather(ffn_in, "tensor", axis=0, tiled=True)
    gate_up = jnp.dot(ffn_all, w_gu_flat, preferred_element_type=f32)
    gate_part = gate_up[:, :hidden]
    up_part = gate_up[:, hidden:]
    sigmoid_gate = jax.nn.sigmoid(gate_part)
    silu_gate = gate_part * sigmoid_gate
    mixed = (silu_gate * up_part).astype(bf16)
    result = resid + lax.psum_scatter(
        jnp.dot(mixed, w_down, preferred_element_type=f32).astype(jnp.bfloat16),
        "tensor",
        scatter_dimension=0,
        tiled=True,
    ).astype(jnp.float32)
    output = result.astype(bf16)
    grad_all = lax.all_gather(cotangent, "tensor", axis=0, tiled=True)
    grad_down = jnp.einsum("sf,sd->fd", mixed, grad_all, preferred_element_type=f32)
    grad_mixed = jnp.einsum("sd,fd->sf", grad_all, w_down, preferred_element_type=f32)
    grad_gate = grad_mixed * up_part * sigmoid_gate * (1.0 + gate_part * (1.0 - sigmoid_gate))
    grad_up = grad_mixed * silu_gate
    grad_gu = jnp.concatenate([grad_gate, grad_up], 1).astype(bf16)
    grad_w_gu = jnp.einsum("sd,sf->df", ffn_all, grad_gu, preferred_element_type=f32).reshape(
        model_width, 2, hidden
    )
    grad_ffn_in = lax.psum_scatter(
        jnp.einsum("sf,df->sd", grad_gu, w_gu_flat, preferred_element_type=f32).astype(
            jnp.bfloat16
        ),
        "tensor",
        scatter_dimension=0,
        tiled=True,
    ).astype(jnp.float32)
    gain_ffn_part = jnp.sum(grad_ffn_in * normed2, axis=0)
    grad_resid = cotangent.astype(f32) + norm_back(grad_ffn_in * gain_ffn, normed2, inverse2)
    branch_all = lax.all_gather(grad_resid.astype(bf16), "tensor", axis=0, tiled=True)
    grad_w_o = jnp.einsum("sc,sd->cd", attended_low, branch_all, preferred_element_type=f32)
    grad_attended = jnp.einsum("sd,cd->sc", branch_all, w_o, preferred_element_type=f32).astype(
        bf16
    )
    grad_attended = grad_attended.reshape(seq_len, kv_heads, group_size, head_dim)

    def attend_back(carried, scanned):
        first_row, lse_block = scanned
        masked, q_block = scores_of(first_row)
        probs = jnp.exp(masked - lse_block[..., None])
        go_block = lax.dynamic_slice_in_dim(grad_attended, first_row, block_rows, 0)
        grad_probs = jnp.einsum("qhgd,thd->hgqt", go_block, values_low, preferred_element_type=f32)
        grad_scores = (
            probs * (grad_probs - jnp.sum(probs * grad_probs, axis=-1, keepdims=True))
        ).astype(bf16)
        keys_next = carried[0] + score_scale * jnp.einsum(
            "hgqt,qhgd->thd", grad_scores, q_block, preferred_element_type=f32
        )
        values_next = carried[1] + jnp.einsum(
            "hgqt,qhgd->thd", probs.astype(bf16), go_block, preferred_element_type=f32
        )
        grad_q_block = score_scale * jnp.einsum(
            "hgqt,thd->qhgd", grad_scores, keys, preferred_element_type=f32
        )
        return ((keys_next, values_next), grad_q_block)

    zero_kv = jnp.zeros((seq_len, kv_heads, head_dim), f32)
    (grad_keys, grad_values), grad_queries = lax.scan(
        attend_back, (zero_kv, zero_kv), (starts, log_sums)
    )
    grad_q_normed = rotate(
        grad_queries.reshape(seq_len, q_heads, head_dim), cosine_table, -sine_table
    )
    q_gain_part = jnp.sum(grad_q_normed * q_normed, axis=(0, 1))
    grad_q_raw = (
        norm_back(grad_q_normed * q_gain, q_normed, q_inverse).astype(bf16).reshape(seq_len, q_cols)
    )
    grad_k_normed = rotate(grad_keys, cosine_table, -sine_table)
    k_gain_part = jnp.sum(grad_k_normed * k_normed, axis=(0, 1))
    grad_k_raw = (
        norm_back(grad_k_normed * k_gain, k_normed, k_inverse)
        .astype(bf16)
        .reshape(seq_len, kv_cols)
    )
    grad_kv = jnp.concatenate([grad_k_raw, grad_values.astype(bf16).reshape(seq_len, kv_cols)], 1)
    grad_w_q = jnp.einsum("sd,sc->dc", attn_all, grad_q_raw, preferred_element_type=f32)
    grad_w_kv = jnp.einsum("sd,sc->dc", attn_all, grad_kv, preferred_element_type=f32).reshape(
        model_width, 2, kv_cols
    )
    grad_attn_in = lax.psum_scatter(
        (
            jnp.einsum("sc,dc->sd", grad_q_raw, w_q, preferred_element_type=f32)
            + jnp.einsum("sc,dc->sd", grad_kv, w_kv_flat, preferred_element_type=f32)
        ).astype(jnp.bfloat16),
        "tensor",
        scatter_dimension=0,
        tiled=True,
    ).astype(jnp.float32)
    gain_attn_part = jnp.sum(grad_attn_in * normed1, axis=0)
    grad_tokens = grad_resid + norm_back(grad_attn_in * gain_attn, normed1, inverse1)
    gain_sums = lax.psum(
        (gain_attn_part, gain_ffn_part, q_gain_part, k_gain_part), ("dp", "tensor")
    )
    shard_q, shard_kv, shard_o, shard_gu, shard_down = (
        lax.psum_scatter(
            grad_w_q.astype(jnp.bfloat16), "dp", scatter_dimension=0, tiled=True
        ).astype(jnp.float32),
        lax.psum_scatter(
            grad_w_kv.astype(jnp.bfloat16), "dp", scatter_dimension=0, tiled=True
        ).astype(jnp.float32),
        lax.psum_scatter(
            grad_w_o.astype(jnp.bfloat16), "dp", scatter_dimension=1, tiled=True
        ).astype(jnp.float32),
        lax.psum_scatter(
            grad_w_gu.astype(jnp.bfloat16), "dp", scatter_dimension=0, tiled=True
        ).astype(jnp.float32),
        lax.psum_scatter(
            grad_down.astype(jnp.bfloat16), "dp", scatter_dimension=1, tiled=True
        ).astype(jnp.float32),
    )
    return (
        output,
        grad_tokens,
        gain_sums[0],
        shard_q,
        shard_kv,
        gain_sums[2],
        gain_sums[3],
        shard_o,
        gain_sums[1],
        shard_gu,
        shard_down,
    )


def solution(mesh):
    in_specs = (
        P(("dp", "tensor"), None),
        P("dp", None),
        P(),
        P(None, "tensor"),
        P(None, None, "tensor"),
        P(),
        P(),
        P("tensor", None),
        P(),
        P(None, None, "tensor"),
        P("tensor", None),
        P(("dp", "tensor"), None),
    )
    out_specs = (
        P(("dp", "tensor"), None),
        P(("dp", "tensor"), None),
        P(),
        P("dp", "tensor"),
        P("dp", None, "tensor"),
        P(),
        P(),
        P("tensor", "dp"),
        P(),
        P("dp", None, "tensor"),
        P("tensor", "dp"),
    )
    paired_axes = mesh.shape["tensor"] == 2 and mesh.shape["dp"] == 16
    body = functools.partial(paired, mesh.shape["dp"]) if paired_axes else shards
    return jax.shard_map(body, mesh=mesh, in_specs=in_specs, out_specs=out_specs, check_vma=False)
```

```python
import functools
import math

import jax
import jax.numpy as jnp
from jax import lax
from jax.experimental import pallas as pl
from jax.experimental.pallas import tpu as pltpu
from jax.sharding import PartitionSpec as P

EPS = 1e-06
THETA = 1000000.0
LOG2E = 1.4426950408889634
LN2 = 0.6931471805599453
BLOCK = 256
PAIR = 128
SAME = 256.0
F32 = jnp.float32
BF16 = jnp.bfloat16
COST_RATE = 1.0e13
VMEM_LIMIT = 56 * 1024 * 1024
BACK_VMEM = 61 * 1024 * 1024


def dot_nn(a, b):
    return lax.dot_general(a, b, (((1,), (0,)), ((), ())), preferred_element_type=F32)


def dot_nt(a, b):
    return lax.dot_general(a, b, (((1,), (1,)), ((), ())), preferred_element_type=F32)


def cost(seconds):
    return pl.CostEstimate(flops=int(seconds * COST_RATE), bytes_accessed=0, transcendentals=0)


def lane_of(shape):
    return lax.broadcasted_iota(jnp.int32, shape, len(shape) - 1)


def head_mean(values):
    high = values.astype(BF16)
    low = (values - high.astype(F32)).astype(BF16)
    row = lax.broadcasted_iota(jnp.int32, (PAIR, PAIR), 0) // 64
    col = lax.broadcasted_iota(jnp.int32, (PAIR, PAIR), 1) // 64
    mean = jnp.where(row == col, 1.0 / 64.0, 0.0).astype(BF16)
    return dot_nn(high, mean) + dot_nn(low, mean)


def swap_halves(values):
    first = lane_of(values.shape) % 64 < 32
    return jnp.where(first, pltpu.roll(values, 96, 1), pltpu.roll(values, 32, 1))


def rope(values, cosine, sine):
    return values * cosine + swap_halves(values) * sine


def row_norm(x):
    return lax.rsqrt(jnp.mean(x * x, axis=-1, keepdims=True) + EPS)


def qkv_kernel(
    x_ref, gain_ref, wq_ref, wk_ref, wv_ref, qg_ref, kg_ref, cos_ref, sin_ref,
    attn_ref, q_ref, kd_ref, vd_ref, qraw_ref, kraw_ref,
):
    x = x_ref[...].astype(F32)
    attn = (x * row_norm(x) * gain_ref[...]).astype(BF16)
    attn_ref[...] = attn
    q = dot_nn(attn, wq_ref[...])
    k = dot_nn(attn, wk_ref[...])
    v = dot_nn(attn, wv_ref[...])
    qraw_ref[...] = q.astype(BF16)
    kraw_ref[...] = k.astype(BF16)
    cosine, sine = cos_ref[...], sin_ref[...]
    for g in range(q.shape[1] // PAIR):
        at = slice(g * PAIR, (g + 1) * PAIR)
        u = q[:, at]
        n = u * lax.rsqrt(head_mean(u * u) + EPS)
        q_ref[:, at] = (rope(n * qg_ref[...], cosine, sine) * (LOG2E / 8.0)).astype(BF16)
    low = lane_of((x.shape[0], PAIR)) < 64
    for p in range(k.shape[1] // PAIR):
        at = slice(p * PAIR, (p + 1) * PAIR)
        u = k[:, at]
        n = u * lax.rsqrt(head_mean(u * u) + EPS)
        roped = rope(n * kg_ref[...], cosine, sine)
        for src, dst in ((roped, kd_ref), (v[:, at], vd_ref)):
            turned = pltpu.roll(src, 64, 1)
            dst[:, 2 * p * PAIR : (2 * p + 1) * PAIR] = jnp.where(low, src, turned).astype(BF16)
            dst[:, (2 * p + 1) * PAIR : (2 * p + 2) * PAIR] = jnp.where(low, turned, src).astype(BF16)


def qkv(x, gain, w_q, w_kv, qg, kg, cosine, sine, half):
    rows, width = x.shape
    qc, kc = w_q.shape[1], w_kv.shape[1] // 2
    nb = rows // BLOCK
    whole = lambda shape, *at: pl.BlockSpec(shape, lambda i: at)
    row = lambda cols: pl.BlockSpec((BLOCK, cols), lambda i: (i, 0))
    table = pl.BlockSpec((BLOCK, PAIR), lambda i: (i + half * nb, 0))
    return pl.pallas_call(
        qkv_kernel,
        grid=(nb,),
        in_specs=[
            row(width), whole((1, width), 0, 0), whole((width, qc), 0, 0),
            whole((width, kc), 0, 0), whole((width, kc), 0, 1),
            whole((1, PAIR), 0, 0), whole((1, PAIR), 0, 0), table, table,
        ],
        out_specs=[row(width), row(qc), row(2 * kc), row(2 * kc), row(qc), row(kc)],
        out_shape=[
            jax.ShapeDtypeStruct((rows, c), BF16) for c in (width, qc, 2 * kc, 2 * kc, qc, kc)
        ],
        compiler_params=pltpu.CompilerParams(vmem_limit_bytes=VMEM_LIMIT),
        cost_estimate=cost(5e-6),
        name="qkv",
    )(x, gain, w_q, w_kv, w_kv, qg, kg, cosine, sine)


MESH = pl.DeviceIdType.MESH
CHUNK = 768
SPLIT = 512
DEPTH = 3


def dot_tn(a, b):
    return lax.dot_general(a, b, (((0,), (0,)), ((), ())), preferred_element_type=F32)


def pack_columns(dst, first, ref):
    rows, width = ref.shape
    low = lane_of((rows, PAIR)) < 64
    for k in range(width // (2 * PAIR)):
        a = ref[:, 2 * k * PAIR : (2 * k + 1) * PAIR].astype(F32)
        b = ref[:, (2 * k + 1) * PAIR : (2 * k + 2) * PAIR].astype(F32)
        lanes = slice(k * PAIR, (k + 1) * PAIR)
        dst[0, first : first + rows, lanes] = jnp.where(low, a, pltpu.roll(b, 64, 1)).astype(BF16)
        dst[1, first : first + rows, lanes] = jnp.where(low, pltpu.roll(a, 64, 1), b).astype(BF16)


BACK_INPUTS = (
    "h_own", "h_oth", "cot_pack", "ffn_pack", "attn_pack", "tok_own", "tok_oth", "y_send", "branch", "do_own", "do_send",
    "w_q", "w_kv", "q_own", "q_oth", "kd_own", "kd_oth", "vd_own", "vd_oth", "o_own", "o_oth", "linv_own", "linv_oth",
    "qraw_own", "qraw_oth", "kraw_own", "kraw_oth",
)
BACK_TABLES = ("segq", "segk", "cos", "sin", "gain_ffn", "qg", "kg")
BACK_OUTPUTS = ("ga_out", "ga_recv", "shards", "gains", "y_recv")


class Names:
    def __init__(self, names, refs):
        self.__dict__.update(zip(names, refs))


def back_kernel(n_dp, scratch_names, *refs):
    m = Names(BACK_INPUTS + BACK_TABLES + BACK_OUTPUTS + scratch_names, refs)
    rows, width = m.tok_own.shape
    hidden = m.h_own.shape[2]
    per_x = hidden // CHUNK
    n_wide = 3 * per_x
    n_chunks = n_wide + 2
    nb = 2 * rows // BLOCK
    t = lax.axis_index("tensor")
    d = lax.axis_index("dp")
    core = lax.rem(d, 2)
    x = lax.rem(d // 2, 2)
    zl = lax.rem(d // 4, 2)
    zh = d // 8
    over_t = {"tensor": 1 - t}
    over_core = {"dp": d + 1 - 2 * core}
    over_x = {"dp": d + 2 - 4 * x}
    over_zl = {"dp": d + 4 - 8 * zl}
    over_zh = {"dp": d + 8 - 16 * zh}
    partners = (over_t, over_core, over_x, over_zl, over_zh)
    low = lane_of((rows, PAIR)) < 64
    own_rows, oth_rows = pl.ds(0, rows), pl.ds(rows, rows)

    barrier = pltpu.get_barrier_semaphore()
    for p in partners:
        pl.semaphore_signal(barrier, inc=1, device_id=p, device_id_type=MESH)
    pl.semaphore_wait(barrier, len(partners))

    def tensor_copy(i, src, dst):
        return pltpu.make_async_remote_copy(
            src_ref=src, dst_ref=dst, send_sem=m.t_send.at[i], recv_sem=m.t_recv.at[i],
            device_id=over_t, device_id_type=MESH,
        )

    do_copy = tensor_copy(1, m.do_send, m.do_recv)
    branch_copy = tensor_copy(2, m.branch_v, m.branch_recv)
    y_copy = tensor_copy(3, m.y_send, m.y_recv)
    ga_copy = tensor_copy(4, m.branch_v, m.ga_recv)

    def rs_copy(stage, c, src, dst, device):
        return pltpu.make_async_remote_copy(
            src_ref=src, dst_ref=dst, send_sem=m.rs_send.at[stage, c], recv_sem=m.rs_recv.at[stage, c],
            device_id=device, device_id_type=MESH,
        )

    left, right = pl.ds(0, SPLIT), pl.ds(SPLIT, CHUNK - SPLIT)
    every = pl.ds(0, 2)
    block_rows = m.sums.shape[4]
    full_rows = pl.ds(0, block_rows)

    def core_copy(c):
        return rs_copy(0, c, m.core_send.at[lax.rem(c, 2)], m.sums.at[c], over_core)

    def first_copies(c):
        return (
            rs_copy(1, c, m.sums.at[c, every, every, 1 - x, full_rows, left], m.r1a.at[c], over_x),
            rs_copy(2, c, m.sums.at[c, every, 1 - zl, every, full_rows, right], m.r1b.at[c], over_zl),
        )

    def second_copies(c):
        return (
            rs_copy(3, c, m.sums.at[c, every, 1 - zl, x, full_rows, left], m.r2a.at[c], over_zl),
            rs_copy(4, c, m.sums.at[c, every, zl, 1 - x, full_rows, right], m.r2b.at[c], over_x),
        )

    def third_copy(c):
        return rs_copy(5, c, m.sums.at[c, 1 - zh, zl, x], m.r3.at[c], over_zh)

    def local(i, src, dst):
        return pltpu.make_async_copy(src, dst, m.l_sem.at[i])

    def both(i, src_own, src_oth, dst):
        return (local(i, src_own, dst.at[own_rows]), local(i + 1, src_oth, dst.at[oth_rows]))

    def start(copies):
        for copy in copies:
            copy.start()

    def wait(copies):
        for copy in copies:
            copy.wait()

    def add_core(c):
        core_copy(c).wait_recv()
        for a in range(2):
            for b in range(2):
                for e in range(2):
                    m.sums[c, a, b, e] = (
                        m.sums[c, a, b, e].astype(F32) + m.kept[lax.rem(c, 2), a, b, e].astype(F32)
                    ).astype(BF16)

    def total_copy(c):
        slot = lax.rem(c, 2)
        return pltpu.make_async_copy(m.totals.at[slot], m.shards.at[c], m.s_sem.at[slot])

    def tick(i):
        @pl.when(i < n_chunks)
        def _():
            a_copy, b_copy = first_copies(i)
            a_copy.wait_recv()
            b_copy.wait_recv()
            for a in range(2):
                for b in range(2):
                    m.sums[i, a, b, x, :, :SPLIT] = (
                        m.sums[i, a, b, x, :, :SPLIT].astype(F32) + m.r1a[i, a, b].astype(F32)
                    ).astype(BF16)
                    m.sums[i, a, zl, b, :, SPLIT:] = (
                        m.sums[i, a, zl, b, :, SPLIT:].astype(F32) + m.r1b[i, a, b].astype(F32)
                    ).astype(BF16)
            start(second_copies(i))

        @pl.when(i + DEPTH < n_chunks - 1)
        def _():
            start(first_copies(i + DEPTH))

        @pl.when((i >= 1) & (i < n_chunks + 1))
        def _():
            c = i - 1
            a_copy, b_copy = second_copies(c)
            a_copy.wait_recv()
            b_copy.wait_recv()
            for a in range(2):
                m.sums[c, a, zl, x, :, :SPLIT] = (
                    m.sums[c, a, zl, x, :, :SPLIT].astype(F32) + m.r2a[c, a].astype(F32)
                ).astype(BF16)
                m.sums[c, a, zl, x, :, SPLIT:] = (
                    m.sums[c, a, zl, x, :, SPLIT:].astype(F32) + m.r2b[c, a].astype(F32)
                ).astype(BF16)
            third_copy(c).start()

        @pl.when((i >= 2) & (i < n_chunks + 2))
        def _():
            c = i - 2
            third_copy(c).wait_recv()

            @pl.when(c >= 2)
            def _():
                total_copy(c - 2).wait()

            m.totals[lax.rem(c, 2)] = m.sums[c, zh, zl, x].astype(F32) + m.r3[c].astype(F32)
            total_copy(c).start()

    def put(ref, slot, lanes, value):
        for a in range(2):
            for b in range(2):
                for e in range(2):
                    k = ((a * 2 + b) * 2 + e) * block_rows
                    ref[slot, a, b, e, :, lanes] = value[k : k + block_rows].astype(BF16)

    do_copy.start()
    packs = [local(i, src, m.packed.at[i]) for i, src in enumerate((m.cot_pack, m.ffn_pack))]
    attn_load = local(0, m.attn_pack, m.packed.at[0])
    start(packs)
    loads = [
        local(2, m.branch, m.branch_v), local(3, m.do_own, m.do_v), local(7, m.w_q, m.wq_v), local(8, m.w_kv, m.wkv_v),
        *both(9, m.o_own, m.o_oth, m.o_v), *both(11, m.kraw_own, m.kraw_oth, m.kraw_v),
    ]

    def tiles(g):
        slot = lax.rem(g, 2)
        lanes = pl.ds(pl.multiple_of(g * PAIR, PAIR), PAIR)
        out = []
        for j, (own, oth, dst) in enumerate((
            (m.q_own, m.q_oth, m.q_v), (m.kd_own, m.kd_oth, m.kd_v), (m.vd_own, m.vd_oth, m.vd_v),
            (m.qraw_own, m.qraw_oth, m.qraw_v), (m.linv_own, m.linv_oth, m.linv_v),
        )):
            out.append(pltpu.make_async_copy(own.at[:, lanes], dst.at[slot, own_rows], m.g_sem.at[slot, 2 * j]))
            out.append(pltpu.make_async_copy(oth.at[:, lanes], dst.at[slot, oth_rows], m.g_sem.at[slot, 2 * j + 1]))
        return out

    def wide_phase(y_v):
        def fetch(c):
            slot = lax.rem(c, 2)
            cols = pl.ds(pl.multiple_of(lax.rem(c, per_x) * CHUNK, CHUNK), CHUNK)
            return [
                pltpu.make_async_copy(
                    h.at[c // per_x, :, cols], y_v.at[slot, at], m.h_sem.at[slot, j]
                )
                for j, (h, at) in enumerate(((m.h_own, own_rows), (m.h_oth, oth_rows)))
            ]

        start(fetch(0))
        start(loads)
        packs[0].wait()

        def chunk(c, which):
            slot = lax.rem(c, 2)
            wait(fetch(c))

            @pl.when(c + 1 < n_wide)
            def _():
                start(fetch(c + 1))

            @pl.when(c >= 2)
            def _():
                core_copy(c - 2).wait_send()

            put(m.core_send, slot, slice(None), dot_tn(m.packed[which, 1 - core], y_v[slot]))
            core_copy(c).start()
            put(m.kept, slot, slice(None), dot_tn(m.packed[which, core], y_v[slot]))

            @pl.when(c >= 1)
            def _():
                add_core(c - 1)

            @pl.when((c >= 1) & (c <= DEPTH))
            def _():
                start(first_copies(c - 1))

            @pl.when((c == n_wide - 4) | (c == n_wide - 2))
            def _():
                tick((c - n_wide + 4) // 2)

        def first(c, carry):
            chunk(c, 0)
            return carry

        lax.fori_loop(0, per_x, first, 0)
        packs[1].wait()
        attn_load.start()

        def second(c, carry):
            chunk(c, 1)
            return carry

        lax.fori_loop(per_x, n_wide, second, 0)
        add_core(n_wide - 1)
        tick(2)

    pl.run_scoped(wide_phase, pltpu.VMEM((2, 2 * rows, CHUNK), BF16))
    start(tiles(0))

    wait(loads)
    attn_load.wait()
    branch_copy.start()
    do_copy.wait_recv()

    def narrow_chunk(p):
        c = n_wide + p
        slot = lax.rem(c, 2)
        core_copy(c - 2).wait_send()
        cols = pl.ds(pl.multiple_of(p * SPLIT, SPLIT), SPLIT)
        o_cols = pl.ds(pl.multiple_of(p * (CHUNK - SPLIT), CHUNK - SPLIT), CHUNK - SPLIT)
        for which, dst in ((1 - core, m.core_send), (core, m.kept)):
            put(dst, slot, slice(0, SPLIT), dot_tn(m.packed[0, which], m.g_v[:, cols]))
            put(dst, slot, slice(SPLIT, CHUNK), dot_tn(m.packed[1, which], m.o_v[:, o_cols]))
        core_copy(c).start()

    def place(block):
        return pl.ds(pl.multiple_of(lax.rem(block + t * (nb // 2), nb) * BLOCK, BLOCK), BLOCK)

    m.qgain[...] = jnp.zeros_like(m.qgain)
    m.kgain[...] = jnp.zeros_like(m.kgain)

    def attention_phase(qx, dox, kx0, kx1, vx0, vx1, kt, dqt, dk0, dk1, dv0, dv1, dks, dvs):
        all_low = lane_of((2 * rows, PAIR)) < 64
        one = jnp.ones((2 * rows, PAIR), F32)
        zero = jnp.zeros((2 * rows, PAIR), BF16)
        qx[:, PAIR:] = m.segq[...]
        kx0[:, PAIR:] = m.segk[...]
        kx1[:, PAIR:] = m.segk[...]
        vx0[:, PAIR:] = jnp.where(all_low, -one, 0.0).astype(BF16)
        vx1[:, PAIR:] = jnp.where(all_low, 0.0, -one).astype(BF16)

        def step(qb, kb, diagonal):
            qs, ks = place(qb), place(kb)
            q, do = qx[qs, :], dox[qs, :]
            for h, (kx, vx, dk, dv) in enumerate(((kx0, vx0, dk0, dv0), (kx1, vx1, dk1, dv1))):
                s = dot_nt(kx[ks, :], q)
                if diagonal:
                    r = lax.broadcasted_iota(jnp.int32, s.shape, 0)
                    s = jnp.where(r <= lane_of(s.shape), s, -1e30)
                e = jnp.exp2(s)
                ds = (e * dot_nt(vx[ks, :], do)).astype(BF16)
                dv[ks, :] += dot_nn(e.astype(BF16), do[:, :PAIR])
                dk[ks, :] += dot_nn(ds, q[:, :PAIR])
                dqt[h * 64 : (h + 1) * 64, qs] += dot_nn(kt[:, ks], ds)

        def group(g, carry):
            slot = lax.rem(g, 2)
            lanes = pl.ds(pl.multiple_of(g * PAIR, PAIR), PAIR)
            p = g // 2
            wait(tiles(g))

            @pl.when(g + 1 < 4)
            def _():
                start(tiles(g + 1))

            qx[:, :PAIR] = m.q_v[slot]
            k, v = m.kd_v[slot], m.vd_v[slot]
            kx0[:, :PAIR] = jnp.where(all_low, k, zero)
            kx1[:, :PAIR] = jnp.where(all_low, zero, k)
            vx0[:, :PAIR] = jnp.where(all_low, v, zero)
            vx1[:, :PAIR] = jnp.where(all_low, zero, v)
            kt[...] = jnp.transpose(k.astype(F32))[:64, :].astype(BF16)
            for at, do_ref in ((own_rows, m.do_v), (oth_rows, m.do_recv)):
                scaled = do_ref[:, lanes].astype(F32) * m.linv_v[slot, at, :]
                dox[at, :PAIR] = scaled.astype(BF16)
                dox[at, PAIR:] = (scaled * m.o_v[at, lanes].astype(F32)).astype(BF16)
            for ref in (dqt, dk0, dk1, dv0, dv1):
                ref[...] = jnp.zeros_like(ref)

            def q_body(qb, c):
                step(qb, qb, True)

                def k_body(kb, cc):
                    step(qb, kb, False)
                    return cc

                lax.fori_loop(jnp.maximum(qb - 2, 0), qb, k_body, 0)
                return c

            lax.fori_loop(0, nb, q_body, 0)

            @pl.when(g == 1)
            def _():
                tick(4)

            g_lanes = pl.ds(pl.multiple_of(p * SPLIT + slot * PAIR, PAIR), PAIR)
            for at in (own_rows, oth_rows):
                dq = jnp.transpose(dqt[:, at]) * 0.125
                normed_grad = rope(dq, m.cos[at, :], -m.sin[at, :])
                raw = m.qraw_v[slot, at, :].astype(F32)
                inverse = lax.rsqrt(head_mean(raw * raw) + EPS)
                u = raw * inverse
                m.qgain[...] += jnp.sum(normed_grad * u, axis=0, keepdims=True)
                w = normed_grad * m.qg[...]
                m.g_v[at, g_lanes] = (inverse * (w - u * head_mean(w * u))).astype(BF16)

            def gathered(a, b, at):
                joined = jnp.where(low, a[at, :], b[at, :])
                return joined + pltpu.roll(joined, 64, 1)

            @pl.when(slot == 0)
            def _():
                for at in (own_rows, oth_rows):
                    dks[at, :] = gathered(dk0, dk1, at)
                    dvs[at, :] = gathered(dv0, dv1, at)

            @pl.when(slot == 1)
            def _():
                k_lanes = pl.ds(pl.multiple_of(p * SPLIT + 2 * PAIR, PAIR), PAIR)
                v_lanes = pl.ds(pl.multiple_of(p * SPLIT + 3 * PAIR, PAIR), PAIR)
                raw_lanes = pl.ds(pl.multiple_of(p * PAIR, PAIR), PAIR)
                for at in (own_rows, oth_rows):
                    dk = jnp.where(low, dks[at, :], gathered(dk0, dk1, at)) * LN2
                    dv = jnp.where(low, dvs[at, :], gathered(dv0, dv1, at))
                    normed_grad = rope(dk, m.cos[at, :], -m.sin[at, :])
                    raw = m.kraw_v[at, raw_lanes].astype(F32)
                    inverse = lax.rsqrt(head_mean(raw * raw) + EPS)
                    u = raw * inverse
                    m.kgain[...] += jnp.sum(normed_grad * u, axis=0, keepdims=True)
                    w = normed_grad * m.kg[...]
                    m.g_v[at, k_lanes] = (inverse * (w - u * head_mean(w * u))).astype(BF16)
                    m.g_v[at, v_lanes] = dv.astype(BF16)

                @pl.when(p == 0)
                def _():
                    branch_copy.wait_recv()
                    y_copy.start()
                    pack_columns(m.packed.at[1], 0, m.branch_v)
                    pack_columns(m.packed.at[1], rows, m.branch_recv)

                narrow_chunk(p)

            @pl.when(g == 2)
            def _():
                add_core(n_wide)

            tick(3 + g + jnp.minimum(g, 1))
            return carry

        lax.fori_loop(0, 4, group, 0)

    pl.run_scoped(
        attention_phase,
        *[pltpu.VMEM((2 * rows, 2 * PAIR), BF16)] * 6,
        pltpu.VMEM((64, 2 * rows), BF16), pltpu.VMEM((PAIR, 2 * rows), F32),
        *[pltpu.VMEM((2 * rows, PAIR), F32)] * 6,
    )

    def attn_in_grad(at):
        out = None
        qc, kc = m.wq_v.shape[1], m.wkv_v.shape[1] // 2
        for p in range(2):
            for ref, base, begin, size in (
                (m.wq_v, 0, 0, 2 * PAIR), (m.wkv_v, 0, 2 * PAIR, PAIR), (m.wkv_v, kc, 3 * PAIR, PAIR)
            ):
                term = dot_nt(
                    m.g_v[at, p * SPLIT + begin : p * SPLIT + begin + size],
                    ref[:, base + p * size : base + (p + 1) * size],
                )
                out = term if out is None else out + term
        return out

    def end_phase(ga_own, tok_v):
        start(both(0, m.tok_own, m.tok_oth, tok_v))
        wait(both(0, m.tok_own, m.tok_oth, tok_v))

        def grad_and_gain(at):
            grad = attn_in_grad(at)
            tokens = tok_v[at, :].astype(F32)
            return grad, jnp.sum(grad * (tokens * row_norm(tokens)), axis=0, keepdims=True)

        branch_copy.wait_send()
        total = jnp.zeros((1, width), F32)
        for i in range(rows // BLOCK):
            grad, part = grad_and_gain(pl.ds(rows + i * BLOCK, BLOCK))
            m.branch_v[i * BLOCK : (i + 1) * BLOCK, :] = grad.astype(BF16)
            total += part
        ga_copy.start()
        add_core(n_chunks - 1)
        start(first_copies(n_chunks - 1))
        tick(n_chunks - 3)
        for i in range(rows // BLOCK):
            grad, part = grad_and_gain(pl.ds(i * BLOCK, BLOCK))
            ga_own[i * BLOCK : (i + 1) * BLOCK, :] = grad
            total += part
        ga_out_copy = local(3, ga_own, m.ga_out)
        ga_out_copy.start()
        for r in range(width // PAIR):
            m.mine[r : r + 1, :] = total[:, r * PAIR : (r + 1) * PAIR]
            at = slice(width // PAIR + r, width // PAIR + r + 1)
            m.mine[at, :] = m.gain_ffn[:, r * PAIR : (r + 1) * PAIR]
        last = 2 * width // PAIR
        m.mine[last : last + 1, :] = m.qgain[...]
        m.mine[last + 1 : last + 2, :] = m.kgain[...]
        m.mine[last + 2 :, :] = jnp.zeros((m.mine.shape[0] - last - 2, PAIR), F32)

        def gain_copy(i, device):
            return pltpu.make_async_remote_copy(
                src_ref=m.gain_out.at[i], dst_ref=m.gain_in.at[i], send_sem=m.gain_sem.at[0, i],
                recv_sem=m.gain_sem.at[1, i], device_id=device, device_id_type=MESH,
            )

        for i, device in enumerate(partners):
            m.gain_out[i] = m.mine[...]
            gain_copy(i, device).start()
            if i >= 1:
                tick(n_chunks - 3 + i)
            gain_copy(i, device).wait_recv()
            m.mine[...] += m.gain_in[i]
        m.gains[...] = m.mine[...]
        y_copy.wait_recv()
        ga_copy.wait_recv()
        for copy in (do_copy, y_copy, ga_copy):
            copy.wait_send()
        for i, device in enumerate(partners):
            gain_copy(i, device).wait_send()
        for c in (n_chunks - 2, n_chunks - 1):
            core_copy(c).wait_send()

        def drain(c, carry):
            for copy in (*first_copies(c), *second_copies(c), third_copy(c)):
                copy.wait_send()
            return carry

        lax.fori_loop(0, n_chunks, drain, 0)
        for c in (n_chunks - 2, n_chunks - 1):
            total_copy(c).wait()
        ga_out_copy.wait()

    pl.run_scoped(end_phase, pltpu.VMEM((rows, width), F32), pltpu.VMEM((2 * rows, width), BF16))


def back(n_dp, values, tables):
    rows, width = values["tok_own"].shape
    hidden = values["h_own"].shape[2]
    seq = 2 * rows
    qc = values["w_q"].shape[1]
    n_chunks = 3 * hidden // CHUNK + 2
    block = width // n_dp
    vm = pltpu.VMEM
    dma = pltpu.SemaphoreType.DMA
    scratch = dict(
        packed=vm((2, 2, seq, width // 2), BF16),
        core_send=vm((2, 2, 2, 2, block, CHUNK), BF16), kept=vm((2, 2, 2, 2, block, CHUNK), BF16),
        sums=vm((n_chunks, 2, 2, 2, block, CHUNK), BF16),
        r1a=vm((n_chunks, 2, 2, block, SPLIT), BF16), r1b=vm((n_chunks, 2, 2, block, CHUNK - SPLIT), BF16),
        r2a=vm((n_chunks, 2, block, SPLIT), BF16), r2b=vm((n_chunks, 2, block, CHUNK - SPLIT), BF16),
        r3=vm((n_chunks, block, CHUNK), BF16), totals=vm((2, block, CHUNK), F32),
        wq_v=vm((width, qc), BF16), wkv_v=vm((width, qc), BF16),
        o_v=vm((seq, qc), BF16), kraw_v=vm((seq, qc // 2), BF16),
        q_v=vm((2, seq, PAIR), BF16), kd_v=vm((2, seq, PAIR), BF16), vd_v=vm((2, seq, PAIR), BF16),
        qraw_v=vm((2, seq, PAIR), BF16), linv_v=vm((2, seq, PAIR), F32),
        g_v=vm((seq, 2 * SPLIT), BF16), do_v=vm((rows, qc), BF16),
        do_recv=vm((rows, qc), BF16),
        branch_v=vm((rows, width), BF16), branch_recv=vm((rows, width), BF16),
        qgain=vm((1, PAIR), F32), kgain=vm((1, PAIR), F32), mine=vm((24, PAIR), F32),
        gain_out=vm((5, 24, PAIR), F32), gain_in=vm((5, 24, PAIR), F32),
        t_send=dma((5,)), t_recv=dma((5,)), rs_send=dma((6, n_chunks)), rs_recv=dma((6, n_chunks)),
        l_sem=dma((14,)), g_sem=dma((2, 10)), h_sem=dma((2, 2)), s_sem=dma((2,)), gain_sem=dma((2, 5)),
    )
    anywhere = pl.BlockSpec(memory_space=pl.ANY)
    vmem = pl.BlockSpec(memory_space=pltpu.VMEM)
    return pl.pallas_call(
        functools.partial(back_kernel, n_dp, tuple(scratch)),
        in_specs=[anywhere] * len(BACK_INPUTS) + [vmem] * len(BACK_TABLES),
        out_specs=[anywhere, anywhere, anywhere, vmem, anywhere],
        out_shape=[
            jax.ShapeDtypeStruct((rows, width), F32),
            jax.ShapeDtypeStruct((rows, width), BF16),
            jax.ShapeDtypeStruct((n_chunks, block, CHUNK), F32), jax.ShapeDtypeStruct((24, PAIR), F32),
            jax.ShapeDtypeStruct((rows, width), BF16),
        ],
        scratch_shapes=list(scratch.values()),
        compiler_params=pltpu.CompilerParams(
            vmem_limit_bytes=BACK_VMEM, collective_id=0, has_side_effects=True
        ),
        cost_estimate=cost(100e-6),
        name="back",
    )(*[values[k] for k in BACK_INPUTS], *[tables[k] for k in BACK_TABLES])


FRONT_INPUTS = (
    "tok_own", "tok_oth", "cot_own", "w_q", "w_kv", "w_o", "w_gu", "w_down",
    "q_own", "kd_own", "vd_own", "attn_own",
)
FRONT_TABLES = ("segq", "segk", "cos", "sin", "gain1", "gain2", "qg", "kg")
FRONT_OUTPUTS = (
    "q_oth", "kd_oth", "vd_oth", "qraw_oth", "kraw_oth", "o_own", "o_oth", "linv_own", "linv_oth",
    "cot_pack", "ffn_pack", "attn_pack", "h_own", "h_oth", "base", "y_send", "gres", "branch", "do_own", "do_send",
    "gain_ffn",
)
PIECES = 4


def front_kernel(scratch_names, *refs):
    m = Names(FRONT_INPUTS + FRONT_TABLES + FRONT_OUTPUTS + scratch_names, refs)
    rows, width = m.tok_own.shape
    hidden = m.w_down.shape[0]
    qc = m.w_q.shape[1]
    kc = m.w_kv.shape[1] // 2
    nb = 2 * rows // BLOCK
    t = lax.axis_index("tensor")
    d = lax.axis_index("dp")
    core = lax.rem(d, 2)
    over_t = {"tensor": 1 - t}
    over_core = {"dp": d + 1 - 2 * core}

    barrier = pltpu.get_barrier_semaphore()
    for p in (over_t, over_core):
        pl.semaphore_signal(barrier, inc=1, device_id=p, device_id_type=MESH)
    pl.semaphore_wait(barrier, 2)

    def remote(i, src, dst, device):
        return pltpu.make_async_remote_copy(
            src_ref=src, dst_ref=dst, send_sem=m.r_send.at[i], recv_sem=m.r_recv.at[i],
            device_id=device, device_id_type=MESH,
        )

    pieces = [pl.ds(i * (rows // PIECES), rows // PIECES) for i in range(PIECES)]
    halves = [pl.ds(i * BLOCK, BLOCK) for i in range(rows // BLOCK)]
    cot_copies = [remote(i, m.cot_own.at[at], m.cot_v.at[1, at], over_t) for i, at in enumerate(pieces)]
    half_o = qc // 2
    mine_o = pl.ds(pl.multiple_of(core * half_o, half_o), half_o)
    wo_copy = remote(4, m.w_o.at[mine_o], m.wot_v.at[mine_o], over_t)
    wo_core = remote(5, m.wot_v.at[mine_o], m.wot_v.at[mine_o], over_core)
    o_copy = remote(6, m.o_v.at[1], m.theirs, over_t)
    ffn_copies = [remote(7 + i, m.ffn_v.at[0, at], m.ffn_v.at[1, at], over_t) for i, at in enumerate(halves)]
    gf_copies = [remote(9 + i, m.gf_send.at[at], m.gf_in.at[at], over_t) for i, at in enumerate(halves)]

    def local(i, src, dst):
        return pltpu.make_async_copy(src, dst, m.l_sem.at[i])

    loads = [
        local(i, src, dst)
        for i, (src, dst) in enumerate((
            (m.tok_oth, m.tok_v.at[1]), (m.w_q, m.wq_v), (m.w_kv, m.wkv_v), (m.q_own, m.q_v.at[0]),
            (m.kd_own, m.kd_v.at[0]), (m.vd_own, m.vd_v.at[0]), (m.w_o, m.wom_v), (m.tok_own, m.tok_v.at[0]),
            (m.attn_own, m.attn_v.at[0]), (m.cot_own, m.cot_v.at[0]), (m.w_gu, m.wgu_v), (m.w_down, m.wd_v),
        ))
    ]
    out_sem = [0]
    stores = []

    def store(src, dst):
        copy = pltpu.make_async_copy(src, dst, m.o_sem.at[out_sem[0]])
        out_sem[0] += 1
        copy.start()
        stores.append(copy)

    wo_copy.start()
    for copy in cot_copies[:3]:
        copy.start()
    for copy in loads:
        copy.start()
    for copy in loads[:6]:
        copy.wait()

    for at in halves:
        table = pl.ds(rows + at.start, BLOCK)
        qkv_kernel(
            m.tok_v.at[1, at], m.gain1, m.wq_v, m.wkv_v.at[:, pl.ds(0, kc)], m.wkv_v.at[:, pl.ds(kc, kc)],
            m.qg, m.kg, m.cos.at[table], m.sin.at[table],
            m.attn_v.at[1, at], m.q_v.at[1, at], m.kd_v.at[1, at], m.vd_v.at[1, at], m.qraw_v.at[at], m.kraw_v.at[at],
        )
    for src, dst in (
        (m.q_v.at[1], m.q_oth), (m.kd_v.at[1], m.kd_oth), (m.vd_v.at[1], m.vd_oth),
        (m.qraw_v, m.qraw_oth), (m.kraw_v, m.kraw_oth),
    ):
        store(src, dst)
    wo_copy.wait_recv()
    wo_core.start()

    def place(block):
        return pl.ds(pl.multiple_of(lax.rem(block + t * (nb // 2), nb) * BLOCK, BLOCK), BLOCK)

    def attention_phase(kx0, kx1, vx0, vx1, acc):
        both = lane_of((2 * rows, PAIR)) < 64
        one = jnp.ones((2 * rows, PAIR), F32)
        low = lane_of((rows, PAIR)) < 64
        zero = jnp.zeros((rows, PAIR), BF16)
        kx0[:, PAIR:] = m.segk[...]
        kx1[:, PAIR:] = m.segk[...]
        vx0[:, PAIR:] = jnp.where(both, one, 0.0).astype(BF16)
        vx1[:, PAIR:] = jnp.where(both, 0.0, one).astype(BF16)

        def half(part, first):
            def group(g, carry):
                lanes = pl.ds(pl.multiple_of(g * PAIR, PAIR), PAIR)
                for i in range(2):
                    at = pl.ds(i * rows, rows)
                    k, v = m.kd_v[i, :, lanes], m.vd_v[i, :, lanes]
                    kx0[at, :PAIR] = jnp.where(low, k, zero)
                    kx1[at, :PAIR] = jnp.where(low, zero, k)
                    vx0[at, :PAIR] = jnp.where(low, v, zero)
                    vx1[at, :PAIR] = jnp.where(low, zero, v)
                for i in range(rows // BLOCK):
                    at = pl.ds(i * BLOCK, BLOCK)
                    q = jnp.concatenate(
                        [m.q_v[part, at, lanes], m.segq[pl.ds(part * rows + i * BLOCK, BLOCK), :]], axis=1
                    )
                    block = first + i

                    def step(kb, diagonal):
                        here = place(kb)
                        total = None
                        for kx, vx in ((kx0, vx0), (kx1, vx1)):
                            s = dot_nt(q, kx[here, :])
                            if diagonal:
                                r = lax.broadcasted_iota(jnp.int32, s.shape, 0)
                                s = jnp.where(lane_of(s.shape) <= r, s, -1e30)
                            term = dot_nn(jnp.exp2(s).astype(BF16), vx[here, :])
                            total = term if total is None else total + term
                        return total

                    acc[...] = step(block, True)

                    def body(kb, c):
                        acc[...] += step(kb, False)
                        return c

                    lax.fori_loop(jnp.maximum(block - 2, 0), block, body, 0)
                    inverse = 1.0 / acc[:, PAIR:]
                    m.o_v[part, at, lanes] = (acc[:, :PAIR] * inverse).astype(BF16)
                    m.linv_v[part, at, lanes] = inverse
                return carry

            lax.fori_loop(0, qc // PAIR, group, 0)

        half(1, (1 - t) * (nb // 2))
        o_copy.start()
        half(0, t * (nb // 2))

    pl.run_scoped(
        attention_phase, *[pltpu.VMEM((2 * rows, 2 * PAIR), BF16)] * 4, pltpu.VMEM((BLOCK, 2 * PAIR), F32)
    )
    for src, dst in (
        (m.o_v.at[0], m.o_own), (m.o_v.at[1], m.o_oth), (m.linv_v.at[0], m.linv_own), (m.linv_v.at[1], m.linv_oth)
    ):
        store(src, dst)

    for copy in loads[6:9]:
        copy.wait()
    pack_columns(m.ffn_pack_v, 0, m.attn_v.at[0])
    pack_columns(m.ffn_pack_v, rows, m.attn_v.at[1])
    attn_store = local(12, m.ffn_pack_v, m.attn_pack)
    attn_store.start()
    wo_core.wait_recv()
    o_copy.wait_recv()
    for i, at in enumerate(halves):
        resid = (
            m.tok_v[0, at, :].astype(F32) + dot_nn(m.o_v[0, at, :], m.wom_v[...]) + dot_nn(m.theirs[at, :], m.wot_v[...])
        )
        m.resid_v[at, :] = resid
        m.ffn_v[0, at, :] = (resid * row_norm(resid) * m.gain2[...]).astype(BF16)
        ffn_copies[i].start()
        if i == 0:
            for copy in cot_copies[3:]:
                copy.start()

    for copy in loads[9:]:
        copy.wait()
    n_tiles = hidden // CHUNK
    h_dst = (m.h_own, m.h_oth)
    h_count = [0]

    def feed_forward(part, at):
        x, c = m.ffn_v.at[part, at], m.cot_v.at[part, at]

        def h_copy(slot, f, rows_at, dst):
            cols = pl.ds(pl.multiple_of(f * CHUNK, CHUNK), CHUNK)
            return pltpu.make_async_copy(m.h_v.at[slot], dst.at[:, rows_at, cols], m.h_sem.at[slot])

        base = h_count[0]
        h_count[0] += n_tiles

        def tile(f, carry):
            slot = lax.rem(base + f, 2)
            cols = pl.ds(pl.multiple_of(f * CHUNK, CHUNK), CHUNK)
            up_cols = pl.ds(pl.multiple_of(hidden + f * CHUNK, CHUNK), CHUNK)
            gate = dot_nn(x[...], m.wgu_v[:, cols])
            up = dot_nn(x[...], m.wgu_v[:, up_cols])
            grad = dot_nt(c[...], m.wd_v[cols, :])

            if base == 0:
                @pl.when(f >= 2)
                def _():
                    h_copy(slot, f, at, h_dst[part]).wait()
            else:
                h_copy(slot, f, at, h_dst[part]).wait()

            sig = 0.5 * jnp.tanh(0.5 * gate) + 0.5
            silu = gate * sig
            mixed = (silu * up).astype(BF16)
            gg = (grad * up * (sig + silu * (1.0 - sig))).astype(BF16)
            gu = (grad * silu).astype(BF16)
            for i, value in enumerate((mixed, gg, gu)):
                m.h_v[slot, i] = value
            h_copy(slot, f, at, h_dst[part]).start()
            y = dot_nn(mixed, m.wd_v[cols, :])
            gf = dot_nt(gg, m.wgu_v[:, cols]) + dot_nt(gu, m.wgu_v[:, up_cols])

            y_to, gf_to = (m.y_oth, m.gf_oth) if part else (m.y_v.at[at], m.gf_v.at[at])

            @pl.when(f == 0)
            def _():
                y_to[...] = y
                gf_to[...] = gf

            @pl.when(f > 0)
            def _():
                y_to[...] += y
                gf_to[...] += gf

            return carry

        lax.fori_loop(0, n_tiles, tile, 0)

    feed_forward(0, halves[0])
    pack_columns(m.cot_pack_v, 0, m.cot_v.at[0])
    attn_store.wait()
    pack_columns(m.ffn_pack_v, 0, m.ffn_v.at[0])
    for i, at in enumerate(halves):
        ffn_copies[i].wait_recv()
        for copy in cot_copies[2 * i : 2 * i + 2]:
            copy.wait_recv()
        feed_forward(1, at)
        m.gf_send[at, :] = m.gf_oth[...].astype(BF16)
        gf_copies[i].start()
        m.y_low[at, :] = m.y_oth[...].astype(BF16)
    store(m.y_low, m.y_send)
    feed_forward(0, halves[1])
    pack_columns(m.cot_pack_v, rows, m.cot_v.at[1])
    pack_columns(m.ffn_pack_v, rows, m.ffn_v.at[1])
    store(m.cot_pack_v, m.cot_pack)
    store(m.ffn_pack_v, m.ffn_pack)

    total = jnp.zeros((1, width), F32)
    for i, at in enumerate(halves):
        gf_copies[i].wait_recv()
        grad = m.gf_v[at, :] + m.gf_in[at, :].astype(F32)
        resid = m.resid_v[at, :]
        inverse = row_norm(resid)
        normed = resid * inverse
        total += jnp.sum(grad * normed, axis=0, keepdims=True)
        w = grad * m.gain2[...]
        gres = m.cot_v[0, at, :].astype(F32) + inverse * (
            w - normed * jnp.mean(w * normed, axis=-1, keepdims=True)
        )
        m.gf_v[at, :] = gres
        branch = gres.astype(BF16)
        m.branch_v[at, :] = branch
        m.do_v[0, at, :] = dot_nt(branch, m.wom_v[...]).astype(BF16)
        m.do_v[1, at, :] = dot_nt(branch, m.wot_v[...]).astype(BF16)
        m.y_v[at, :] += resid
    for src, dst in (
        (m.do_v.at[1], m.do_send), (m.do_v.at[0], m.do_own), (m.branch_v, m.branch), (m.gf_v, m.gres),
        (m.y_v, m.base),
    ):
        store(src, dst)
    m.gain_ffn[...] = total
    for copy in (*cot_copies, wo_copy, wo_core, o_copy, *ffn_copies, *gf_copies):
        copy.wait_send()
    for slot in range(2):
        pltpu.make_async_copy(m.h_v.at[slot], m.h_own.at[:, halves[1], pl.ds(0, CHUNK)], m.h_sem.at[slot]).wait()
    for copy in stores:
        copy.wait()


def front(values, tables):
    rows, width = values["tok_own"].shape
    hidden = values["w_down"].shape[0]
    qc = values["w_q"].shape[1]
    seq = 2 * rows
    vm = pltpu.VMEM
    dma = pltpu.SemaphoreType.DMA
    scratch = dict(
        tok_v=vm((2, rows, width), BF16), cot_v=vm((2, rows, width), BF16),
        wq_v=vm((width, qc), BF16), wkv_v=vm((width, qc), BF16), wom_v=vm((qc, width), BF16), wot_v=vm((qc, width), BF16),
        wgu_v=vm((width, 2 * hidden), BF16), wd_v=vm((hidden, width), BF16),
        q_v=vm((2, rows, qc), BF16), kd_v=vm((2, rows, qc), BF16), vd_v=vm((2, rows, qc), BF16),
        attn_v=vm((2, rows, width), BF16), qraw_v=vm((rows, qc), BF16), kraw_v=vm((rows, qc // 2), BF16),
        o_v=vm((2, rows, qc), BF16), linv_v=vm((2, rows, qc), F32), theirs=vm((rows, qc), BF16),
        resid_v=vm((rows, width), F32), ffn_v=vm((2, rows, width), BF16),
        h_v=vm((2, 3, BLOCK, CHUNK), BF16), y_v=vm((rows, width), F32), gf_v=vm((rows, width), F32),
        y_oth=vm((BLOCK, width), F32), gf_oth=vm((BLOCK, width), F32),
        y_low=vm((rows, width), BF16), gf_send=vm((rows, width), BF16), gf_in=vm((rows, width), BF16),
        cot_pack_v=vm((2, seq, width // 2), BF16),
        ffn_pack_v=vm((2, seq, width // 2), BF16), branch_v=vm((rows, width), BF16), do_v=vm((2, rows, qc), BF16),
        r_send=dma((11,)), r_recv=dma((11,)), l_sem=dma((13,)), o_sem=dma((20,)), h_sem=dma((2,)),
    )
    anywhere = pl.BlockSpec(memory_space=pl.ANY)
    vmem = pl.BlockSpec(memory_space=pltpu.VMEM)
    low, full = (lambda *shape: jax.ShapeDtypeStruct(shape, BF16)), (lambda *shape: jax.ShapeDtypeStruct(shape, F32))
    shapes = dict(
        q_oth=low(rows, qc), kd_oth=low(rows, qc), vd_oth=low(rows, qc),
        qraw_oth=low(rows, qc), kraw_oth=low(rows, qc // 2), o_own=low(rows, qc), o_oth=low(rows, qc),
        linv_own=full(rows, qc), linv_oth=full(rows, qc),
        cot_pack=low(2, seq, width // 2), ffn_pack=low(2, seq, width // 2), attn_pack=low(2, seq, width // 2),
        h_own=low(3, rows, hidden), h_oth=low(3, rows, hidden), base=full(rows, width), y_send=low(rows, width),
        gres=full(rows, width), branch=low(rows, width), do_own=low(rows, qc), do_send=low(rows, qc),
        gain_ffn=full(1, width),
    )
    outs = pl.pallas_call(
        functools.partial(front_kernel, tuple(scratch)),
        in_specs=[anywhere] * len(FRONT_INPUTS) + [vmem] * len(FRONT_TABLES),
        out_specs=[anywhere] * (len(FRONT_OUTPUTS) - 1) + [vmem],
        out_shape=[shapes[k] for k in FRONT_OUTPUTS],
        scratch_shapes=list(scratch.values()),
        compiler_params=pltpu.CompilerParams(
            vmem_limit_bytes=BACK_VMEM, collective_id=1, has_side_effects=True
        ),
        cost_estimate=cost(100e-6),
        name="front",
    )(*[values[k] for k in FRONT_INPUTS], *[tables[k] for k in FRONT_TABLES])
    return dict(zip(FRONT_OUTPUTS, outs))


def finish_kernel(
    base_ref, yr_ref, ga_ref, gr_ref, x_ref, gres_ref, gain_ref, shards_ref,
    out_ref, gt_ref, q_ref, kv_ref, o_ref, gu_ref, down_ref,
):
    out_ref[...] = (base_ref[...] + yr_ref[...].astype(F32)).astype(BF16)
    x = x_ref[...].astype(F32)
    inverse = row_norm(x)
    normed = x * inverse
    w = (ga_ref[...] + gr_ref[...].astype(F32)) * gain_ref[...]
    gt_ref[...] = gres_ref[...] + inverse * (w - normed * jnp.mean(w * normed, axis=-1, keepdims=True))
    n_chunks = shards_ref.shape[0]
    per_x = (n_chunks - 2) // 3
    two = 2 * PAIR
    step = pl.program_id(0)

    @pl.when(step < per_x)
    def _():
        down_ref[...] = shards_ref[step]
        gu_ref[:, 0, :] = shards_ref[per_x + step]
        gu_ref[:, 1, :] = shards_ref[2 * per_x + step]

    @pl.when(step == per_x)
    def _():
        for p in range(2):
            shard = shards_ref[3 * per_x + p]
            q_ref[:, p * two : (p + 1) * two] = shard[:, :two]
            kv_ref[:, 0, p * PAIR : (p + 1) * PAIR] = shard[:, two : two + PAIR]
            kv_ref[:, 1, p * PAIR : (p + 1) * PAIR] = shard[:, two + PAIR : 2 * two]
            o_ref[:, p * two : (p + 1) * two] = shard[:, 2 * two :]


def finish(base, y_recv, ga_own, ga_recv, x, gres, gain, shards):
    rows, width = x.shape
    n_chunks, block, _ = shards.shape
    hidden = (n_chunks - 2) // 3 * CHUNK
    per_x = hidden // CHUNK
    row = pl.BlockSpec((rows // (per_x + 1), width), lambda i: (i, 0))
    fixed = lambda shape: pl.BlockSpec(shape, lambda i: (0,) * len(shape))
    shapes = [(block, SPLIT), (block, 2, SPLIT // 2), (block, SPLIT), (block, 2, hidden), (block, hidden)]
    piece = lambda i: jnp.minimum(i, per_x - 1)
    return pl.pallas_call(
        finish_kernel,
        grid=(per_x + 1,),
        in_specs=[row] * 6 + [fixed((1, width)), fixed(shards.shape)],
        out_specs=[row, row]
        + [fixed(shape) for shape in shapes[:3]]
        + [
            pl.BlockSpec((block, 2, CHUNK), lambda i: (0, 0, piece(i))),
            pl.BlockSpec((block, CHUNK), lambda i: (0, piece(i))),
        ],
        out_shape=[jax.ShapeDtypeStruct((rows, width), BF16), jax.ShapeDtypeStruct((rows, width), F32)]
        + [jax.ShapeDtypeStruct(shape, F32) for shape in shapes],
        compiler_params=pltpu.CompilerParams(vmem_limit_bytes=VMEM_LIMIT),
        cost_estimate=cost(6e-6),
        name="finish",
    )(base, y_recv, ga_own, ga_recv, x, gres, gain, shards)


def swap(value, axis, size, bit):
    return lax.ppermute(value, axis, [(i, i ^ bit) for i in range(size)])


def after(value, *others):
    return lax.optimization_barrier((value,) + others)[0]


def paired(
    n_dp, tokens, doc_ids, gain_attn, w_q, w_kv, q_gain, k_gain, w_o, gain_ffn, w_gu, w_down, cotangent
):
    rows, width = tokens.shape
    head_dim = q_gain.shape[0]
    hidden = w_down.shape[0]
    seq = doc_ids.shape[1]
    t = lax.axis_index("tensor")
    over = functools.partial(swap, axis="tensor", size=2, bit=1)

    tokens_oth = over(tokens)

    segment = doc_ids[0]
    segment = jnp.where(t == 0, segment, jnp.roll(segment, rows))
    lanes = jnp.arange(PAIR, dtype=jnp.int32)[None, :]
    match = lanes == segment[:, None]
    marker = lanes == 8
    segk = (match | marker).astype(BF16)
    segq = (jnp.where(match, SAME, 0.0) - jnp.where(marker, SAME, 0.0)).astype(BF16)
    half_dim = head_dim // 2
    frequency = jnp.exp(-math.log(THETA) * 2.0 * jnp.arange(half_dim, dtype=F32) / head_dim)
    position = (jnp.arange(seq, dtype=jnp.int32) + t * rows) % seq
    angles = position.astype(F32)[:, None] * frequency[None, :]
    cos, sin = jnp.cos(angles), jnp.sin(angles)
    cosine = jnp.concatenate([cos] * 4, axis=1)
    sine = jnp.concatenate([-sin, sin] * 2, axis=1)
    gain1, gain2 = gain_attn.reshape(1, width), gain_ffn.reshape(1, width)
    qg = jnp.concatenate([q_gain, q_gain]).reshape(1, PAIR)
    kg = jnp.concatenate([k_gain, k_gain]).reshape(1, PAIR)
    w_kv = w_kv.reshape(width, -1)
    w_gu = w_gu.reshape(width, 2 * hidden)
    tables = dict(segq=segq, segk=segk, cos=cosine, sin=sine, gain1=gain1, gain2=gain2, qg=qg, kg=kg)

    attn_own, q_own, kd_own, vd_own, qraw_own, kraw_own = qkv(
        tokens, gain1, w_q, w_kv, qg, kg, cosine, sine, 0
    )
    values = dict(
        tok_own=tokens, tok_oth=tokens_oth, cot_own=cotangent, w_q=w_q, w_kv=w_kv, w_o=w_o, w_gu=w_gu, w_down=w_down,
        attn_own=attn_own, q_own=q_own, kd_own=kd_own, vd_own=vd_own, qraw_own=qraw_own, kraw_own=kraw_own,
    )
    values.update(front(values, tables))
    tables.update(gain_ffn=values["gain_ffn"])
    ga_own, ga_recv, shards, gains, y_recv = back(n_dp, values, tables)
    m = width // PAIR
    fold = lambda row: row[:head_dim] + row[head_dim:]
    output, grad_tokens, grad_q, grad_kv, grad_o, grad_gu, grad_down = finish(
        values["base"], y_recv, ga_own, ga_recv, tokens, values["gres"], gain1, shards
    )
    return (
        output,
        grad_tokens,
        gains[:m].reshape(width),
        grad_q,
        grad_kv,
        fold(gains[2 * m]),
        fold(gains[2 * m + 1]),
        grad_o.T,
        gains[m : 2 * m].reshape(width),
        grad_gu,
        grad_down.T,
    )


def normalize(values):
    inverse = lax.rsqrt(jnp.mean(values * values, axis=-1, keepdims=True) + EPS)
    return (values * inverse, inverse)


def norm_back(grad_normed, normed, inverse):
    return inverse * (grad_normed - normed * jnp.mean(grad_normed * normed, axis=-1, keepdims=True))


def rotate(values, cosine_table, sine_table):
    half_dim = values.shape[-1] // 2
    first_half = values[..., :half_dim]
    second_half = values[..., half_dim:]
    return jnp.concatenate(
        [
            first_half * cosine_table - second_half * sine_table,
            second_half * cosine_table + first_half * sine_table,
        ],
        -1,
    )


def shards(
    tokens, doc_ids, gain_attn, w_q, w_kv, q_gain, k_gain, w_o, gain_ffn, w_gu, w_down, cotangent
):
    f32 = jnp.float32
    bf16 = jnp.bfloat16
    rows_dev, model_width = tokens.shape
    head_dim = q_gain.shape[0]
    q_cols = w_q.shape[1]
    q_heads = q_cols // head_dim
    kv_cols = w_kv.shape[2]
    kv_heads = kv_cols // head_dim
    group_size = q_heads // kv_heads
    hidden = w_gu.shape[2]
    seq_len = doc_ids.shape[1]
    segment = doc_ids[0]
    block_rows = min(512, seq_len)
    blocks = seq_len // block_rows
    score_scale = head_dim ** (-0.5)
    w_kv_flat = w_kv.reshape(model_width, 2 * kv_cols)
    w_gu_flat = w_gu.reshape(model_width, 2 * hidden)
    half_dim = head_dim // 2
    frequency = jnp.exp(-math.log(THETA) * 2.0 * jnp.arange(half_dim, dtype=f32) / head_dim)
    angles = jnp.arange(seq_len, dtype=f32)[:, None] * frequency[None, :]
    cosine_table = jnp.cos(angles)[:, None, :]
    sine_table = jnp.sin(angles)[:, None, :]
    key_pos = jnp.arange(seq_len, dtype=jnp.int32)
    x_float = tokens.astype(f32)
    normed1, inverse1 = normalize(x_float)
    attn_in = (normed1 * gain_attn).astype(bf16)
    attn_all = lax.all_gather(attn_in, "tensor", axis=0, tiled=True)
    q_raw = jnp.dot(attn_all, w_q, preferred_element_type=f32).reshape(seq_len, q_heads, head_dim)
    kv_raw = jnp.dot(attn_all, w_kv_flat, preferred_element_type=f32).reshape(
        seq_len, 2, kv_heads, head_dim
    )
    q_normed, q_inverse = normalize(q_raw)
    k_normed, k_inverse = normalize(kv_raw[:, 0])
    queries = rotate(q_normed * q_gain, cosine_table, sine_table).astype(bf16)
    queries = queries.reshape(seq_len, kv_heads, group_size, head_dim)
    keys = rotate(k_normed * k_gain, cosine_table, sine_table).astype(bf16)
    values_low = kv_raw[:, 1].astype(bf16)

    def scores_of(first_row):
        q_block = lax.dynamic_slice_in_dim(queries, first_row, block_rows, 0)
        seg_block = lax.dynamic_slice_in_dim(segment, first_row, block_rows, 0)
        raw_scores = (
            jnp.einsum("qhgd,thd->hgqt", q_block, keys, preferred_element_type=f32) * score_scale
        )
        query_pos = first_row + jnp.arange(block_rows, dtype=jnp.int32)
        allowed = (key_pos[None, :] <= query_pos[:, None]) & (
            seg_block[:, None] == segment[None, :]
        )
        return (jnp.where(allowed, raw_scores, -1e30), q_block)

    def attend(first_row):
        masked, q_block = scores_of(first_row)
        row_max = jnp.max(masked, axis=-1, keepdims=True)
        exponent = jnp.exp(masked - row_max)
        denominator = jnp.sum(exponent, axis=-1, keepdims=True)
        probs = (exponent / denominator).astype(bf16)
        attended_block = jnp.einsum("hgqt,thd->qhgd", probs, values_low, preferred_element_type=f32)
        return (attended_block, (row_max + jnp.log(denominator))[..., 0])

    starts = jnp.arange(blocks, dtype=jnp.int32) * block_rows
    attended, log_sums = lax.map(attend, starts)
    attended_low = attended.reshape(seq_len, q_cols).astype(bf16)
    resid = x_float + lax.psum_scatter(
        jnp.dot(attended_low, w_o, preferred_element_type=f32),
        "tensor",
        scatter_dimension=0,
        tiled=True,
    )
    normed2, inverse2 = normalize(resid)
    ffn_in = (normed2 * gain_ffn).astype(bf16)
    ffn_all = lax.all_gather(ffn_in, "tensor", axis=0, tiled=True)
    gate_up = jnp.dot(ffn_all, w_gu_flat, preferred_element_type=f32)
    gate_part = gate_up[:, :hidden]
    up_part = gate_up[:, hidden:]
    sigmoid_gate = jax.nn.sigmoid(gate_part)
    silu_gate = gate_part * sigmoid_gate
    mixed = (silu_gate * up_part).astype(bf16)
    result = resid + lax.psum_scatter(
        jnp.dot(mixed, w_down, preferred_element_type=f32).astype(jnp.bfloat16),
        "tensor",
        scatter_dimension=0,
        tiled=True,
    ).astype(jnp.float32)
    output = result.astype(bf16)
    grad_all = lax.all_gather(cotangent, "tensor", axis=0, tiled=True)
    grad_down = jnp.einsum("sf,sd->fd", mixed, grad_all, preferred_element_type=f32)
    grad_mixed = jnp.einsum("sd,fd->sf", grad_all, w_down, preferred_element_type=f32)
    grad_gate = grad_mixed * up_part * sigmoid_gate * (1.0 + gate_part * (1.0 - sigmoid_gate))
    grad_up = grad_mixed * silu_gate
    grad_gu = jnp.concatenate([grad_gate, grad_up], 1).astype(bf16)
    grad_w_gu = jnp.einsum("sd,sf->df", ffn_all, grad_gu, preferred_element_type=f32).reshape(
        model_width, 2, hidden
    )
    grad_ffn_in = lax.psum_scatter(
        jnp.einsum("sf,df->sd", grad_gu, w_gu_flat, preferred_element_type=f32).astype(
            jnp.bfloat16
        ),
        "tensor",
        scatter_dimension=0,
        tiled=True,
    ).astype(jnp.float32)
    gain_ffn_part = jnp.sum(grad_ffn_in * normed2, axis=0)
    grad_resid = cotangent.astype(f32) + norm_back(grad_ffn_in * gain_ffn, normed2, inverse2)
    branch_all = lax.all_gather(grad_resid.astype(bf16), "tensor", axis=0, tiled=True)
    grad_w_o = jnp.einsum("sc,sd->cd", attended_low, branch_all, preferred_element_type=f32)
    grad_attended = jnp.einsum("sd,cd->sc", branch_all, w_o, preferred_element_type=f32).astype(
        bf16
    )
    grad_attended = grad_attended.reshape(seq_len, kv_heads, group_size, head_dim)

    def attend_back(carried, scanned):
        first_row, lse_block = scanned
        masked, q_block = scores_of(first_row)
        probs = jnp.exp(masked - lse_block[..., None])
        go_block = lax.dynamic_slice_in_dim(grad_attended, first_row, block_rows, 0)
        grad_probs = jnp.einsum("qhgd,thd->hgqt", go_block, values_low, preferred_element_type=f32)
        grad_scores = (
            probs * (grad_probs - jnp.sum(probs * grad_probs, axis=-1, keepdims=True))
        ).astype(bf16)
        keys_next = carried[0] + score_scale * jnp.einsum(
            "hgqt,qhgd->thd", grad_scores, q_block, preferred_element_type=f32
        )
        values_next = carried[1] + jnp.einsum(
            "hgqt,qhgd->thd", probs.astype(bf16), go_block, preferred_element_type=f32
        )
        grad_q_block = score_scale * jnp.einsum(
            "hgqt,thd->qhgd", grad_scores, keys, preferred_element_type=f32
        )
        return ((keys_next, values_next), grad_q_block)

    zero_kv = jnp.zeros((seq_len, kv_heads, head_dim), f32)
    (grad_keys, grad_values), grad_queries = lax.scan(
        attend_back, (zero_kv, zero_kv), (starts, log_sums)
    )
    grad_q_normed = rotate(
        grad_queries.reshape(seq_len, q_heads, head_dim), cosine_table, -sine_table
    )
    q_gain_part = jnp.sum(grad_q_normed * q_normed, axis=(0, 1))
    grad_q_raw = (
        norm_back(grad_q_normed * q_gain, q_normed, q_inverse).astype(bf16).reshape(seq_len, q_cols)
    )
    grad_k_normed = rotate(grad_keys, cosine_table, -sine_table)
    k_gain_part = jnp.sum(grad_k_normed * k_normed, axis=(0, 1))
    grad_k_raw = (
        norm_back(grad_k_normed * k_gain, k_normed, k_inverse)
        .astype(bf16)
        .reshape(seq_len, kv_cols)
    )
    grad_kv = jnp.concatenate([grad_k_raw, grad_values.astype(bf16).reshape(seq_len, kv_cols)], 1)
    grad_w_q = jnp.einsum("sd,sc->dc", attn_all, grad_q_raw, preferred_element_type=f32)
    grad_w_kv = jnp.einsum("sd,sc->dc", attn_all, grad_kv, preferred_element_type=f32).reshape(
        model_width, 2, kv_cols
    )
    grad_attn_in = lax.psum_scatter(
        (
            jnp.einsum("sc,dc->sd", grad_q_raw, w_q, preferred_element_type=f32)
            + jnp.einsum("sc,dc->sd", grad_kv, w_kv_flat, preferred_element_type=f32)
        ).astype(jnp.bfloat16),
        "tensor",
        scatter_dimension=0,
        tiled=True,
    ).astype(jnp.float32)
    gain_attn_part = jnp.sum(grad_attn_in * normed1, axis=0)
    grad_tokens = grad_resid + norm_back(grad_attn_in * gain_attn, normed1, inverse1)
    gain_sums = lax.psum(
        (gain_attn_part, gain_ffn_part, q_gain_part, k_gain_part), ("dp", "tensor")
    )
    shard_q, shard_kv, shard_o, shard_gu, shard_down = (
        lax.psum_scatter(
            grad_w_q.astype(jnp.bfloat16), "dp", scatter_dimension=0, tiled=True
        ).astype(jnp.float32),
        lax.psum_scatter(
            grad_w_kv.astype(jnp.bfloat16), "dp", scatter_dimension=0, tiled=True
        ).astype(jnp.float32),
        lax.psum_scatter(
            grad_w_o.astype(jnp.bfloat16), "dp", scatter_dimension=1, tiled=True
        ).astype(jnp.float32),
        lax.psum_scatter(
            grad_w_gu.astype(jnp.bfloat16), "dp", scatter_dimension=0, tiled=True
        ).astype(jnp.float32),
        lax.psum_scatter(
            grad_down.astype(jnp.bfloat16), "dp", scatter_dimension=1, tiled=True
        ).astype(jnp.float32),
    )
    return (
        output,
        grad_tokens,
        gain_sums[0],
        shard_q,
        shard_kv,
        gain_sums[2],
        gain_sums[3],
        shard_o,
        gain_sums[1],
        shard_gu,
        shard_down,
    )


def solution(mesh):
    in_specs = (
        P(("dp", "tensor"), None),
        P("dp", None),
        P(),
        P(None, "tensor"),
        P(None, None, "tensor"),
        P(),
        P(),
        P("tensor", None),
        P(),
        P(None, None, "tensor"),
        P("tensor", None),
        P(("dp", "tensor"), None),
    )
    out_specs = (
        P(("dp", "tensor"), None),
        P(("dp", "tensor"), None),
        P(),
        P("dp", "tensor"),
        P("dp", None, "tensor"),
        P(),
        P(),
        P("tensor", "dp"),
        P(),
        P("dp", None, "tensor"),
        P("tensor", "dp"),
    )
    paired_axes = mesh.shape["tensor"] == 2 and mesh.shape["dp"] == 16
    body = functools.partial(paired, mesh.shape["dp"]) if paired_axes else shards
    return jax.shard_map(body, mesh=mesh, in_specs=in_specs, out_specs=out_specs, check_vma=False)
```

```python
import functools
import math

import jax
import jax.numpy as jnp
from jax import lax
from jax.experimental import pallas as pl
from jax.experimental.pallas import tpu as pltpu
from jax.sharding import PartitionSpec as P

EPS = 1e-06
THETA = 1000000.0
LOG2E = 1.4426950408889634
LN2 = 0.6931471805599453
BLOCK = 256
PAIR = 128
SAME = 256.0
F32 = jnp.float32
BF16 = jnp.bfloat16
COST_RATE = 1.0e13
VMEM_LIMIT = 56 * 1024 * 1024
BACK_VMEM = 61 * 1024 * 1024


def dot_nn(a, b):
    return lax.dot_general(a, b, (((1,), (0,)), ((), ())), preferred_element_type=F32)


def dot_nt(a, b):
    return lax.dot_general(a, b, (((1,), (1,)), ((), ())), preferred_element_type=F32)


def cost(seconds):
    return pl.CostEstimate(flops=int(seconds * COST_RATE), bytes_accessed=0, transcendentals=0)


def lane_of(shape):
    return lax.broadcasted_iota(jnp.int32, shape, len(shape) - 1)


def head_mean(values):
    high = values.astype(BF16)
    low = (values - high.astype(F32)).astype(BF16)
    row = lax.broadcasted_iota(jnp.int32, (PAIR, PAIR), 0) // 64
    col = lax.broadcasted_iota(jnp.int32, (PAIR, PAIR), 1) // 64
    mean = jnp.where(row == col, 1.0 / 64.0, 0.0).astype(BF16)
    return dot_nn(high, mean) + dot_nn(low, mean)


def swap_halves(values):
    first = lane_of(values.shape) % 64 < 32
    return jnp.where(first, pltpu.roll(values, 96, 1), pltpu.roll(values, 32, 1))


def rope(values, cosine, sine):
    return values * cosine + swap_halves(values) * sine


def row_norm(x):
    return lax.rsqrt(jnp.mean(x * x, axis=-1, keepdims=True) + EPS)


def qkv_kernel(
    x_ref, gain_ref, wq_ref, wk_ref, wv_ref, qg_ref, kg_ref, cos_ref, sin_ref,
    attn_ref, q_ref, kd_ref, vd_ref, qraw_ref, kraw_ref,
):
    x = x_ref[...].astype(F32)
    attn = (x * row_norm(x) * gain_ref[...]).astype(BF16)
    attn_ref[...] = attn
    q = dot_nn(attn, wq_ref[...])
    k = dot_nn(attn, wk_ref[...])
    v = dot_nn(attn, wv_ref[...])
    qraw_ref[...] = q.astype(BF16)
    kraw_ref[...] = k.astype(BF16)
    cosine, sine = cos_ref[...], sin_ref[...]
    for g in range(q.shape[1] // PAIR):
        at = slice(g * PAIR, (g + 1) * PAIR)
        u = q[:, at]
        n = u * lax.rsqrt(head_mean(u * u) + EPS)
        q_ref[:, at] = (rope(n * qg_ref[...], cosine, sine) * (LOG2E / 8.0)).astype(BF16)
    low = lane_of((x.shape[0], PAIR)) < 64
    for p in range(k.shape[1] // PAIR):
        at = slice(p * PAIR, (p + 1) * PAIR)
        u = k[:, at]
        n = u * lax.rsqrt(head_mean(u * u) + EPS)
        roped = rope(n * kg_ref[...], cosine, sine)
        for src, dst in ((roped, kd_ref), (v[:, at], vd_ref)):
            turned = pltpu.roll(src, 64, 1)
            dst[:, 2 * p * PAIR : (2 * p + 1) * PAIR] = jnp.where(low, src, turned).astype(BF16)
            dst[:, (2 * p + 1) * PAIR : (2 * p + 2) * PAIR] = jnp.where(low, turned, src).astype(BF16)


def qkv(x, gain, w_q, w_kv, qg, kg, cosine, sine, half):
    rows, width = x.shape
    qc, kc = w_q.shape[1], w_kv.shape[1] // 2
    nb = rows // BLOCK
    whole = lambda shape, *at: pl.BlockSpec(shape, lambda i: at)
    row = lambda cols: pl.BlockSpec((BLOCK, cols), lambda i: (i, 0))
    table = pl.BlockSpec((BLOCK, PAIR), lambda i: (i + half * nb, 0))
    return pl.pallas_call(
        qkv_kernel,
        grid=(nb,),
        in_specs=[
            row(width), whole((1, width), 0, 0), whole((width, qc), 0, 0),
            whole((width, kc), 0, 0), whole((width, kc), 0, 1),
            whole((1, PAIR), 0, 0), whole((1, PAIR), 0, 0), table, table,
        ],
        out_specs=[row(width), row(qc), row(2 * kc), row(2 * kc), row(qc), row(kc)],
        out_shape=[
            jax.ShapeDtypeStruct((rows, c), BF16) for c in (width, qc, 2 * kc, 2 * kc, qc, kc)
        ],
        compiler_params=pltpu.CompilerParams(vmem_limit_bytes=VMEM_LIMIT),
        cost_estimate=cost(5e-6),
        name="qkv",
    )(x, gain, w_q, w_kv, w_kv, qg, kg, cosine, sine)


MESH = pl.DeviceIdType.MESH
CHUNK = 768
SPLIT = 512
DEPTH = 2


def dot_tn(a, b):
    return lax.dot_general(a, b, (((0,), (0,)), ((), ())), preferred_element_type=F32)


def pack_columns(dst, first, ref):
    rows, width = ref.shape
    low = lane_of((rows, PAIR)) < 64
    for k in range(width // (2 * PAIR)):
        a = ref[:, 2 * k * PAIR : (2 * k + 1) * PAIR].astype(F32)
        b = ref[:, (2 * k + 1) * PAIR : (2 * k + 2) * PAIR].astype(F32)
        lanes = slice(k * PAIR, (k + 1) * PAIR)
        dst[0, first : first + rows, lanes] = jnp.where(low, a, pltpu.roll(b, 64, 1)).astype(BF16)
        dst[1, first : first + rows, lanes] = jnp.where(low, pltpu.roll(a, 64, 1), b).astype(BF16)


BACK_INPUTS = (
    "h", "cot_pack", "ffn_pack", "attn_pack", "tok_own", "tok_oth", "y_send", "branch", "do_own", "do_send",
    "w_q", "w_kv", "q_own", "q_oth", "kd_own", "kd_oth", "vd_own", "vd_oth", "o_own", "o_oth", "linv_own", "linv_oth",
    "qraw_own", "qraw_oth", "kraw_own", "kraw_oth",
)
BACK_TABLES = ("segq", "segk", "cos", "sin", "gain_ffn", "qg", "kg")
BACK_OUTPUTS = ("ga_out", "ga_recv", "shards", "gains", "y_recv")


class Names:
    def __init__(self, names, refs):
        self.__dict__.update(zip(names, refs))


def back_kernel(n_dp, scratch_names, *refs):
    m = Names(BACK_INPUTS + BACK_TABLES + BACK_OUTPUTS + scratch_names, refs)
    rows, width = m.tok_own.shape
    hidden = m.h.shape[3]
    per_x = hidden // CHUNK
    n_wide = 3 * per_x
    n_chunks = n_wide + 2
    nb = 2 * rows // BLOCK
    t = lax.axis_index("tensor")
    d = lax.axis_index("dp")
    core = lax.rem(d, 2)
    x = lax.rem(d // 2, 2)
    zl = lax.rem(d // 4, 2)
    zh = d // 8
    over_t = {"tensor": 1 - t}
    over_core = {"dp": d + 1 - 2 * core}
    over_x = {"dp": d + 2 - 4 * x}
    over_zl = {"dp": d + 4 - 8 * zl}
    over_zh = {"dp": d + 8 - 16 * zh}
    partners = (over_t, over_core, over_x, over_zl, over_zh)
    low = lane_of((rows, PAIR)) < 64
    own_rows, oth_rows = pl.ds(0, rows), pl.ds(rows, rows)

    barrier = pltpu.get_barrier_semaphore()
    for p in partners:
        pl.semaphore_signal(barrier, inc=1, device_id=p, device_id_type=MESH)
    pl.semaphore_wait(barrier, len(partners))

    def tensor_copy(i, src, dst):
        return pltpu.make_async_remote_copy(
            src_ref=src, dst_ref=dst, send_sem=m.t_send.at[i], recv_sem=m.t_recv.at[i],
            device_id=over_t, device_id_type=MESH,
        )

    do_copy = tensor_copy(1, m.do_send, m.do_recv)
    branch_copy = tensor_copy(2, m.branch_v, m.branch_recv)
    y_copy = tensor_copy(3, m.y_send, m.y_recv)
    ga_copy = tensor_copy(4, m.branch_v, m.ga_recv)

    def rs_copy(stage, c, src, dst, device):
        return pltpu.make_async_remote_copy(
            src_ref=src, dst_ref=dst, send_sem=m.rs_send.at[stage, c], recv_sem=m.rs_recv.at[stage, c],
            device_id=device, device_id_type=MESH,
        )

    left, right = pl.ds(0, SPLIT), pl.ds(SPLIT, CHUNK - SPLIT)
    every = pl.ds(0, 2)
    block_rows = m.sums.shape[4]
    full_rows = pl.ds(0, block_rows)

    def core_copy(c):
        return rs_copy(0, c, m.core_send.at[lax.rem(c, 2)], m.sums.at[c], over_core)

    def first_copies(c):
        return (
            rs_copy(1, c, m.sums.at[c, every, every, 1 - x, full_rows, left], m.r1a.at[c], over_x),
            rs_copy(2, c, m.sums.at[c, every, 1 - zl, every, full_rows, right], m.r1b.at[c], over_zl),
        )

    def second_copies(c):
        return (
            rs_copy(3, c, m.sums.at[c, every, 1 - zl, x, full_rows, left], m.r2a.at[c], over_zl),
            rs_copy(4, c, m.sums.at[c, every, zl, 1 - x, full_rows, right], m.r2b.at[c], over_x),
        )

    def third_copy(c):
        return rs_copy(5, c, m.sums.at[c, 1 - zh, zl, x], m.r3.at[c], over_zh)

    def local(i, src, dst):
        return pltpu.make_async_copy(src, dst, m.l_sem.at[i])

    def both(i, src_own, src_oth, dst):
        return (local(i, src_own, dst.at[own_rows]), local(i + 1, src_oth, dst.at[oth_rows]))

    def start(copies):
        for copy in copies:
            copy.start()

    def wait(copies):
        for copy in copies:
            copy.wait()

    def add_core(c):
        core_copy(c).wait_recv()
        for a in range(2):
            for b in range(2):
                for e in range(2):
                    m.sums[c, a, b, e] = (
                        m.sums[c, a, b, e].astype(F32) + m.kept[lax.rem(c, 2), a, b, e].astype(F32)
                    ).astype(BF16)

    def total_copy(c):
        slot = lax.rem(c, 2)
        return pltpu.make_async_copy(m.totals.at[slot], m.shards.at[c], m.s_sem.at[slot])

    def tick(i):
        @pl.when(i < n_chunks)
        def _():
            a_copy, b_copy = first_copies(i)
            a_copy.wait_recv()
            b_copy.wait_recv()
            for a in range(2):
                for b in range(2):
                    m.sums[i, a, b, x, :, :SPLIT] = (
                        m.sums[i, a, b, x, :, :SPLIT].astype(F32) + m.r1a[i, a, b].astype(F32)
                    ).astype(BF16)
                    m.sums[i, a, zl, b, :, SPLIT:] = (
                        m.sums[i, a, zl, b, :, SPLIT:].astype(F32) + m.r1b[i, a, b].astype(F32)
                    ).astype(BF16)
            start(second_copies(i))

        @pl.when(i + DEPTH < n_chunks - 1)
        def _():
            start(first_copies(i + DEPTH))

        @pl.when((i >= 1) & (i < n_chunks + 1))
        def _():
            c = i - 1
            a_copy, b_copy = second_copies(c)
            a_copy.wait_recv()
            b_copy.wait_recv()
            for a in range(2):
                m.sums[c, a, zl, x, :, :SPLIT] = (
                    m.sums[c, a, zl, x, :, :SPLIT].astype(F32) + m.r2a[c, a].astype(F32)
                ).astype(BF16)
                m.sums[c, a, zl, x, :, SPLIT:] = (
                    m.sums[c, a, zl, x, :, SPLIT:].astype(F32) + m.r2b[c, a].astype(F32)
                ).astype(BF16)
            third_copy(c).start()

        @pl.when((i >= 2) & (i < n_chunks + 2))
        def _():
            c = i - 2
            third_copy(c).wait_recv()

            @pl.when(c >= 2)
            def _():
                total_copy(c - 2).wait()

            m.totals[lax.rem(c, 2)] = m.sums[c, zh, zl, x].astype(F32) + m.r3[c].astype(F32)
            total_copy(c).start()

    def put(ref, slot, lanes, value):
        for a in range(2):
            for b in range(2):
                for e in range(2):
                    k = ((a * 2 + b) * 2 + e) * block_rows
                    ref[slot, a, b, e, :, lanes] = value[k : k + block_rows].astype(BF16)

    do_copy.start()
    packs = [local(i, src, m.packed.at[i]) for i, src in enumerate((m.cot_pack, m.ffn_pack))]
    attn_load = local(0, m.attn_pack, m.packed.at[0])
    start(packs)
    loads = [
        local(2, m.branch, m.branch_v), local(3, m.do_own, m.do_v), local(7, m.w_q, m.wq_v), local(8, m.w_kv, m.wkv_v),
        *both(9, m.o_own, m.o_oth, m.o_v), *both(11, m.kraw_own, m.kraw_oth, m.kraw_v),
    ]

    def tiles(g):
        slot = lax.rem(g, 2)
        lanes = pl.ds(pl.multiple_of(g * PAIR, PAIR), PAIR)
        out = []
        for j, (own, oth, dst) in enumerate((
            (m.q_own, m.q_oth, m.q_v), (m.kd_own, m.kd_oth, m.kd_v), (m.vd_own, m.vd_oth, m.vd_v),
            (m.qraw_own, m.qraw_oth, m.qraw_v), (m.linv_own, m.linv_oth, m.linv_v),
        )):
            out.append(pltpu.make_async_copy(own.at[:, lanes], dst.at[slot, own_rows], m.g_sem.at[slot, 2 * j]))
            out.append(pltpu.make_async_copy(oth.at[:, lanes], dst.at[slot, oth_rows], m.g_sem.at[slot, 2 * j + 1]))
        return out

    def wide_phase(y_v):
        def fetch(c):
            slot = lax.rem(c, 2)
            cols = pl.ds(pl.multiple_of(lax.rem(c, per_x) * CHUNK, CHUNK), CHUNK)
            return [
                pltpu.make_async_copy(
                    m.h.at[j, c // per_x, :, cols], y_v.at[slot, at], m.h_sem.at[slot, j]
                )
                for j, at in enumerate((own_rows, oth_rows))
            ]

        start(fetch(0))
        start(loads)
        packs[0].wait()
        loads[0].wait()

        def chunk(c, carry):
            slot = lax.rem(c, 2)
            which = jnp.minimum(c // per_x, 1)
            wait(fetch(c))

            @pl.when(c == per_x)
            def _():
                packs[1].wait()
                attn_load.start()

            @pl.when(c + 1 < n_wide)
            def _():
                start(fetch(c + 1))

            @pl.when(c >= 2)
            def _():
                core_copy(c - 2).wait_send()

            put(m.core_send, slot, slice(None), dot_tn(m.packed[which, 1 - core], y_v[slot]))
            core_copy(c).start()
            put(m.kept, slot, slice(None), dot_tn(m.packed[which, core], y_v[slot]))

            @pl.when(c >= 1)
            def _():
                add_core(c - 1)

            @pl.when((c >= 1) & (c <= DEPTH))
            def _():
                start(first_copies(c - 1))

            @pl.when(c == n_wide - 4)
            def _():
                do_copy.wait_recv()
                branch_copy.start()

            @pl.when((c == n_wide - 4) | (c == n_wide - 2))
            def _():
                tick((c - n_wide + 4) // 2)

            return carry

        lax.fori_loop(0, n_wide, chunk, 0)
        add_core(n_wide - 1)
        tick(2)

    pl.run_scoped(wide_phase, pltpu.VMEM((2, 2 * rows, CHUNK), BF16))
    start(tiles(0))

    wait(loads[1:])
    attn_load.wait()
    y_copy.start()

    def narrow_chunk(p):
        c = n_wide + p
        slot = lax.rem(c, 2)
        core_copy(c - 2).wait_send()
        cols = pl.ds(pl.multiple_of(p * SPLIT, SPLIT), SPLIT)
        o_cols = pl.ds(pl.multiple_of(p * (CHUNK - SPLIT), CHUNK - SPLIT), CHUNK - SPLIT)
        for which, dst in ((1 - core, m.core_send), (core, m.kept)):
            put(dst, slot, slice(0, SPLIT), dot_tn(m.packed[0, which], m.g_v[:, cols]))
            put(dst, slot, slice(SPLIT, CHUNK), dot_tn(m.packed[1, which], m.o_v[:, o_cols]))
        core_copy(c).start()

    def place(block):
        return pl.ds(pl.multiple_of(lax.rem(block + t * (nb // 2), nb) * BLOCK, BLOCK), BLOCK)

    m.qgain[...] = jnp.zeros_like(m.qgain)
    m.kgain[...] = jnp.zeros_like(m.kgain)

    def attention_phase(qx, dox, kx0, kx1, vx0, vx1, kt, dqt, dk0, dk1, dv0, dv1, dks, dvs):
        all_low = lane_of((2 * rows, PAIR)) < 64
        one = jnp.ones((2 * rows, PAIR), F32)
        zero = jnp.zeros((2 * rows, PAIR), BF16)
        qx[:, PAIR:] = m.segq[...]
        kx0[:, PAIR:] = m.segk[...]
        kx1[:, PAIR:] = m.segk[...]
        vx0[:, PAIR:] = jnp.where(all_low, -one, 0.0).astype(BF16)
        vx1[:, PAIR:] = jnp.where(all_low, 0.0, -one).astype(BF16)

        def step(qb, kb, diagonal):
            qs, ks = place(qb), place(kb)
            q, do = qx[qs, :], dox[qs, :]
            for h, (kx, vx, dk, dv) in enumerate(((kx0, vx0, dk0, dv0), (kx1, vx1, dk1, dv1))):
                s = dot_nt(kx[ks, :], q)
                if diagonal:
                    r = lax.broadcasted_iota(jnp.int32, s.shape, 0)
                    s = jnp.where(r <= lane_of(s.shape), s, -1e30)
                e = jnp.exp2(s)
                ds = (e * dot_nt(vx[ks, :], do)).astype(BF16)
                dv[ks, :] += dot_nn(e.astype(BF16), do[:, :PAIR])
                dk[ks, :] += dot_nn(ds, q[:, :PAIR])
                dqt[h * 64 : (h + 1) * 64, qs] += dot_nn(kt[:, ks], ds)

        def group(g, carry):
            slot = lax.rem(g, 2)
            lanes = pl.ds(pl.multiple_of(g * PAIR, PAIR), PAIR)
            p = g // 2
            wait(tiles(g))

            @pl.when(g + 1 < 4)
            def _():
                start(tiles(g + 1))

            qx[:, :PAIR] = m.q_v[slot]
            k, v = m.kd_v[slot], m.vd_v[slot]
            kx0[:, :PAIR] = jnp.where(all_low, k, zero)
            kx1[:, :PAIR] = jnp.where(all_low, zero, k)
            vx0[:, :PAIR] = jnp.where(all_low, v, zero)
            vx1[:, :PAIR] = jnp.where(all_low, zero, v)
            kt[...] = jnp.transpose(k.astype(F32))[:64, :].astype(BF16)
            for at, do_ref in ((own_rows, m.do_v), (oth_rows, m.do_recv)):
                scaled = do_ref[:, lanes].astype(F32) * m.linv_v[slot, at, :]
                dox[at, :PAIR] = scaled.astype(BF16)
                dox[at, PAIR:] = (scaled * m.o_v[at, lanes].astype(F32)).astype(BF16)
            for ref in (dqt, dk0, dk1, dv0, dv1):
                ref[...] = jnp.zeros_like(ref)

            def q_body(qb, c):
                step(qb, qb, True)

                def k_body(kb, cc):
                    step(qb, kb, False)
                    return cc

                lax.fori_loop(jnp.maximum(qb - 2, 0), qb, k_body, 0)
                return c

            lax.fori_loop(0, nb, q_body, 0)

            @pl.when(g == 1)
            def _():
                tick(4)

            g_lanes = pl.ds(pl.multiple_of(p * SPLIT + slot * PAIR, PAIR), PAIR)
            for at in (own_rows, oth_rows):
                dq = jnp.transpose(dqt[:, at]) * 0.125
                normed_grad = rope(dq, m.cos[at, :], -m.sin[at, :])
                raw = m.qraw_v[slot, at, :].astype(F32)
                inverse = lax.rsqrt(head_mean(raw * raw) + EPS)
                u = raw * inverse
                m.qgain[...] += jnp.sum(normed_grad * u, axis=0, keepdims=True)
                w = normed_grad * m.qg[...]
                m.g_v[at, g_lanes] = (inverse * (w - u * head_mean(w * u))).astype(BF16)

            def gathered(a, b, at):
                joined = jnp.where(low, a[at, :], b[at, :])
                return joined + pltpu.roll(joined, 64, 1)

            @pl.when(slot == 0)
            def _():
                for at in (own_rows, oth_rows):
                    dks[at, :] = gathered(dk0, dk1, at)
                    dvs[at, :] = gathered(dv0, dv1, at)

            @pl.when(slot == 1)
            def _():
                k_lanes = pl.ds(pl.multiple_of(p * SPLIT + 2 * PAIR, PAIR), PAIR)
                v_lanes = pl.ds(pl.multiple_of(p * SPLIT + 3 * PAIR, PAIR), PAIR)
                raw_lanes = pl.ds(pl.multiple_of(p * PAIR, PAIR), PAIR)
                for at in (own_rows, oth_rows):
                    dk = jnp.where(low, dks[at, :], gathered(dk0, dk1, at)) * LN2
                    dv = jnp.where(low, dvs[at, :], gathered(dv0, dv1, at))
                    normed_grad = rope(dk, m.cos[at, :], -m.sin[at, :])
                    raw = m.kraw_v[at, raw_lanes].astype(F32)
                    inverse = lax.rsqrt(head_mean(raw * raw) + EPS)
                    u = raw * inverse
                    m.kgain[...] += jnp.sum(normed_grad * u, axis=0, keepdims=True)
                    w = normed_grad * m.kg[...]
                    m.g_v[at, k_lanes] = (inverse * (w - u * head_mean(w * u))).astype(BF16)
                    m.g_v[at, v_lanes] = dv.astype(BF16)

                @pl.when(p == 0)
                def _():
                    branch_copy.wait_recv()
                    pack_columns(m.packed.at[1], 0, m.branch_v)
                    pack_columns(m.packed.at[1], rows, m.branch_recv)

                narrow_chunk(p)

            @pl.when(g == 2)
            def _():
                add_core(n_wide)

            tick(3 + g + jnp.minimum(g, 1))
            return carry

        lax.fori_loop(0, 4, group, 0)

    pl.run_scoped(
        attention_phase,
        *[pltpu.VMEM((2 * rows, 2 * PAIR), BF16)] * 6,
        pltpu.VMEM((64, 2 * rows), BF16), pltpu.VMEM((PAIR, 2 * rows), F32),
        *[pltpu.VMEM((2 * rows, PAIR), F32)] * 6,
    )

    def attn_in_grad(at):
        out = None
        qc, kc = m.wq_v.shape[1], m.wkv_v.shape[1] // 2
        for p in range(2):
            for ref, base, begin, size in (
                (m.wq_v, 0, 0, 2 * PAIR), (m.wkv_v, 0, 2 * PAIR, PAIR), (m.wkv_v, kc, 3 * PAIR, PAIR)
            ):
                term = dot_nt(
                    m.g_v[at, p * SPLIT + begin : p * SPLIT + begin + size],
                    ref[:, base + p * size : base + (p + 1) * size],
                )
                out = term if out is None else out + term
        return out

    def end_phase(ga_own, tok_v):
        start(both(0, m.tok_own, m.tok_oth, tok_v))
        wait(both(0, m.tok_own, m.tok_oth, tok_v))

        def grad_and_gain(at):
            grad = attn_in_grad(at)
            tokens = tok_v[at, :].astype(F32)
            return grad, jnp.sum(grad * (tokens * row_norm(tokens)), axis=0, keepdims=True)

        branch_copy.wait_send()
        total = jnp.zeros((1, width), F32)
        for i in range(rows // BLOCK):
            grad, part = grad_and_gain(pl.ds(rows + i * BLOCK, BLOCK))
            m.branch_v[i * BLOCK : (i + 1) * BLOCK, :] = grad.astype(BF16)
            total += part
        ga_copy.start()
        add_core(n_chunks - 1)
        start(first_copies(n_chunks - 1))
        tick(n_chunks - 3)
        for i in range(rows // BLOCK):
            grad, part = grad_and_gain(pl.ds(i * BLOCK, BLOCK))
            ga_own[i * BLOCK : (i + 1) * BLOCK, :] = grad.astype(BF16)
            total += part
        ga_out_copy = local(3, ga_own, m.ga_out)
        ga_out_copy.start()
        for r in range(width // PAIR):
            m.mine[r : r + 1, :] = total[:, r * PAIR : (r + 1) * PAIR]
            at = slice(width // PAIR + r, width // PAIR + r + 1)
            m.mine[at, :] = m.gain_ffn[:, r * PAIR : (r + 1) * PAIR]
        last = 2 * width // PAIR
        m.mine[last : last + 1, :] = m.qgain[...]
        m.mine[last + 1 : last + 2, :] = m.kgain[...]
        m.mine[last + 2 :, :] = jnp.zeros((m.mine.shape[0] - last - 2, PAIR), F32)

        def gain_copy(i, device):
            return pltpu.make_async_remote_copy(
                src_ref=m.gain_out.at[i], dst_ref=m.gain_in.at[i], send_sem=m.gain_sem.at[0, i],
                recv_sem=m.gain_sem.at[1, i], device_id=device, device_id_type=MESH,
            )

        for i, device in enumerate(partners):
            m.gain_out[i] = m.mine[...]
            gain_copy(i, device).start()
            if i >= 1:
                tick(n_chunks - 3 + i)
            gain_copy(i, device).wait_recv()
            m.mine[...] += m.gain_in[i]
        m.gains[...] = m.mine[...]
        y_copy.wait_recv()
        ga_copy.wait_recv()
        for copy in (do_copy, y_copy, ga_copy):
            copy.wait_send()
        for i, device in enumerate(partners):
            gain_copy(i, device).wait_send()
        for c in (n_chunks - 2, n_chunks - 1):
            core_copy(c).wait_send()

        def drain(c, carry):
            for copy in (*first_copies(c), *second_copies(c), third_copy(c)):
                copy.wait_send()
            return carry

        lax.fori_loop(0, n_chunks, drain, 0)
        for c in (n_chunks - 2, n_chunks - 1):
            total_copy(c).wait()
        ga_out_copy.wait()

    pl.run_scoped(end_phase, pltpu.VMEM((rows, width), BF16), pltpu.VMEM((2 * rows, width), BF16))


def back(n_dp, values, tables):
    rows, width = values["tok_own"].shape
    hidden = values["h"].shape[3]
    seq = 2 * rows
    qc = values["w_q"].shape[1]
    n_chunks = 3 * hidden // CHUNK + 2
    block = width // n_dp
    vm = pltpu.VMEM
    dma = pltpu.SemaphoreType.DMA
    scratch = dict(
        packed=vm((2, 2, seq, width // 2), BF16),
        core_send=vm((2, 2, 2, 2, block, CHUNK), BF16), kept=vm((2, 2, 2, 2, block, CHUNK), BF16),
        sums=vm((n_chunks, 2, 2, 2, block, CHUNK), BF16),
        r1a=vm((n_chunks, 2, 2, block, SPLIT), BF16), r1b=vm((n_chunks, 2, 2, block, CHUNK - SPLIT), BF16),
        r2a=vm((n_chunks, 2, block, SPLIT), BF16), r2b=vm((n_chunks, 2, block, CHUNK - SPLIT), BF16),
        r3=vm((n_chunks, block, CHUNK), BF16), totals=vm((2, block, CHUNK), F32),
        wq_v=vm((width, qc), BF16), wkv_v=vm((width, qc), BF16),
        o_v=vm((seq, qc), BF16), kraw_v=vm((seq, qc // 2), BF16),
        q_v=vm((2, seq, PAIR), BF16), kd_v=vm((2, seq, PAIR), BF16), vd_v=vm((2, seq, PAIR), BF16),
        qraw_v=vm((2, seq, PAIR), BF16), linv_v=vm((2, seq, PAIR), F32),
        g_v=vm((seq, 2 * SPLIT), BF16), do_v=vm((rows, qc), BF16),
        do_recv=vm((rows, qc), BF16),
        branch_v=vm((rows, width), BF16), branch_recv=vm((rows, width), BF16),
        qgain=vm((1, PAIR), F32), kgain=vm((1, PAIR), F32), mine=vm((24, PAIR), F32),
        gain_out=vm((5, 24, PAIR), F32), gain_in=vm((5, 24, PAIR), F32),
        t_send=dma((5,)), t_recv=dma((5,)), rs_send=dma((6, n_chunks)), rs_recv=dma((6, n_chunks)),
        l_sem=dma((14,)), g_sem=dma((2, 10)), h_sem=dma((2, 2)), s_sem=dma((2,)), gain_sem=dma((2, 5)),
    )
    anywhere = pl.BlockSpec(memory_space=pl.ANY)
    vmem = pl.BlockSpec(memory_space=pltpu.VMEM)
    return pl.pallas_call(
        functools.partial(back_kernel, n_dp, tuple(scratch)),
        in_specs=[anywhere] * len(BACK_INPUTS) + [vmem] * len(BACK_TABLES),
        out_specs=[anywhere, anywhere, anywhere, vmem, anywhere],
        out_shape=[
            jax.ShapeDtypeStruct((rows, width), BF16),
            jax.ShapeDtypeStruct((rows, width), BF16),
            jax.ShapeDtypeStruct((n_chunks, block, CHUNK), F32), jax.ShapeDtypeStruct((24, PAIR), F32),
            jax.ShapeDtypeStruct((rows, width), BF16),
        ],
        scratch_shapes=list(scratch.values()),
        compiler_params=pltpu.CompilerParams(
            vmem_limit_bytes=BACK_VMEM, collective_id=0, has_side_effects=True
        ),
        cost_estimate=cost(100e-6),
        name="back",
    )(*[values[k] for k in BACK_INPUTS], *[tables[k] for k in BACK_TABLES])


FRONT_INPUTS = (
    "tok_own", "tok_oth", "cot_own", "w_q", "w_kv", "w_o", "w_gu", "w_down",
    "q_own", "kd_own", "vd_own", "attn_own",
)
FRONT_TABLES = ("segq", "segk", "cos", "sin", "gain1", "gain2", "qg", "kg")
FRONT_OUTPUTS = (
    "q_oth", "kd_oth", "vd_oth", "qraw_oth", "kraw_oth", "o_own", "o_oth", "linv_own", "linv_oth",
    "cot_pack", "ffn_pack", "attn_pack", "h", "base", "y_send", "branch", "do_own", "do_send",
    "gain_ffn",
)
PIECES = 4


def front_kernel(scratch_names, *refs):
    m = Names(FRONT_INPUTS + FRONT_TABLES + FRONT_OUTPUTS + scratch_names, refs)
    rows, width = m.tok_own.shape
    hidden = m.w_down.shape[0]
    qc = m.w_q.shape[1]
    kc = m.w_kv.shape[1] // 2
    nb = 2 * rows // BLOCK
    t = lax.axis_index("tensor")
    d = lax.axis_index("dp")
    core = lax.rem(d, 2)
    over_t = {"tensor": 1 - t}
    over_core = {"dp": d + 1 - 2 * core}

    barrier = pltpu.get_barrier_semaphore()
    for p in (over_t, over_core):
        pl.semaphore_signal(barrier, inc=1, device_id=p, device_id_type=MESH)
    pl.semaphore_wait(barrier, 2)

    def remote(i, src, dst, device):
        return pltpu.make_async_remote_copy(
            src_ref=src, dst_ref=dst, send_sem=m.r_send.at[i], recv_sem=m.r_recv.at[i],
            device_id=device, device_id_type=MESH,
        )

    pieces = [pl.ds(i * (rows // PIECES), rows // PIECES) for i in range(PIECES)]
    halves = [pl.ds(i * BLOCK, BLOCK) for i in range(rows // BLOCK)]
    cot_copies = [remote(i, m.cot_own.at[at], m.cot_v.at[1, at], over_t) for i, at in enumerate(pieces)]
    half_o = qc // 2
    mine_o = pl.ds(pl.multiple_of(core * half_o, half_o), half_o)
    wo_copy = remote(4, m.w_o.at[mine_o], m.wot_v.at[mine_o], over_t)
    wo_core = remote(5, m.wot_v.at[mine_o], m.wot_v.at[mine_o], over_core)
    o_copy = remote(6, m.o_v.at[1], m.theirs, over_t)
    ffn_copies = [remote(7 + i, m.ffn_v.at[0, at], m.ffn_v.at[1, at], over_t) for i, at in enumerate(halves)]
    gf_copies = [remote(9 + i, m.gf_send.at[at], m.gf_in.at[at], over_t) for i, at in enumerate(halves)]

    def local(i, src, dst):
        return pltpu.make_async_copy(src, dst, m.l_sem.at[i])

    loads = [
        local(i, src, dst)
        for i, (src, dst) in enumerate((
            (m.tok_oth, m.tok_v.at[1]), (m.w_q, m.wq_v), (m.w_kv, m.wkv_v), (m.q_own, m.q_v.at[0]),
            (m.kd_own, m.kd_v.at[0]), (m.vd_own, m.vd_v.at[0]), (m.w_o, m.wom_v), (m.tok_own, m.tok_v.at[0]),
            (m.attn_own, m.attn_v.at[0]), (m.cot_own, m.cot_v.at[0]), (m.w_gu, m.wgu_v), (m.w_down, m.wd_v),
        ))
    ]
    out_sem = [0]
    stores = []

    def store(src, dst):
        copy = pltpu.make_async_copy(src, dst, m.o_sem.at[out_sem[0]])
        out_sem[0] += 1
        copy.start()
        stores.append(copy)

    wo_copy.start()
    for copy in cot_copies[:3]:
        copy.start()
    for copy in loads:
        copy.start()
    for copy in loads[:6]:
        copy.wait()

    for at in halves:
        table = pl.ds(rows + at.start, BLOCK)
        qkv_kernel(
            m.tok_v.at[1, at], m.gain1, m.wq_v, m.wkv_v.at[:, pl.ds(0, kc)], m.wkv_v.at[:, pl.ds(kc, kc)],
            m.qg, m.kg, m.cos.at[table], m.sin.at[table],
            m.attn_v.at[1, at], m.q_v.at[1, at], m.kd_v.at[1, at], m.vd_v.at[1, at], m.qraw_v.at[at], m.kraw_v.at[at],
        )
    for src, dst in (
        (m.q_v.at[1], m.q_oth), (m.kd_v.at[1], m.kd_oth), (m.vd_v.at[1], m.vd_oth),
        (m.qraw_v, m.qraw_oth), (m.kraw_v, m.kraw_oth),
    ):
        store(src, dst)
    wo_copy.wait_recv()
    wo_core.start()

    def place(block):
        return pl.ds(pl.multiple_of(lax.rem(block + t * (nb // 2), nb) * BLOCK, BLOCK), BLOCK)

    def attention_phase(kx0, kx1, vx0, vx1, acc):
        both = lane_of((2 * rows, PAIR)) < 64
        one = jnp.ones((2 * rows, PAIR), F32)
        low = lane_of((rows, PAIR)) < 64
        zero = jnp.zeros((rows, PAIR), BF16)
        kx0[:, PAIR:] = m.segk[...]
        kx1[:, PAIR:] = m.segk[...]
        vx0[:, PAIR:] = jnp.where(both, one, 0.0).astype(BF16)
        vx1[:, PAIR:] = jnp.where(both, 0.0, one).astype(BF16)

        def half(which, carry):
            part = 1 - which
            first = lax.rem(part + t, 2) * (nb // 2)

            def group(g, carry):
                lanes = pl.ds(pl.multiple_of(g * PAIR, PAIR), PAIR)
                for i in range(2):
                    at = pl.ds(i * rows, rows)
                    k, v = m.kd_v[i, :, lanes], m.vd_v[i, :, lanes]
                    kx0[at, :PAIR] = jnp.where(low, k, zero)
                    kx1[at, :PAIR] = jnp.where(low, zero, k)
                    vx0[at, :PAIR] = jnp.where(low, v, zero)
                    vx1[at, :PAIR] = jnp.where(low, zero, v)

                def q_block(i, c):
                    at = pl.ds(pl.multiple_of(i * BLOCK, BLOCK), BLOCK)
                    seg_at = pl.ds(pl.multiple_of(part * rows + i * BLOCK, BLOCK), BLOCK)
                    q = jnp.concatenate([m.q_v[part, at, lanes], m.segq[seg_at, :]], axis=1)
                    block = first + i

                    def step(kb, diagonal):
                        here = place(kb)
                        total = None
                        for kx, vx in ((kx0, vx0), (kx1, vx1)):
                            s = dot_nt(q, kx[here, :])
                            if diagonal:
                                r = lax.broadcasted_iota(jnp.int32, s.shape, 0)
                                s = jnp.where(lane_of(s.shape) <= r, s, -1e30)
                            term = dot_nn(jnp.exp2(s).astype(BF16), vx[here, :])
                            total = term if total is None else total + term
                        return total

                    acc[...] = step(block, True)

                    def body(kb, c):
                        acc[...] += step(kb, False)
                        return c

                    lax.fori_loop(jnp.maximum(block - 2, 0), block, body, 0)
                    inverse = 1.0 / acc[:, PAIR:]
                    m.o_v[part, at, lanes] = (acc[:, :PAIR] * inverse).astype(BF16)
                    m.linv_v[part, at, lanes] = inverse
                    return c

                lax.fori_loop(0, rows // BLOCK, q_block, 0)
                return carry

            lax.fori_loop(0, qc // PAIR, group, 0)

            @pl.when(which == 0)
            def _():
                o_copy.start()
                cot_copies[3].start()

            return carry

        lax.fori_loop(0, 2, half, 0)

    pl.run_scoped(
        attention_phase, *[pltpu.VMEM((2 * rows, 2 * PAIR), BF16)] * 4, pltpu.VMEM((BLOCK, 2 * PAIR), F32)
    )
    for src, dst in (
        (m.o_v.at[0], m.o_own), (m.o_v.at[1], m.o_oth), (m.linv_v.at[0], m.linv_own), (m.linv_v.at[1], m.linv_oth)
    ):
        store(src, dst)

    for copy in loads[6:9]:
        copy.wait()
    pack_columns(m.ffn_pack_v, 0, m.attn_v.at[0])
    pack_columns(m.ffn_pack_v, rows, m.attn_v.at[1])
    attn_store = local(12, m.ffn_pack_v, m.attn_pack)
    attn_store.start()
    wo_core.wait_recv()
    o_copy.wait_recv()
    for i, at in enumerate(halves):
        resid = (
            m.tok_v[0, at, :].astype(F32) + dot_nn(m.o_v[0, at, :], m.wom_v[...]) + dot_nn(m.theirs[at, :], m.wot_v[...])
        )
        m.resid_v[at, :] = resid
        m.ffn_v[0, at, :] = (resid * row_norm(resid) * m.gain2[...]).astype(BF16)
        ffn_copies[i].start()

    for copy in loads[9:]:
        copy.wait()
    n_tiles = hidden // CHUNK

    def h_copy(slot, part, at, f):
        cols = pl.ds(pl.multiple_of(f * CHUNK, CHUNK), CHUNK)
        return pltpu.make_async_copy(m.h_v.at[slot], m.h.at[part, :, at, cols], m.h_sem.at[slot])

    def piece(n, carry):
        part = lax.rem((n + 1) // 2, 2)
        at = pl.ds(pl.multiple_of((n // 2) * BLOCK, BLOCK), BLOCK)
        to = pl.ds(pl.multiple_of((2 * part + (1 - part) * (n // 3)) * BLOCK, BLOCK), BLOCK)
        for i in range(2):
            @pl.when(n == 1 + i)
            def _():
                ffn_copies[i].wait_recv()
                for copy in cot_copies[2 * i : 2 * i + 2]:
                    copy.wait_recv()

        def tile(f, c):
            slot = lax.rem(n * n_tiles + f, 2)
            cols = pl.ds(pl.multiple_of(f * CHUNK, CHUNK), CHUNK)
            up_cols = pl.ds(pl.multiple_of(hidden + f * CHUNK, CHUNK), CHUNK)
            x = m.ffn_v[part, at, :]
            gate = dot_nn(x, m.wgu_v[:, cols])
            up = dot_nn(x, m.wgu_v[:, up_cols])
            grad = dot_nt(m.cot_v[part, at, :], m.wd_v[cols, :])

            @pl.when(n * n_tiles + f >= 2)
            def _():
                h_copy(slot, part, at, f).wait()

            sig = 0.5 * jnp.tanh(0.5 * gate) + 0.5
            silu = gate * sig
            mixed = (silu * up).astype(BF16)
            gg = (grad * up * (sig + silu * (1.0 - sig))).astype(BF16)
            gu = (grad * silu).astype(BF16)
            for i, value in enumerate((mixed, gg, gu)):
                m.h_v[slot, i] = value
            h_copy(slot, part, at, f).start()
            y = dot_nn(mixed, m.wd_v[cols, :])
            gf = dot_nt(gg, m.wgu_v[:, cols]) + dot_nt(gu, m.wgu_v[:, up_cols])

            @pl.when(f == 0)
            def _():
                m.y_v[to, :] = y
                m.gf_v[to, :] = gf

            @pl.when(f > 0)
            def _():
                m.y_v[to, :] += y
                m.gf_v[to, :] += gf

            return c

        lax.fori_loop(0, n_tiles, tile, 0)

        @pl.when(n == 0)
        def _():
            pack_columns(m.cot_pack_v, 0, m.cot_v.at[0])
            attn_store.wait()
            pack_columns(m.ffn_pack_v, 0, m.ffn_v.at[0])

        for i in range(2):
            @pl.when(n == 1 + i)
            def _():
                m.gf_send[halves[i], :] = m.gf_v[2 * BLOCK :, :].astype(BF16)
                gf_copies[i].start()
                m.attn_v[1, halves[i], :] = m.y_v[2 * BLOCK :, :].astype(BF16)

        return carry

    lax.fori_loop(0, 4, piece, 0)
    store(m.attn_v.at[1], m.y_send)
    pack_columns(m.cot_pack_v, rows, m.cot_v.at[1])
    pack_columns(m.ffn_pack_v, rows, m.ffn_v.at[1])
    store(m.cot_pack_v, m.cot_pack)
    store(m.ffn_pack_v, m.ffn_pack)

    total = jnp.zeros((1, width), F32)
    for i, at in enumerate(halves):
        gf_copies[i].wait_recv()
        grad = m.gf_v[at, :] + m.gf_in[at, :].astype(F32)
        resid = m.resid_v[at, :]
        inverse = row_norm(resid)
        normed = resid * inverse
        total += jnp.sum(grad * normed, axis=0, keepdims=True)
        w = grad * m.gain2[...]
        gres = m.cot_v[0, at, :].astype(F32) + inverse * (
            w - normed * jnp.mean(w * normed, axis=-1, keepdims=True)
        )
        branch = gres.astype(BF16)
        m.attn_v[0, at, :] = branch
        m.do_v[0, at, :] = dot_nt(branch, m.wom_v[...]).astype(BF16)
        m.do_v[1, at, :] = dot_nt(branch, m.wot_v[...]).astype(BF16)
        m.tok_v[0, at, :] = (m.y_v[at, :] + resid).astype(BF16)
    for src, dst in (
        (m.do_v.at[1], m.do_send), (m.do_v.at[0], m.do_own), (m.attn_v.at[0], m.branch),
        (m.tok_v.at[0], m.base),
    ):
        store(src, dst)
    m.gain_ffn[...] = total
    for copy in (*cot_copies, wo_copy, wo_core, o_copy, *ffn_copies, *gf_copies):
        copy.wait_send()
    for slot in range(2):
        pltpu.make_async_copy(m.h_v.at[slot], m.h.at[0, :, halves[1], pl.ds(0, CHUNK)], m.h_sem.at[slot]).wait()
    for copy in stores:
        copy.wait()


def front(values, tables):
    rows, width = values["tok_own"].shape
    hidden = values["w_down"].shape[0]
    qc = values["w_q"].shape[1]
    seq = 2 * rows
    vm = pltpu.VMEM
    dma = pltpu.SemaphoreType.DMA
    scratch = dict(
        tok_v=vm((2, rows, width), BF16), cot_v=vm((2, rows, width), BF16),
        wq_v=vm((width, qc), BF16), wkv_v=vm((width, qc), BF16), wom_v=vm((qc, width), BF16), wot_v=vm((qc, width), BF16),
        wgu_v=vm((width, 2 * hidden), BF16), wd_v=vm((hidden, width), BF16),
        q_v=vm((2, rows, qc), BF16), kd_v=vm((2, rows, qc), BF16), vd_v=vm((2, rows, qc), BF16),
        attn_v=vm((2, rows, width), BF16), qraw_v=vm((rows, qc), BF16), kraw_v=vm((rows, qc // 2), BF16),
        o_v=vm((2, rows, qc), BF16), linv_v=vm((2, rows, qc), F32), theirs=vm((rows, qc), BF16),
        resid_v=vm((rows, width), F32), ffn_v=vm((2, rows, width), BF16),
        h_v=vm((2, 3, BLOCK, CHUNK), BF16), y_v=vm((3 * BLOCK, width), F32), gf_v=vm((3 * BLOCK, width), F32),
        gf_send=vm((rows, width), BF16), gf_in=vm((rows, width), BF16),
        cot_pack_v=vm((2, seq, width // 2), BF16),
        ffn_pack_v=vm((2, seq, width // 2), BF16), do_v=vm((2, rows, qc), BF16),
        r_send=dma((11,)), r_recv=dma((11,)), l_sem=dma((13,)), o_sem=dma((20,)), h_sem=dma((2,)),
    )
    anywhere = pl.BlockSpec(memory_space=pl.ANY)
    vmem = pl.BlockSpec(memory_space=pltpu.VMEM)
    low, full = (lambda *shape: jax.ShapeDtypeStruct(shape, BF16)), (lambda *shape: jax.ShapeDtypeStruct(shape, F32))
    shapes = dict(
        q_oth=low(rows, qc), kd_oth=low(rows, qc), vd_oth=low(rows, qc),
        qraw_oth=low(rows, qc), kraw_oth=low(rows, qc // 2), o_own=low(rows, qc), o_oth=low(rows, qc),
        linv_own=full(rows, qc), linv_oth=full(rows, qc),
        cot_pack=low(2, seq, width // 2), ffn_pack=low(2, seq, width // 2), attn_pack=low(2, seq, width // 2),
        h=low(2, 3, rows, hidden), base=low(rows, width), y_send=low(rows, width),
        branch=low(rows, width), do_own=low(rows, qc), do_send=low(rows, qc),
        gain_ffn=full(1, width),
    )
    outs = pl.pallas_call(
        functools.partial(front_kernel, tuple(scratch)),
        in_specs=[anywhere] * len(FRONT_INPUTS) + [vmem] * len(FRONT_TABLES),
        out_specs=[anywhere] * (len(FRONT_OUTPUTS) - 1) + [vmem],
        out_shape=[shapes[k] for k in FRONT_OUTPUTS],
        scratch_shapes=list(scratch.values()),
        compiler_params=pltpu.CompilerParams(
            vmem_limit_bytes=BACK_VMEM, collective_id=1, has_side_effects=True
        ),
        cost_estimate=cost(100e-6),
        name="front",
    )(*[values[k] for k in FRONT_INPUTS], *[tables[k] for k in FRONT_TABLES])
    return dict(zip(FRONT_OUTPUTS, outs))


def finish_kernel(
    base_ref, yr_ref, ga_ref, gr_ref, x_ref, gres_ref, gain_ref, shards_ref, gains_ref,
    out_ref, gt_ref, q_ref, kv_ref, o_ref, g1_ref, g2_ref, gq_ref, gk_ref, gu_ref, down_ref,
):
    out_ref[...] = (base_ref[...].astype(F32) + yr_ref[...].astype(F32)).astype(BF16)
    x = x_ref[...].astype(F32)
    inverse = row_norm(x)
    normed = x * inverse
    w = (ga_ref[...].astype(F32) + gr_ref[...].astype(F32)) * gain_ref[...]
    gt_ref[...] = gres_ref[...].astype(F32) + inverse * (w - normed * jnp.mean(w * normed, axis=-1, keepdims=True))
    n_chunks = shards_ref.shape[0]
    per_x = (n_chunks - 2) // 3
    two = 2 * PAIR
    step = pl.program_id(0)

    @pl.when(step < per_x)
    def _():
        down_ref[...] = shards_ref[step]
        gu_ref[:, 0, :] = shards_ref[per_x + step]
        gu_ref[:, 1, :] = shards_ref[2 * per_x + step]

    @pl.when(step == per_x)
    def _():
        n = g1_ref.shape[0]
        g1_ref[...] = gains_ref[:n, :]
        g2_ref[...] = gains_ref[n : 2 * n, :]
        for i, ref in enumerate((gq_ref, gk_ref)):
            row = gains_ref[2 * n + i : 2 * n + i + 1, :]
            ref[...] = row[:, :64] + row[:, 64:]
        for p in range(2):
            shard = shards_ref[3 * per_x + p]
            q_ref[:, p * two : (p + 1) * two] = shard[:, :two]
            kv_ref[:, 0, p * PAIR : (p + 1) * PAIR] = shard[:, two : two + PAIR]
            kv_ref[:, 1, p * PAIR : (p + 1) * PAIR] = shard[:, two + PAIR : 2 * two]
            o_ref[:, p * two : (p + 1) * two] = shard[:, 2 * two :]


def finish(base, y_recv, ga_own, ga_recv, x, gres, gain, shards, gains):
    rows, width = x.shape
    n_chunks, block, _ = shards.shape
    hidden = (n_chunks - 2) // 3 * CHUNK
    per_x = hidden // CHUNK
    row = pl.BlockSpec((rows // (per_x + 1), width), lambda i: (i, 0))
    fixed = lambda shape: pl.BlockSpec(shape, lambda i: (0,) * len(shape))
    m = width // PAIR
    shapes = [(block, SPLIT), (block, 2, SPLIT // 2), (block, SPLIT), (m, PAIR), (m, PAIR), (1, 64), (1, 64)]
    shapes += [(block, 2, hidden), (block, hidden)]
    piece = lambda i: jnp.minimum(i, per_x - 1)
    return pl.pallas_call(
        finish_kernel,
        grid=(per_x + 1,),
        in_specs=[row] * 6 + [fixed((1, width)), fixed(shards.shape), fixed(gains.shape)],
        out_specs=[row, row]
        + [fixed(shape) for shape in shapes[:7]]
        + [
            pl.BlockSpec((block, 2, CHUNK), lambda i: (0, 0, piece(i))),
            pl.BlockSpec((block, CHUNK), lambda i: (0, piece(i))),
        ],
        out_shape=[jax.ShapeDtypeStruct((rows, width), BF16), jax.ShapeDtypeStruct((rows, width), F32)]
        + [jax.ShapeDtypeStruct(shape, F32) for shape in shapes],
        compiler_params=pltpu.CompilerParams(vmem_limit_bytes=VMEM_LIMIT),
        cost_estimate=cost(6e-6),
        name="finish",
    )(base, y_recv, ga_own, ga_recv, x, gres, gain, shards, gains)


def swap(value, axis, size, bit):
    return lax.ppermute(value, axis, [(i, i ^ bit) for i in range(size)])


def after(value, *others):
    return lax.optimization_barrier((value,) + others)[0]


def paired(
    n_dp, tokens, doc_ids, gain_attn, w_q, w_kv, q_gain, k_gain, w_o, gain_ffn, w_gu, w_down, cotangent
):
    rows, width = tokens.shape
    head_dim = q_gain.shape[0]
    hidden = w_down.shape[0]
    seq = doc_ids.shape[1]
    t = lax.axis_index("tensor")
    over = functools.partial(swap, axis="tensor", size=2, bit=1)

    tokens_oth = over(tokens)

    segment = doc_ids[0]
    segment = jnp.where(t == 0, segment, jnp.roll(segment, rows))
    lanes = jnp.arange(PAIR, dtype=jnp.int32)[None, :]
    match = lanes == segment[:, None]
    marker = lanes == 8
    segk = (match | marker).astype(BF16)
    segq = (jnp.where(match, SAME, 0.0) - jnp.where(marker, SAME, 0.0)).astype(BF16)
    half_dim = head_dim // 2
    frequency = jnp.exp(-math.log(THETA) * 2.0 * jnp.arange(half_dim, dtype=F32) / head_dim)
    position = (jnp.arange(seq, dtype=jnp.int32) + t * rows) % seq
    angles = position.astype(F32)[:, None] * frequency[None, :]
    cos, sin = jnp.cos(angles), jnp.sin(angles)
    cosine = jnp.concatenate([cos] * 4, axis=1)
    sine = jnp.concatenate([-sin, sin] * 2, axis=1)
    gain1, gain2 = gain_attn.reshape(1, width), gain_ffn.reshape(1, width)
    qg = jnp.concatenate([q_gain, q_gain]).reshape(1, PAIR)
    kg = jnp.concatenate([k_gain, k_gain]).reshape(1, PAIR)
    w_kv = w_kv.reshape(width, -1)
    w_gu = w_gu.reshape(width, 2 * hidden)
    tables = dict(segq=segq, segk=segk, cos=cosine, sin=sine, gain1=gain1, gain2=gain2, qg=qg, kg=kg)

    attn_own, q_own, kd_own, vd_own, qraw_own, kraw_own = qkv(
        tokens, gain1, w_q, w_kv, qg, kg, cosine, sine, 0
    )
    values = dict(
        tok_own=tokens, tok_oth=tokens_oth, cot_own=cotangent, w_q=w_q, w_kv=w_kv, w_o=w_o, w_gu=w_gu, w_down=w_down,
        attn_own=attn_own, q_own=q_own, kd_own=kd_own, vd_own=vd_own, qraw_own=qraw_own, kraw_own=kraw_own,
    )
    values.update(front(values, tables))
    tables.update(gain_ffn=values["gain_ffn"])
    ga_own, ga_recv, shards, gains, y_recv = back(n_dp, values, tables)
    output, grad_tokens, grad_q, grad_kv, grad_o, sum_1, sum_2, sum_q, sum_k, grad_gu, grad_down = finish(
        values["base"], y_recv, ga_own, ga_recv, tokens, values["branch"], gain1, shards, gains
    )
    return (
        output,
        grad_tokens,
        sum_1.reshape(width),
        grad_q,
        grad_kv,
        sum_q.reshape(head_dim),
        sum_k.reshape(head_dim),
        grad_o.T,
        sum_2.reshape(width),
        grad_gu,
        grad_down.T,
    )


def normalize(values):
    inverse = lax.rsqrt(jnp.mean(values * values, axis=-1, keepdims=True) + EPS)
    return (values * inverse, inverse)


def norm_back(grad_normed, normed, inverse):
    return inverse * (grad_normed - normed * jnp.mean(grad_normed * normed, axis=-1, keepdims=True))


def rotate(values, cosine_table, sine_table):
    half_dim = values.shape[-1] // 2
    first_half = values[..., :half_dim]
    second_half = values[..., half_dim:]
    return jnp.concatenate(
        [
            first_half * cosine_table - second_half * sine_table,
            second_half * cosine_table + first_half * sine_table,
        ],
        -1,
    )


def shards(
    tokens, doc_ids, gain_attn, w_q, w_kv, q_gain, k_gain, w_o, gain_ffn, w_gu, w_down, cotangent
):
    f32 = jnp.float32
    bf16 = jnp.bfloat16
    rows_dev, model_width = tokens.shape
    head_dim = q_gain.shape[0]
    q_cols = w_q.shape[1]
    q_heads = q_cols // head_dim
    kv_cols = w_kv.shape[2]
    kv_heads = kv_cols // head_dim
    group_size = q_heads // kv_heads
    hidden = w_gu.shape[2]
    seq_len = doc_ids.shape[1]
    segment = doc_ids[0]
    block_rows = min(512, seq_len)
    blocks = seq_len // block_rows
    score_scale = head_dim ** (-0.5)
    w_kv_flat = w_kv.reshape(model_width, 2 * kv_cols)
    w_gu_flat = w_gu.reshape(model_width, 2 * hidden)
    half_dim = head_dim // 2
    frequency = jnp.exp(-math.log(THETA) * 2.0 * jnp.arange(half_dim, dtype=f32) / head_dim)
    angles = jnp.arange(seq_len, dtype=f32)[:, None] * frequency[None, :]
    cosine_table = jnp.cos(angles)[:, None, :]
    sine_table = jnp.sin(angles)[:, None, :]
    key_pos = jnp.arange(seq_len, dtype=jnp.int32)
    x_float = tokens.astype(f32)
    normed1, inverse1 = normalize(x_float)
    attn_in = (normed1 * gain_attn).astype(bf16)
    attn_all = lax.all_gather(attn_in, "tensor", axis=0, tiled=True)
    q_raw = jnp.dot(attn_all, w_q, preferred_element_type=f32).reshape(seq_len, q_heads, head_dim)
    kv_raw = jnp.dot(attn_all, w_kv_flat, preferred_element_type=f32).reshape(
        seq_len, 2, kv_heads, head_dim
    )
    q_normed, q_inverse = normalize(q_raw)
    k_normed, k_inverse = normalize(kv_raw[:, 0])
    queries = rotate(q_normed * q_gain, cosine_table, sine_table).astype(bf16)
    queries = queries.reshape(seq_len, kv_heads, group_size, head_dim)
    keys = rotate(k_normed * k_gain, cosine_table, sine_table).astype(bf16)
    values_low = kv_raw[:, 1].astype(bf16)

    def scores_of(first_row):
        q_block = lax.dynamic_slice_in_dim(queries, first_row, block_rows, 0)
        seg_block = lax.dynamic_slice_in_dim(segment, first_row, block_rows, 0)
        raw_scores = (
            jnp.einsum("qhgd,thd->hgqt", q_block, keys, preferred_element_type=f32) * score_scale
        )
        query_pos = first_row + jnp.arange(block_rows, dtype=jnp.int32)
        allowed = (key_pos[None, :] <= query_pos[:, None]) & (
            seg_block[:, None] == segment[None, :]
        )
        return (jnp.where(allowed, raw_scores, -1e30), q_block)

    def attend(first_row):
        masked, q_block = scores_of(first_row)
        row_max = jnp.max(masked, axis=-1, keepdims=True)
        exponent = jnp.exp(masked - row_max)
        denominator = jnp.sum(exponent, axis=-1, keepdims=True)
        probs = (exponent / denominator).astype(bf16)
        attended_block = jnp.einsum("hgqt,thd->qhgd", probs, values_low, preferred_element_type=f32)
        return (attended_block, (row_max + jnp.log(denominator))[..., 0])

    starts = jnp.arange(blocks, dtype=jnp.int32) * block_rows
    attended, log_sums = lax.map(attend, starts)
    attended_low = attended.reshape(seq_len, q_cols).astype(bf16)
    resid = x_float + lax.psum_scatter(
        jnp.dot(attended_low, w_o, preferred_element_type=f32),
        "tensor",
        scatter_dimension=0,
        tiled=True,
    )
    normed2, inverse2 = normalize(resid)
    ffn_in = (normed2 * gain_ffn).astype(bf16)
    ffn_all = lax.all_gather(ffn_in, "tensor", axis=0, tiled=True)
    gate_up = jnp.dot(ffn_all, w_gu_flat, preferred_element_type=f32)
    gate_part = gate_up[:, :hidden]
    up_part = gate_up[:, hidden:]
    sigmoid_gate = jax.nn.sigmoid(gate_part)
    silu_gate = gate_part * sigmoid_gate
    mixed = (silu_gate * up_part).astype(bf16)
    result = resid + lax.psum_scatter(
        jnp.dot(mixed, w_down, preferred_element_type=f32).astype(jnp.bfloat16),
        "tensor",
        scatter_dimension=0,
        tiled=True,
    ).astype(jnp.float32)
    output = result.astype(bf16)
    grad_all = lax.all_gather(cotangent, "tensor", axis=0, tiled=True)
    grad_down = jnp.einsum("sf,sd->fd", mixed, grad_all, preferred_element_type=f32)
    grad_mixed = jnp.einsum("sd,fd->sf", grad_all, w_down, preferred_element_type=f32)
    grad_gate = grad_mixed * up_part * sigmoid_gate * (1.0 + gate_part * (1.0 - sigmoid_gate))
    grad_up = grad_mixed * silu_gate
    grad_gu = jnp.concatenate([grad_gate, grad_up], 1).astype(bf16)
    grad_w_gu = jnp.einsum("sd,sf->df", ffn_all, grad_gu, preferred_element_type=f32).reshape(
        model_width, 2, hidden
    )
    grad_ffn_in = lax.psum_scatter(
        jnp.einsum("sf,df->sd", grad_gu, w_gu_flat, preferred_element_type=f32).astype(
            jnp.bfloat16
        ),
        "tensor",
        scatter_dimension=0,
        tiled=True,
    ).astype(jnp.float32)
    gain_ffn_part = jnp.sum(grad_ffn_in * normed2, axis=0)
    grad_resid = cotangent.astype(f32) + norm_back(grad_ffn_in * gain_ffn, normed2, inverse2)
    branch_all = lax.all_gather(grad_resid.astype(bf16), "tensor", axis=0, tiled=True)
    grad_w_o = jnp.einsum("sc,sd->cd", attended_low, branch_all, preferred_element_type=f32)
    grad_attended = jnp.einsum("sd,cd->sc", branch_all, w_o, preferred_element_type=f32).astype(
        bf16
    )
    grad_attended = grad_attended.reshape(seq_len, kv_heads, group_size, head_dim)

    def attend_back(carried, scanned):
        first_row, lse_block = scanned
        masked, q_block = scores_of(first_row)
        probs = jnp.exp(masked - lse_block[..., None])
        go_block = lax.dynamic_slice_in_dim(grad_attended, first_row, block_rows, 0)
        grad_probs = jnp.einsum("qhgd,thd->hgqt", go_block, values_low, preferred_element_type=f32)
        grad_scores = (
            probs * (grad_probs - jnp.sum(probs * grad_probs, axis=-1, keepdims=True))
        ).astype(bf16)
        keys_next = carried[0] + score_scale * jnp.einsum(
            "hgqt,qhgd->thd", grad_scores, q_block, preferred_element_type=f32
        )
        values_next = carried[1] + jnp.einsum(
            "hgqt,qhgd->thd", probs.astype(bf16), go_block, preferred_element_type=f32
        )
        grad_q_block = score_scale * jnp.einsum(
            "hgqt,thd->qhgd", grad_scores, keys, preferred_element_type=f32
        )
        return ((keys_next, values_next), grad_q_block)

    zero_kv = jnp.zeros((seq_len, kv_heads, head_dim), f32)
    (grad_keys, grad_values), grad_queries = lax.scan(
        attend_back, (zero_kv, zero_kv), (starts, log_sums)
    )
    grad_q_normed = rotate(
        grad_queries.reshape(seq_len, q_heads, head_dim), cosine_table, -sine_table
    )
    q_gain_part = jnp.sum(grad_q_normed * q_normed, axis=(0, 1))
    grad_q_raw = (
        norm_back(grad_q_normed * q_gain, q_normed, q_inverse).astype(bf16).reshape(seq_len, q_cols)
    )
    grad_k_normed = rotate(grad_keys, cosine_table, -sine_table)
    k_gain_part = jnp.sum(grad_k_normed * k_normed, axis=(0, 1))
    grad_k_raw = (
        norm_back(grad_k_normed * k_gain, k_normed, k_inverse)
        .astype(bf16)
        .reshape(seq_len, kv_cols)
    )
    grad_kv = jnp.concatenate([grad_k_raw, grad_values.astype(bf16).reshape(seq_len, kv_cols)], 1)
    grad_w_q = jnp.einsum("sd,sc->dc", attn_all, grad_q_raw, preferred_element_type=f32)
    grad_w_kv = jnp.einsum("sd,sc->dc", attn_all, grad_kv, preferred_element_type=f32).reshape(
        model_width, 2, kv_cols
    )
    grad_attn_in = lax.psum_scatter(
        (
            jnp.einsum("sc,dc->sd", grad_q_raw, w_q, preferred_element_type=f32)
            + jnp.einsum("sc,dc->sd", grad_kv, w_kv_flat, preferred_element_type=f32)
        ).astype(jnp.bfloat16),
        "tensor",
        scatter_dimension=0,
        tiled=True,
    ).astype(jnp.float32)
    gain_attn_part = jnp.sum(grad_attn_in * normed1, axis=0)
    grad_tokens = grad_resid + norm_back(grad_attn_in * gain_attn, normed1, inverse1)
    gain_sums = lax.psum(
        (gain_attn_part, gain_ffn_part, q_gain_part, k_gain_part), ("dp", "tensor")
    )
    shard_q, shard_kv, shard_o, shard_gu, shard_down = (
        lax.psum_scatter(
            grad_w_q.astype(jnp.bfloat16), "dp", scatter_dimension=0, tiled=True
        ).astype(jnp.float32),
        lax.psum_scatter(
            grad_w_kv.astype(jnp.bfloat16), "dp", scatter_dimension=0, tiled=True
        ).astype(jnp.float32),
        lax.psum_scatter(
            grad_w_o.astype(jnp.bfloat16), "dp", scatter_dimension=1, tiled=True
        ).astype(jnp.float32),
        lax.psum_scatter(
            grad_w_gu.astype(jnp.bfloat16), "dp", scatter_dimension=0, tiled=True
        ).astype(jnp.float32),
        lax.psum_scatter(
            grad_down.astype(jnp.bfloat16), "dp", scatter_dimension=1, tiled=True
        ).astype(jnp.float32),
    )
    return (
        output,
        grad_tokens,
        gain_sums[0],
        shard_q,
        shard_kv,
        gain_sums[2],
        gain_sums[3],
        shard_o,
        gain_sums[1],
        shard_gu,
        shard_down,
    )


def solution(mesh):
    in_specs = (
        P(("dp", "tensor"), None),
        P("dp", None),
        P(),
        P(None, "tensor"),
        P(None, None, "tensor"),
        P(),
        P(),
        P("tensor", None),
        P(),
        P(None, None, "tensor"),
        P("tensor", None),
        P(("dp", "tensor"), None),
    )
    out_specs = (
        P(("dp", "tensor"), None),
        P(("dp", "tensor"), None),
        P(),
        P("dp", "tensor"),
        P("dp", None, "tensor"),
        P(),
        P(),
        P("tensor", "dp"),
        P(),
        P("dp", None, "tensor"),
        P("tensor", "dp"),
    )
    paired_axes = mesh.shape["tensor"] == 2 and mesh.shape["dp"] == 16
    body = functools.partial(paired, mesh.shape["dp"]) if paired_axes else shards
    return jax.shard_map(body, mesh=mesh, in_specs=in_specs, out_specs=out_specs, check_vma=False)
```

```python
import functools
import math

import jax
import jax.numpy as jnp
from jax import lax
from jax.experimental import pallas as pl
from jax.experimental.pallas import tpu as pltpu
from jax.sharding import PartitionSpec as P

EPS = 1e-06
THETA = 1000000.0
LOG2E = 1.4426950408889634
LN2 = 0.6931471805599453
BLOCK = 256
PAIR = 128
SAME = 256.0
F32 = jnp.float32
BF16 = jnp.bfloat16
COST_RATE = 1.0e13
VMEM_LIMIT = 56 * 1024 * 1024
BACK_VMEM = 61 * 1024 * 1024


def dot_nn(a, b):
    return lax.dot_general(a, b, (((1,), (0,)), ((), ())), preferred_element_type=F32)


def dot_nt(a, b):
    return lax.dot_general(a, b, (((1,), (1,)), ((), ())), preferred_element_type=F32)


def cost(seconds):
    return pl.CostEstimate(flops=int(seconds * COST_RATE), bytes_accessed=0, transcendentals=0)


def lane_of(shape):
    return lax.broadcasted_iota(jnp.int32, shape, len(shape) - 1)


def head_mean(values):
    high = values.astype(BF16)
    low = (values - high.astype(F32)).astype(BF16)
    row = lax.broadcasted_iota(jnp.int32, (PAIR, PAIR), 0) // 64
    col = lax.broadcasted_iota(jnp.int32, (PAIR, PAIR), 1) // 64
    mean = jnp.where(row == col, 1.0 / 64.0, 0.0).astype(BF16)
    return dot_nn(high, mean) + dot_nn(low, mean)


def swap_halves(values):
    first = lane_of(values.shape) % 64 < 32
    return jnp.where(first, pltpu.roll(values, 96, 1), pltpu.roll(values, 32, 1))


def rope(values, cosine, sine):
    return values * cosine + swap_halves(values) * sine


def row_norm(x):
    return lax.rsqrt(jnp.mean(x * x, axis=-1, keepdims=True) + EPS)


def qkv_kernel(
    x_ref, gain_ref, wq_ref, wk_ref, wv_ref, qg_ref, kg_ref, cos_ref, sin_ref,
    attn_ref, q_ref, kd_ref, vd_ref, qraw_ref, kraw_ref,
):
    x = x_ref[...].astype(F32)
    attn = (x * row_norm(x) * gain_ref[...]).astype(BF16)
    attn_ref[...] = attn
    q = dot_nn(attn, wq_ref[...])
    k = dot_nn(attn, wk_ref[...])
    v = dot_nn(attn, wv_ref[...])
    qraw_ref[...] = q.astype(BF16)
    kraw_ref[...] = k.astype(BF16)
    cosine, sine = cos_ref[...], sin_ref[...]
    for g in range(q.shape[1] // PAIR):
        at = slice(g * PAIR, (g + 1) * PAIR)
        u = q[:, at]
        n = u * lax.rsqrt(head_mean(u * u) + EPS)
        q_ref[:, at] = (rope(n * qg_ref[...], cosine, sine) * (LOG2E / 8.0)).astype(BF16)
    low = lane_of((x.shape[0], PAIR)) < 64
    for p in range(k.shape[1] // PAIR):
        at = slice(p * PAIR, (p + 1) * PAIR)
        u = k[:, at]
        n = u * lax.rsqrt(head_mean(u * u) + EPS)
        roped = rope(n * kg_ref[...], cosine, sine)
        for src, dst in ((roped, kd_ref), (v[:, at], vd_ref)):
            turned = pltpu.roll(src, 64, 1)
            dst[:, 2 * p * PAIR : (2 * p + 1) * PAIR] = jnp.where(low, src, turned).astype(BF16)
            dst[:, (2 * p + 1) * PAIR : (2 * p + 2) * PAIR] = jnp.where(low, turned, src).astype(BF16)


def qkv(x, gain, w_q, w_kv, qg, kg, cosine, sine, half):
    rows, width = x.shape
    qc, kc = w_q.shape[1], w_kv.shape[1] // 2
    nb = rows // BLOCK
    whole = lambda shape, *at: pl.BlockSpec(shape, lambda i: at)
    row = lambda cols: pl.BlockSpec((BLOCK, cols), lambda i: (i, 0))
    table = pl.BlockSpec((BLOCK, PAIR), lambda i: (i + half * nb, 0))
    return pl.pallas_call(
        qkv_kernel,
        grid=(nb,),
        in_specs=[
            row(width), whole((1, width), 0, 0), whole((width, qc), 0, 0),
            whole((width, kc), 0, 0), whole((width, kc), 0, 1),
            whole((1, PAIR), 0, 0), whole((1, PAIR), 0, 0), table, table,
        ],
        out_specs=[row(width), row(qc), row(2 * kc), row(2 * kc), row(qc), row(kc)],
        out_shape=[
            jax.ShapeDtypeStruct((rows, c), BF16) for c in (width, qc, 2 * kc, 2 * kc, qc, kc)
        ],
        compiler_params=pltpu.CompilerParams(vmem_limit_bytes=VMEM_LIMIT),
        cost_estimate=cost(5e-6),
        name="qkv",
    )(x, gain, w_q, w_kv, w_kv, qg, kg, cosine, sine)


MESH = pl.DeviceIdType.MESH
CHUNK = 768
SPLIT = 512
DEPTH = 2


def dot_tn(a, b):
    return lax.dot_general(a, b, (((0,), (0,)), ((), ())), preferred_element_type=F32)


def pack_columns(dst, first, ref):
    rows, width = ref.shape
    low = lane_of((rows, PAIR)) < 64
    for k in range(width // (2 * PAIR)):
        a = ref[:, 2 * k * PAIR : (2 * k + 1) * PAIR].astype(F32)
        b = ref[:, (2 * k + 1) * PAIR : (2 * k + 2) * PAIR].astype(F32)
        lanes = slice(k * PAIR, (k + 1) * PAIR)
        dst[0, first : first + rows, lanes] = jnp.where(low, a, pltpu.roll(b, 64, 1)).astype(BF16)
        dst[1, first : first + rows, lanes] = jnp.where(low, pltpu.roll(a, 64, 1), b).astype(BF16)


BACK_INPUTS = (
    "h", "cot_pack", "ffn_pack", "attn_pack", "tok_own", "tok_oth", "y_send", "branch", "do_own", "do_send",
    "w_q", "w_kv", "q_own", "q_oth", "kd_own", "kd_oth", "vd_own", "vd_oth", "o_own", "o_oth", "linv_own", "linv_oth",
    "qraw_own", "qraw_oth", "kraw_own", "kraw_oth",
)
BACK_TABLES = ("segq", "segk", "cos", "sin", "gain_ffn", "qg", "kg")
BACK_OUTPUTS = ("ga_out", "ga_recv", "shards", "gains", "y_recv")


class Names:
    def __init__(self, names, refs):
        self.__dict__.update(zip(names, refs))


def back_kernel(n_dp, scratch_names, *refs):
    m = Names(BACK_INPUTS + BACK_TABLES + BACK_OUTPUTS + scratch_names, refs)
    rows, width = m.tok_own.shape
    hidden = m.h.shape[3]
    per_x = hidden // CHUNK
    n_wide = 3 * per_x
    n_chunks = n_wide + 2
    nb = 2 * rows // BLOCK
    t = lax.axis_index("tensor")
    d = lax.axis_index("dp")
    core = lax.rem(d, 2)
    x = lax.rem(d // 2, 2)
    zl = lax.rem(d // 4, 2)
    zh = d // 8
    over_t = {"tensor": 1 - t}
    over_core = {"dp": d + 1 - 2 * core}
    over_x = {"dp": d + 2 - 4 * x}
    over_zl = {"dp": d + 4 - 8 * zl}
    over_zh = {"dp": d + 8 - 16 * zh}
    partners = (over_t, over_core, over_x, over_zl, over_zh)
    low = lane_of((rows, PAIR)) < 64
    own_rows, oth_rows = pl.ds(0, rows), pl.ds(rows, rows)

    barrier = pltpu.get_barrier_semaphore()
    for p in partners:
        pl.semaphore_signal(barrier, inc=1, device_id=p, device_id_type=MESH)
    pl.semaphore_wait(barrier, len(partners))

    def tensor_copy(i, src, dst):
        return pltpu.make_async_remote_copy(
            src_ref=src, dst_ref=dst, send_sem=m.t_send.at[i], recv_sem=m.t_recv.at[i],
            device_id=over_t, device_id_type=MESH,
        )

    do_copy = tensor_copy(1, m.do_send, m.do_recv)
    branch_copy = tensor_copy(2, m.branch_v, m.branch_recv)
    y_copy = tensor_copy(3, m.y_send, m.y_recv)
    ga_copy = tensor_copy(4, m.branch_v, m.ga_recv)

    def rs_copy(stage, c, src, dst, device):
        return pltpu.make_async_remote_copy(
            src_ref=src, dst_ref=dst, send_sem=m.rs_send.at[stage, c], recv_sem=m.rs_recv.at[stage, c],
            device_id=device, device_id_type=MESH,
        )

    left, right = pl.ds(0, SPLIT), pl.ds(SPLIT, CHUNK - SPLIT)
    every = pl.ds(0, 2)
    block_rows = m.sums.shape[4]
    full_rows = pl.ds(0, block_rows)

    def core_copy(c):
        return rs_copy(0, c, m.core_send.at[lax.rem(c, 2)], m.sums.at[c], over_core)

    def first_copies(c):
        return (
            rs_copy(1, c, m.sums.at[c, every, every, 1 - x, full_rows, left], m.r1a.at[c], over_x),
            rs_copy(2, c, m.sums.at[c, every, 1 - zl, every, full_rows, right], m.r1b.at[c], over_zl),
        )

    def second_copies(c):
        return (
            rs_copy(3, c, m.sums.at[c, every, 1 - zl, x, full_rows, left], m.r2a.at[c], over_zl),
            rs_copy(4, c, m.sums.at[c, every, zl, 1 - x, full_rows, right], m.r2b.at[c], over_x),
        )

    def third_copy(c):
        return rs_copy(5, c, m.sums.at[c, 1 - zh, zl, x], m.r3.at[c], over_zh)

    def local(i, src, dst):
        return pltpu.make_async_copy(src, dst, m.l_sem.at[i])

    def both(i, src_own, src_oth, dst):
        return (local(i, src_own, dst.at[own_rows]), local(i + 1, src_oth, dst.at[oth_rows]))

    def start(copies):
        for copy in copies:
            copy.start()

    def wait(copies):
        for copy in copies:
            copy.wait()

    def add_core(c):
        core_copy(c).wait_recv()
        for a in range(2):
            for b in range(2):
                for e in range(2):
                    m.sums[c, a, b, e] = (
                        m.sums[c, a, b, e].astype(F32) + m.kept[lax.rem(c, 2), a, b, e].astype(F32)
                    ).astype(BF16)

    def total_copy(c):
        slot = lax.rem(c, 2)
        return pltpu.make_async_copy(m.totals.at[slot], m.shards.at[c], m.s_sem.at[slot])

    def tick(i):
        @pl.when(i < n_chunks)
        def _():
            a_copy, b_copy = first_copies(i)
            a_copy.wait_recv()
            b_copy.wait_recv()
            for a in range(2):
                for b in range(2):
                    m.sums[i, a, b, x, :, :SPLIT] = (
                        m.sums[i, a, b, x, :, :SPLIT].astype(F32) + m.r1a[i, a, b].astype(F32)
                    ).astype(BF16)
                    m.sums[i, a, zl, b, :, SPLIT:] = (
                        m.sums[i, a, zl, b, :, SPLIT:].astype(F32) + m.r1b[i, a, b].astype(F32)
                    ).astype(BF16)
            start(second_copies(i))

        @pl.when(i + DEPTH < n_chunks - 1)
        def _():
            start(first_copies(i + DEPTH))

        @pl.when((i >= 1) & (i < n_chunks + 1))
        def _():
            c = i - 1
            a_copy, b_copy = second_copies(c)
            a_copy.wait_recv()
            b_copy.wait_recv()
            for a in range(2):
                m.sums[c, a, zl, x, :, :SPLIT] = (
                    m.sums[c, a, zl, x, :, :SPLIT].astype(F32) + m.r2a[c, a].astype(F32)
                ).astype(BF16)
                m.sums[c, a, zl, x, :, SPLIT:] = (
                    m.sums[c, a, zl, x, :, SPLIT:].astype(F32) + m.r2b[c, a].astype(F32)
                ).astype(BF16)
            third_copy(c).start()

        @pl.when((i >= 2) & (i < n_chunks + 2))
        def _():
            c = i - 2
            third_copy(c).wait_recv()

            @pl.when(c >= 2)
            def _():
                total_copy(c - 2).wait()

            m.totals[lax.rem(c, 2)] = m.sums[c, zh, zl, x].astype(F32) + m.r3[c].astype(F32)
            total_copy(c).start()

    def put(ref, slot, lanes, value):
        for a in range(2):
            for b in range(2):
                for e in range(2):
                    k = ((a * 2 + b) * 2 + e) * block_rows
                    ref[slot, a, b, e, :, lanes] = value[k : k + block_rows].astype(BF16)

    do_copy.start()
    packs = [local(i, src, m.packed.at[i]) for i, src in enumerate((m.cot_pack, m.ffn_pack))]
    attn_load = local(0, m.attn_pack, m.packed.at[0])
    start(packs)
    loads = [
        local(2, m.branch, m.branch_v), local(3, m.do_own, m.do_v), local(7, m.w_q, m.wq_v), local(8, m.w_kv, m.wkv_v),
        *both(9, m.o_own, m.o_oth, m.o_v), *both(11, m.kraw_own, m.kraw_oth, m.kraw_v),
    ]

    def tiles(g):
        slot = lax.rem(g, 2)
        lanes = pl.ds(pl.multiple_of(g * PAIR, PAIR), PAIR)
        out = []
        for j, (own, oth, dst) in enumerate((
            (m.q_own, m.q_oth, m.q_v), (m.kd_own, m.kd_oth, m.kd_v), (m.vd_own, m.vd_oth, m.vd_v),
            (m.qraw_own, m.qraw_oth, m.qraw_v), (m.linv_own, m.linv_oth, m.linv_v),
        )):
            out.append(pltpu.make_async_copy(own.at[:, lanes], dst.at[slot, own_rows], m.g_sem.at[slot, 2 * j]))
            out.append(pltpu.make_async_copy(oth.at[:, lanes], dst.at[slot, oth_rows], m.g_sem.at[slot, 2 * j + 1]))
        return out

    def wide_phase(y_v):
        def fetch(c):
            slot = lax.rem(c, 2)
            cols = pl.ds(pl.multiple_of(lax.rem(c, per_x) * CHUNK, CHUNK), CHUNK)
            return [
                pltpu.make_async_copy(
                    m.h.at[j, c // per_x, :, cols], y_v.at[slot, at], m.h_sem.at[slot, j]
                )
                for j, at in enumerate((own_rows, oth_rows))
            ]

        start(fetch(0))
        start(loads)
        packs[0].wait()
        loads[0].wait()

        def chunk(c, carry):
            slot = lax.rem(c, 2)
            which = jnp.minimum(c // per_x, 1)
            wait(fetch(c))

            @pl.when(c == per_x)
            def _():
                packs[1].wait()
                attn_load.start()

            @pl.when(c + 1 < n_wide)
            def _():
                start(fetch(c + 1))

            @pl.when(c >= 2)
            def _():
                core_copy(c - 2).wait_send()

            put(m.core_send, slot, slice(None), dot_tn(m.packed[which, 1 - core], y_v[slot]))
            core_copy(c).start()
            put(m.kept, slot, slice(None), dot_tn(m.packed[which, core], y_v[slot]))

            @pl.when(c >= 1)
            def _():
                add_core(c - 1)

            @pl.when((c >= 1) & (c <= DEPTH))
            def _():
                start(first_copies(c - 1))

            @pl.when(c == n_wide - 4)
            def _():
                do_copy.wait_recv()
                branch_copy.start()

            @pl.when((c == n_wide - 4) | (c == n_wide - 2))
            def _():
                tick((c - n_wide + 4) // 2)

            return carry

        lax.fori_loop(0, n_wide, chunk, 0)
        add_core(n_wide - 1)
        tick(2)

    pl.run_scoped(wide_phase, pltpu.VMEM((2, 2 * rows, CHUNK), BF16))
    start(tiles(0))

    wait(loads[1:])
    attn_load.wait()
    y_copy.start()

    def narrow_chunk(p):
        c = n_wide + p
        slot = lax.rem(c, 2)
        core_copy(c - 2).wait_send()
        cols = pl.ds(pl.multiple_of(p * SPLIT, SPLIT), SPLIT)
        o_cols = pl.ds(pl.multiple_of(p * (CHUNK - SPLIT), CHUNK - SPLIT), CHUNK - SPLIT)
        for which, dst in ((1 - core, m.core_send), (core, m.kept)):
            put(dst, slot, slice(0, SPLIT), dot_tn(m.packed[0, which], m.g_v[:, cols]))
            put(dst, slot, slice(SPLIT, CHUNK), dot_tn(m.packed[1, which], m.o_v[:, o_cols]))
        core_copy(c).start()

    def place(block):
        return pl.ds(pl.multiple_of(lax.rem(block + t * (nb // 2), nb) * BLOCK, BLOCK), BLOCK)

    m.qgain[...] = jnp.zeros_like(m.qgain)
    m.kgain[...] = jnp.zeros_like(m.kgain)

    def attention_phase(qx, dox, kx0, kx1, vx0, vx1, kt, dqt, dk0, dk1, dv0, dv1, dks, dvs):
        all_low = lane_of((2 * rows, PAIR)) < 64
        one = jnp.ones((2 * rows, PAIR), F32)
        zero = jnp.zeros((2 * rows, PAIR), BF16)
        qx[:, PAIR:] = m.segq[...]
        kx0[:, PAIR:] = m.segk[...]
        kx1[:, PAIR:] = m.segk[...]
        vx0[:, PAIR:] = jnp.where(all_low, -one, 0.0).astype(BF16)
        vx1[:, PAIR:] = jnp.where(all_low, 0.0, -one).astype(BF16)

        def step(qb, kb, diagonal):
            qs, ks = place(qb), place(kb)
            q, do = qx[qs, :], dox[qs, :]
            for h, (kx, vx, dk, dv) in enumerate(((kx0, vx0, dk0, dv0), (kx1, vx1, dk1, dv1))):
                s = dot_nt(kx[ks, :], q)
                if diagonal:
                    r = lax.broadcasted_iota(jnp.int32, s.shape, 0)
                    s = jnp.where(r <= lane_of(s.shape), s, -1e30)
                e = jnp.exp2(s)
                ds = (e * dot_nt(vx[ks, :], do)).astype(BF16)
                dv[ks, :] += dot_nn(e.astype(BF16), do[:, :PAIR])
                dk[ks, :] += dot_nn(ds, q[:, :PAIR])
                dqt[h * 64 : (h + 1) * 64, qs] += dot_nn(kt[:, ks], ds)

        def group(g, carry):
            slot = lax.rem(g, 2)
            lanes = pl.ds(pl.multiple_of(g * PAIR, PAIR), PAIR)
            p = g // 2
            wait(tiles(g))

            @pl.when(g + 1 < 4)
            def _():
                start(tiles(g + 1))

            qx[:, :PAIR] = m.q_v[slot]
            k, v = m.kd_v[slot], m.vd_v[slot]
            kx0[:, :PAIR] = jnp.where(all_low, k, zero)
            kx1[:, :PAIR] = jnp.where(all_low, zero, k)
            vx0[:, :PAIR] = jnp.where(all_low, v, zero)
            vx1[:, :PAIR] = jnp.where(all_low, zero, v)
            kt[...] = jnp.transpose(k.astype(F32))[:64, :].astype(BF16)
            for at, do_ref in ((own_rows, m.do_v), (oth_rows, m.do_recv)):
                scaled = do_ref[:, lanes].astype(F32) * m.linv_v[slot, at, :]
                dox[at, :PAIR] = scaled.astype(BF16)
                dox[at, PAIR:] = (scaled * m.o_v[at, lanes].astype(F32)).astype(BF16)
            for ref in (dqt, dk0, dk1, dv0, dv1):
                ref[...] = jnp.zeros_like(ref)

            def q_body(qb, c):
                step(qb, qb, True)

                def k_body(kb, cc):
                    step(qb, kb, False)
                    return cc

                lax.fori_loop(jnp.maximum(qb - 2, 0), qb, k_body, 0)
                return c

            lax.fori_loop(0, nb, q_body, 0)

            @pl.when(g == 1)
            def _():
                tick(4)

            g_lanes = pl.ds(pl.multiple_of(p * SPLIT + slot * PAIR, PAIR), PAIR)
            for at in (own_rows, oth_rows):
                dq = jnp.transpose(dqt[:, at]) * 0.125
                normed_grad = rope(dq, m.cos[at, :], -m.sin[at, :])
                raw = m.qraw_v[slot, at, :].astype(F32)
                inverse = lax.rsqrt(head_mean(raw * raw) + EPS)
                u = raw * inverse
                m.qgain[...] += jnp.sum(normed_grad * u, axis=0, keepdims=True)
                w = normed_grad * m.qg[...]
                m.g_v[at, g_lanes] = (inverse * (w - u * head_mean(w * u))).astype(BF16)

            def gathered(a, b, at):
                joined = jnp.where(low, a[at, :], b[at, :])
                return joined + pltpu.roll(joined, 64, 1)

            @pl.when(slot == 0)
            def _():
                for at in (own_rows, oth_rows):
                    dks[at, :] = gathered(dk0, dk1, at)
                    dvs[at, :] = gathered(dv0, dv1, at)

            @pl.when(slot == 1)
            def _():
                k_lanes = pl.ds(pl.multiple_of(p * SPLIT + 2 * PAIR, PAIR), PAIR)
                v_lanes = pl.ds(pl.multiple_of(p * SPLIT + 3 * PAIR, PAIR), PAIR)
                raw_lanes = pl.ds(pl.multiple_of(p * PAIR, PAIR), PAIR)
                for at in (own_rows, oth_rows):
                    dk = jnp.where(low, dks[at, :], gathered(dk0, dk1, at)) * LN2
                    dv = jnp.where(low, dvs[at, :], gathered(dv0, dv1, at))
                    normed_grad = rope(dk, m.cos[at, :], -m.sin[at, :])
                    raw = m.kraw_v[at, raw_lanes].astype(F32)
                    inverse = lax.rsqrt(head_mean(raw * raw) + EPS)
                    u = raw * inverse
                    m.kgain[...] += jnp.sum(normed_grad * u, axis=0, keepdims=True)
                    w = normed_grad * m.kg[...]
                    m.g_v[at, k_lanes] = (inverse * (w - u * head_mean(w * u))).astype(BF16)
                    m.g_v[at, v_lanes] = dv.astype(BF16)

                @pl.when(p == 0)
                def _():
                    branch_copy.wait_recv()
                    pack_columns(m.packed.at[1], 0, m.branch_v)
                    pack_columns(m.packed.at[1], rows, m.branch_recv)

                narrow_chunk(p)

            @pl.when(g == 2)
            def _():
                add_core(n_wide)

            tick(3 + g + jnp.minimum(g, 1))
            return carry

        lax.fori_loop(0, 4, group, 0)

    pl.run_scoped(
        attention_phase,
        *[pltpu.VMEM((2 * rows, 2 * PAIR), BF16)] * 6,
        pltpu.VMEM((64, 2 * rows), BF16), pltpu.VMEM((PAIR, 2 * rows), F32),
        *[pltpu.VMEM((2 * rows, PAIR), F32)] * 6,
    )

    def attn_in_grad(at):
        out = None
        qc, kc = m.wq_v.shape[1], m.wkv_v.shape[1] // 2
        for p in range(2):
            for ref, base, begin, size in (
                (m.wq_v, 0, 0, 2 * PAIR), (m.wkv_v, 0, 2 * PAIR, PAIR), (m.wkv_v, kc, 3 * PAIR, PAIR)
            ):
                term = dot_nt(
                    m.g_v[at, p * SPLIT + begin : p * SPLIT + begin + size],
                    ref[:, base + p * size : base + (p + 1) * size],
                )
                out = term if out is None else out + term
        return out

    def end_phase(ga_own, tok_v):
        start(both(0, m.tok_own, m.tok_oth, tok_v))
        wait(both(0, m.tok_own, m.tok_oth, tok_v))

        def grad_and_gain(at):
            grad = attn_in_grad(at)
            tokens = tok_v[at, :].astype(F32)
            return grad, jnp.sum(grad * (tokens * row_norm(tokens)), axis=0, keepdims=True)

        branch_copy.wait_send()
        total = jnp.zeros((1, width), F32)
        for i in range(rows // BLOCK):
            grad, part = grad_and_gain(pl.ds(rows + i * BLOCK, BLOCK))
            m.branch_v[i * BLOCK : (i + 1) * BLOCK, :] = grad.astype(BF16)
            total += part
        ga_copy.start()
        add_core(n_chunks - 1)
        start(first_copies(n_chunks - 1))
        tick(n_chunks - 3)
        for i in range(rows // BLOCK):
            grad, part = grad_and_gain(pl.ds(i * BLOCK, BLOCK))
            ga_own[i * BLOCK : (i + 1) * BLOCK, :] = grad.astype(BF16)
            total += part
        ga_out_copy = local(3, ga_own, m.ga_out)
        ga_out_copy.start()
        for r in range(width // PAIR):
            m.mine[r : r + 1, :] = total[:, r * PAIR : (r + 1) * PAIR]
            at = slice(width // PAIR + r, width // PAIR + r + 1)
            m.mine[at, :] = m.gain_ffn[:, r * PAIR : (r + 1) * PAIR]
        last = 2 * width // PAIR
        m.mine[last : last + 1, :] = m.qgain[...]
        m.mine[last + 1 : last + 2, :] = m.kgain[...]
        m.mine[last + 2 :, :] = jnp.zeros((m.mine.shape[0] - last - 2, PAIR), F32)

        def gain_copy(i, device):
            return pltpu.make_async_remote_copy(
                src_ref=m.gain_out.at[i], dst_ref=m.gain_in.at[i], send_sem=m.gain_sem.at[0, i],
                recv_sem=m.gain_sem.at[1, i], device_id=device, device_id_type=MESH,
            )

        for i, device in enumerate(partners):
            m.gain_out[i] = m.mine[...]
            gain_copy(i, device).start()
            if i >= 1:
                tick(n_chunks - 3 + i)
            gain_copy(i, device).wait_recv()
            m.mine[...] += m.gain_in[i]
        m.gains[...] = m.mine[...]
        y_copy.wait_recv()
        ga_copy.wait_recv()
        for copy in (do_copy, y_copy, ga_copy):
            copy.wait_send()
        for i, device in enumerate(partners):
            gain_copy(i, device).wait_send()
        for c in (n_chunks - 2, n_chunks - 1):
            core_copy(c).wait_send()

        def drain(c, carry):
            for copy in (*first_copies(c), *second_copies(c), third_copy(c)):
                copy.wait_send()
            return carry

        lax.fori_loop(0, n_chunks, drain, 0)
        for c in (n_chunks - 2, n_chunks - 1):
            total_copy(c).wait()
        ga_out_copy.wait()

    pl.run_scoped(end_phase, pltpu.VMEM((rows, width), BF16), pltpu.VMEM((2 * rows, width), BF16))


def back(n_dp, values, tables):
    rows, width = values["tok_own"].shape
    hidden = values["h"].shape[3]
    seq = 2 * rows
    qc = values["w_q"].shape[1]
    n_chunks = 3 * hidden // CHUNK + 2
    block = width // n_dp
    vm = pltpu.VMEM
    dma = pltpu.SemaphoreType.DMA
    scratch = dict(
        packed=vm((2, 2, seq, width // 2), BF16),
        core_send=vm((2, 2, 2, 2, block, CHUNK), BF16), kept=vm((2, 2, 2, 2, block, CHUNK), BF16),
        sums=vm((n_chunks, 2, 2, 2, block, CHUNK), BF16),
        r1a=vm((n_chunks, 2, 2, block, SPLIT), BF16), r1b=vm((n_chunks, 2, 2, block, CHUNK - SPLIT), BF16),
        r2a=vm((n_chunks, 2, block, SPLIT), BF16), r2b=vm((n_chunks, 2, block, CHUNK - SPLIT), BF16),
        r3=vm((n_chunks, block, CHUNK), BF16), totals=vm((2, block, CHUNK), F32),
        wq_v=vm((width, qc), BF16), wkv_v=vm((width, qc), BF16),
        o_v=vm((seq, qc), BF16), kraw_v=vm((seq, qc // 2), BF16),
        q_v=vm((2, seq, PAIR), BF16), kd_v=vm((2, seq, PAIR), BF16), vd_v=vm((2, seq, PAIR), BF16),
        qraw_v=vm((2, seq, PAIR), BF16), linv_v=vm((2, seq, PAIR), F32),
        g_v=vm((seq, 2 * SPLIT), BF16), do_v=vm((rows, qc), BF16),
        do_recv=vm((rows, qc), BF16),
        branch_v=vm((rows, width), BF16), branch_recv=vm((rows, width), BF16),
        qgain=vm((1, PAIR), F32), kgain=vm((1, PAIR), F32), mine=vm((24, PAIR), F32),
        gain_out=vm((5, 24, PAIR), F32), gain_in=vm((5, 24, PAIR), F32),
        t_send=dma((5,)), t_recv=dma((5,)), rs_send=dma((6, n_chunks)), rs_recv=dma((6, n_chunks)),
        l_sem=dma((14,)), g_sem=dma((2, 10)), h_sem=dma((2, 2)), s_sem=dma((2,)), gain_sem=dma((2, 5)),
    )
    anywhere = pl.BlockSpec(memory_space=pl.ANY)
    vmem = pl.BlockSpec(memory_space=pltpu.VMEM)
    return pl.pallas_call(
        functools.partial(back_kernel, n_dp, tuple(scratch)),
        in_specs=[anywhere] * len(BACK_INPUTS) + [vmem] * len(BACK_TABLES),
        out_specs=[anywhere, anywhere, anywhere, vmem, anywhere],
        out_shape=[
            jax.ShapeDtypeStruct((rows, width), BF16),
            jax.ShapeDtypeStruct((rows, width), BF16),
            jax.ShapeDtypeStruct((n_chunks, block, CHUNK), F32), jax.ShapeDtypeStruct((24, PAIR), F32),
            jax.ShapeDtypeStruct((rows, width), BF16),
        ],
        scratch_shapes=list(scratch.values()),
        compiler_params=pltpu.CompilerParams(
            vmem_limit_bytes=BACK_VMEM, collective_id=0, has_side_effects=True
        ),
        cost_estimate=cost(100e-6),
        name="back",
    )(*[values[k] for k in BACK_INPUTS], *[tables[k] for k in BACK_TABLES])


FRONT_INPUTS = (
    "tok_own", "tok_oth", "cot_own", "w_q", "w_kv", "w_o", "w_gu", "w_down",
    "q_own", "kd_own", "vd_own", "attn_own",
)
FRONT_TABLES = ("segq", "segk", "cos", "sin", "gain1", "gain2", "qg", "kg")
FRONT_OUTPUTS = (
    "q_oth", "kd_oth", "vd_oth", "qraw_oth", "kraw_oth", "o_own", "o_oth", "linv_own", "linv_oth",
    "cot_pack", "ffn_pack", "attn_pack", "h", "base", "y_send", "branch", "do_own", "do_send",
    "gain_ffn",
)
PIECES = 4


def front_kernel(scratch_names, *refs):
    m = Names(FRONT_INPUTS + FRONT_TABLES + FRONT_OUTPUTS + scratch_names, refs)
    rows, width = m.tok_own.shape
    hidden = m.w_down.shape[0]
    qc = m.w_q.shape[1]
    kc = m.w_kv.shape[1] // 2
    nb = 2 * rows // BLOCK
    t = lax.axis_index("tensor")
    d = lax.axis_index("dp")
    core = lax.rem(d, 2)
    x_at = lax.rem(d // 2, 2)
    over_x = {"dp": d + 2 - 4 * x_at}
    over_t = {"tensor": 1 - t}
    over_core = {"dp": d + 1 - 2 * core}

    barrier = pltpu.get_barrier_semaphore()
    for p in (over_t, over_core, over_x):
        pl.semaphore_signal(barrier, inc=1, device_id=p, device_id_type=MESH)
    pl.semaphore_wait(barrier, 3)

    def remote(i, src, dst, device):
        return pltpu.make_async_remote_copy(
            src_ref=src, dst_ref=dst, send_sem=m.r_send.at[i], recv_sem=m.r_recv.at[i],
            device_id=device, device_id_type=MESH,
        )

    pieces = [pl.ds(i * (rows // PIECES), rows // PIECES) for i in range(PIECES)]
    halves = [pl.ds(i * BLOCK, BLOCK) for i in range(rows // BLOCK)]
    cot_copies = [remote(i, m.cot_own.at[at], m.cot_v.at[1, at], over_t) for i, at in enumerate(pieces)]
    part_o = qc // 4

    def wo_part(x_of, core_of):
        return pl.ds(pl.multiple_of((2 * x_of + core_of) * part_o, part_o), part_o)

    mine_o, core_o = wo_part(x_at, core), wo_part(x_at, 1 - core)
    wo_copy = remote(4, m.w_o.at[mine_o], m.wot_v.at[mine_o], over_t)
    wo_core = remote(5, m.wot_v.at[mine_o], m.wot_v.at[mine_o], over_core)
    wo_x = (
        remote(11, m.wot_v.at[mine_o], m.wot_v.at[mine_o], over_x),
        remote(12, m.wot_v.at[core_o], m.wot_v.at[core_o], over_x),
    )
    o_copy = remote(6, m.o_v.at[1], m.theirs, over_t)
    ffn_copies = [remote(7 + i, m.ffn_v.at[0, at], m.ffn_v.at[1, at], over_t) for i, at in enumerate(halves)]
    gf_copies = [remote(9 + i, m.gf_send.at[at], m.gf_in.at[at], over_t) for i, at in enumerate(halves)]

    def local(i, src, dst):
        return pltpu.make_async_copy(src, dst, m.l_sem.at[i])

    loads = [
        local(i, src, dst)
        for i, (src, dst) in enumerate((
            (m.tok_oth, m.tok_v.at[1]), (m.w_q, m.wq_v), (m.w_kv, m.wkv_v), (m.q_own, m.q_v.at[0]),
            (m.kd_own, m.kd_v.at[0]), (m.vd_own, m.vd_v.at[0]), (m.w_o, m.wom_v), (m.tok_own, m.tok_v.at[0]),
            (m.attn_own, m.attn_v.at[0]), (m.cot_own, m.cot_v.at[0]), (m.w_gu, m.wgu_v), (m.w_down, m.wd_v),
        ))
    ]
    out_sem = [0]
    stores = []

    def store(src, dst):
        copy = pltpu.make_async_copy(src, dst, m.o_sem.at[out_sem[0]])
        out_sem[0] += 1
        copy.start()
        stores.append(copy)

    wo_copy.start()
    for copy in cot_copies[:3]:
        copy.start()
    for copy in loads:
        copy.start()
    for copy in loads[:6]:
        copy.wait()

    for at in halves:
        table = pl.ds(rows + at.start, BLOCK)
        qkv_kernel(
            m.tok_v.at[1, at], m.gain1, m.wq_v, m.wkv_v.at[:, pl.ds(0, kc)], m.wkv_v.at[:, pl.ds(kc, kc)],
            m.qg, m.kg, m.cos.at[table], m.sin.at[table],
            m.attn_v.at[1, at], m.q_v.at[1, at], m.kd_v.at[1, at], m.vd_v.at[1, at], m.qraw_v.at[at], m.kraw_v.at[at],
        )
    for src, dst in (
        (m.q_v.at[1], m.q_oth), (m.kd_v.at[1], m.kd_oth), (m.vd_v.at[1], m.vd_oth),
        (m.qraw_v, m.qraw_oth), (m.kraw_v, m.kraw_oth),
    ):
        store(src, dst)
    wo_copy.wait_recv()
    wo_core.start()
    wo_x[0].start()

    def place(block):
        return pl.ds(pl.multiple_of(lax.rem(block + t * (nb // 2), nb) * BLOCK, BLOCK), BLOCK)

    def attention_phase(kx0, kx1, vx0, vx1, acc):
        both = lane_of((2 * rows, PAIR)) < 64
        one = jnp.ones((2 * rows, PAIR), F32)
        low = lane_of((rows, PAIR)) < 64
        zero = jnp.zeros((rows, PAIR), BF16)
        kx0[:, PAIR:] = m.segk[...]
        kx1[:, PAIR:] = m.segk[...]
        vx0[:, PAIR:] = jnp.where(both, one, 0.0).astype(BF16)
        vx1[:, PAIR:] = jnp.where(both, 0.0, one).astype(BF16)

        def half(which, carry):
            part = 1 - which
            first = lax.rem(part + t, 2) * (nb // 2)

            def group(g, carry):
                lanes = pl.ds(pl.multiple_of(g * PAIR, PAIR), PAIR)
                for i in range(2):
                    at = pl.ds(i * rows, rows)
                    k, v = m.kd_v[i, :, lanes], m.vd_v[i, :, lanes]
                    kx0[at, :PAIR] = jnp.where(low, k, zero)
                    kx1[at, :PAIR] = jnp.where(low, zero, k)
                    vx0[at, :PAIR] = jnp.where(low, v, zero)
                    vx1[at, :PAIR] = jnp.where(low, zero, v)

                def q_block(i, c):
                    at = pl.ds(pl.multiple_of(i * BLOCK, BLOCK), BLOCK)
                    seg_at = pl.ds(pl.multiple_of(part * rows + i * BLOCK, BLOCK), BLOCK)
                    q = jnp.concatenate([m.q_v[part, at, lanes], m.segq[seg_at, :]], axis=1)
                    block = first + i

                    def step(kb, diagonal):
                        here = place(kb)
                        total = None
                        for kx, vx in ((kx0, vx0), (kx1, vx1)):
                            s = dot_nt(q, kx[here, :])
                            if diagonal:
                                r = lax.broadcasted_iota(jnp.int32, s.shape, 0)
                                s = jnp.where(lane_of(s.shape) <= r, s, -1e30)
                            term = dot_nn(jnp.exp2(s).astype(BF16), vx[here, :])
                            total = term if total is None else total + term
                        return total

                    acc[...] = step(block, True)

                    def body(kb, c):
                        acc[...] += step(kb, False)
                        return c

                    lax.fori_loop(jnp.maximum(block - 2, 0), block, body, 0)
                    inverse = 1.0 / acc[:, PAIR:]
                    m.o_v[part, at, lanes] = (acc[:, :PAIR] * inverse).astype(BF16)
                    m.linv_v[part, at, lanes] = inverse
                    return c

                lax.fori_loop(0, rows // BLOCK, q_block, 0)
                return carry

            lax.fori_loop(0, qc // PAIR, group, 0)

            @pl.when(which == 0)
            def _():
                o_copy.start()
                wo_core.wait_recv()
                wo_x[1].start()
                cot_copies[3].start()

            return carry

        lax.fori_loop(0, 2, half, 0)

    pl.run_scoped(
        attention_phase, *[pltpu.VMEM((2 * rows, 2 * PAIR), BF16)] * 4, pltpu.VMEM((BLOCK, 2 * PAIR), F32)
    )
    for src, dst in (
        (m.o_v.at[0], m.o_own), (m.o_v.at[1], m.o_oth), (m.linv_v.at[0], m.linv_own), (m.linv_v.at[1], m.linv_oth)
    ):
        store(src, dst)

    for copy in loads[6:9]:
        copy.wait()
    pack_columns(m.ffn_pack_v, 0, m.attn_v.at[0])
    pack_columns(m.ffn_pack_v, rows, m.attn_v.at[1])
    attn_store = local(12, m.ffn_pack_v, m.attn_pack)
    attn_store.start()
    for copy in wo_x:
        copy.wait_recv()
    o_copy.wait_recv()
    for i, at in enumerate(halves):
        resid = (
            m.tok_v[0, at, :].astype(F32) + dot_nn(m.o_v[0, at, :], m.wom_v[...]) + dot_nn(m.theirs[at, :], m.wot_v[...])
        )
        m.resid_v[at, :] = resid
        m.ffn_v[0, at, :] = (resid * row_norm(resid) * m.gain2[...]).astype(BF16)
        ffn_copies[i].start()

    for copy in loads[9:]:
        copy.wait()
    n_tiles = hidden // CHUNK

    def h_copy(slot, part, at, f):
        cols = pl.ds(pl.multiple_of(f * CHUNK, CHUNK), CHUNK)
        return pltpu.make_async_copy(m.h_v.at[slot], m.h.at[part, :, at, cols], m.h_sem.at[slot])

    def piece(n, carry):
        part = lax.rem((n + 1) // 2, 2)
        at = pl.ds(pl.multiple_of((n // 2) * BLOCK, BLOCK), BLOCK)
        to = pl.ds(pl.multiple_of((2 * part + (1 - part) * (n // 3)) * BLOCK, BLOCK), BLOCK)
        for i in range(2):
            @pl.when(n == 1 + i)
            def _():
                ffn_copies[i].wait_recv()
                for copy in cot_copies[2 * i : 2 * i + 2]:
                    copy.wait_recv()

        def tile(f, c):
            slot = lax.rem(n * n_tiles + f, 2)
            cols = pl.ds(pl.multiple_of(f * CHUNK, CHUNK), CHUNK)
            up_cols = pl.ds(pl.multiple_of(hidden + f * CHUNK, CHUNK), CHUNK)
            x = m.ffn_v[part, at, :]
            gate = dot_nn(x, m.wgu_v[:, cols])
            up = dot_nn(x, m.wgu_v[:, up_cols])
            grad = dot_nt(m.cot_v[part, at, :], m.wd_v[cols, :])

            @pl.when(n * n_tiles + f >= 2)
            def _():
                h_copy(slot, part, at, f).wait()

            sig = 0.5 * jnp.tanh(0.5 * gate) + 0.5
            silu = gate * sig
            mixed = (silu * up).astype(BF16)
            gg = (grad * up * (sig + silu * (1.0 - sig))).astype(BF16)
            gu = (grad * silu).astype(BF16)
            for i, value in enumerate((mixed, gg, gu)):
                m.h_v[slot, i] = value
            h_copy(slot, part, at, f).start()
            y = dot_nn(mixed, m.wd_v[cols, :])
            gf = dot_nt(gg, m.wgu_v[:, cols]) + dot_nt(gu, m.wgu_v[:, up_cols])

            @pl.when(f == 0)
            def _():
                m.y_v[to, :] = y
                m.gf_v[to, :] = gf

            @pl.when(f > 0)
            def _():
                m.y_v[to, :] += y
                m.gf_v[to, :] += gf

            return c

        lax.fori_loop(0, n_tiles, tile, 0)

        @pl.when(n == 0)
        def _():
            pack_columns(m.cot_pack_v, 0, m.cot_v.at[0])
            attn_store.wait()
            pack_columns(m.ffn_pack_v, 0, m.ffn_v.at[0])

        for i in range(2):
            @pl.when(n == 1 + i)
            def _():
                m.gf_send[halves[i], :] = m.gf_v[2 * BLOCK :, :].astype(BF16)
                gf_copies[i].start()
                m.attn_v[1, halves[i], :] = m.y_v[2 * BLOCK :, :].astype(BF16)

        return carry

    lax.fori_loop(0, 4, piece, 0)
    store(m.attn_v.at[1], m.y_send)
    pack_columns(m.cot_pack_v, rows, m.cot_v.at[1])
    pack_columns(m.ffn_pack_v, rows, m.ffn_v.at[1])
    store(m.cot_pack_v, m.cot_pack)
    store(m.ffn_pack_v, m.ffn_pack)

    total = jnp.zeros((1, width), F32)
    for i, at in enumerate(halves):
        gf_copies[i].wait_recv()
        grad = m.gf_v[at, :] + m.gf_in[at, :].astype(F32)
        resid = m.resid_v[at, :]
        inverse = row_norm(resid)
        normed = resid * inverse
        total += jnp.sum(grad * normed, axis=0, keepdims=True)
        w = grad * m.gain2[...]
        gres = m.cot_v[0, at, :].astype(F32) + inverse * (
            w - normed * jnp.mean(w * normed, axis=-1, keepdims=True)
        )
        branch = gres.astype(BF16)
        m.attn_v[0, at, :] = branch
        m.do_v[0, at, :] = dot_nt(branch, m.wom_v[...]).astype(BF16)
        m.do_v[1, at, :] = dot_nt(branch, m.wot_v[...]).astype(BF16)
        m.tok_v[0, at, :] = (m.y_v[at, :] + resid).astype(BF16)
    for src, dst in (
        (m.do_v.at[1], m.do_send), (m.do_v.at[0], m.do_own), (m.attn_v.at[0], m.branch),
        (m.tok_v.at[0], m.base),
    ):
        store(src, dst)
    m.gain_ffn[...] = total
    for copy in (*cot_copies, wo_copy, wo_core, *wo_x, o_copy, *ffn_copies, *gf_copies):
        copy.wait_send()
    for slot in range(2):
        pltpu.make_async_copy(m.h_v.at[slot], m.h.at[0, :, halves[1], pl.ds(0, CHUNK)], m.h_sem.at[slot]).wait()
    for copy in stores:
        copy.wait()


def front(values, tables):
    rows, width = values["tok_own"].shape
    hidden = values["w_down"].shape[0]
    qc = values["w_q"].shape[1]
    seq = 2 * rows
    vm = pltpu.VMEM
    dma = pltpu.SemaphoreType.DMA
    scratch = dict(
        tok_v=vm((2, rows, width), BF16), cot_v=vm((2, rows, width), BF16),
        wq_v=vm((width, qc), BF16), wkv_v=vm((width, qc), BF16), wom_v=vm((qc, width), BF16), wot_v=vm((qc, width), BF16),
        wgu_v=vm((width, 2 * hidden), BF16), wd_v=vm((hidden, width), BF16),
        q_v=vm((2, rows, qc), BF16), kd_v=vm((2, rows, qc), BF16), vd_v=vm((2, rows, qc), BF16),
        attn_v=vm((2, rows, width), BF16), qraw_v=vm((rows, qc), BF16), kraw_v=vm((rows, qc // 2), BF16),
        o_v=vm((2, rows, qc), BF16), linv_v=vm((2, rows, qc), F32), theirs=vm((rows, qc), BF16),
        resid_v=vm((rows, width), F32), ffn_v=vm((2, rows, width), BF16),
        h_v=vm((2, 3, BLOCK, CHUNK), BF16), y_v=vm((3 * BLOCK, width), F32), gf_v=vm((3 * BLOCK, width), F32),
        gf_send=vm((rows, width), BF16), gf_in=vm((rows, width), BF16),
        cot_pack_v=vm((2, seq, width // 2), BF16),
        ffn_pack_v=vm((2, seq, width // 2), BF16), do_v=vm((2, rows, qc), BF16),
        r_send=dma((13,)), r_recv=dma((13,)), l_sem=dma((13,)), o_sem=dma((20,)), h_sem=dma((2,)),
    )
    anywhere = pl.BlockSpec(memory_space=pl.ANY)
    vmem = pl.BlockSpec(memory_space=pltpu.VMEM)
    low, full = (lambda *shape: jax.ShapeDtypeStruct(shape, BF16)), (lambda *shape: jax.ShapeDtypeStruct(shape, F32))
    shapes = dict(
        q_oth=low(rows, qc), kd_oth=low(rows, qc), vd_oth=low(rows, qc),
        qraw_oth=low(rows, qc), kraw_oth=low(rows, qc // 2), o_own=low(rows, qc), o_oth=low(rows, qc),
        linv_own=full(rows, qc), linv_oth=full(rows, qc),
        cot_pack=low(2, seq, width // 2), ffn_pack=low(2, seq, width // 2), attn_pack=low(2, seq, width // 2),
        h=low(2, 3, rows, hidden), base=low(rows, width), y_send=low(rows, width),
        branch=low(rows, width), do_own=low(rows, qc), do_send=low(rows, qc),
        gain_ffn=full(1, width),
    )
    outs = pl.pallas_call(
        functools.partial(front_kernel, tuple(scratch)),
        in_specs=[anywhere] * len(FRONT_INPUTS) + [vmem] * len(FRONT_TABLES),
        out_specs=[anywhere] * (len(FRONT_OUTPUTS) - 1) + [vmem],
        out_shape=[shapes[k] for k in FRONT_OUTPUTS],
        scratch_shapes=list(scratch.values()),
        compiler_params=pltpu.CompilerParams(
            vmem_limit_bytes=BACK_VMEM, collective_id=1, has_side_effects=True
        ),
        cost_estimate=cost(100e-6),
        name="front",
    )(*[values[k] for k in FRONT_INPUTS], *[tables[k] for k in FRONT_TABLES])
    return dict(zip(FRONT_OUTPUTS, outs))


def finish_kernel(
    base_ref, yr_ref, ga_ref, gr_ref, x_ref, gres_ref, gain_ref, shards_ref, gains_ref,
    out_ref, gt_ref, q_ref, kv_ref, o_ref, g1_ref, g2_ref, gq_ref, gk_ref, gu_ref, down_ref,
):
    out_ref[...] = (base_ref[...].astype(F32) + yr_ref[...].astype(F32)).astype(BF16)
    x = x_ref[...].astype(F32)
    inverse = row_norm(x)
    normed = x * inverse
    w = (ga_ref[...].astype(F32) + gr_ref[...].astype(F32)) * gain_ref[...]
    gt_ref[...] = gres_ref[...].astype(F32) + inverse * (w - normed * jnp.mean(w * normed, axis=-1, keepdims=True))
    n_chunks = shards_ref.shape[0]
    per_x = (n_chunks - 2) // 3
    two = 2 * PAIR
    step = pl.program_id(0)

    @pl.when(step < per_x)
    def _():
        down_ref[...] = shards_ref[step]
        gu_ref[:, 0, :] = shards_ref[per_x + step]
        gu_ref[:, 1, :] = shards_ref[2 * per_x + step]

    @pl.when(step == per_x)
    def _():
        n = g1_ref.shape[0]
        g1_ref[...] = gains_ref[:n, :]
        g2_ref[...] = gains_ref[n : 2 * n, :]
        for i, ref in enumerate((gq_ref, gk_ref)):
            row = gains_ref[2 * n + i : 2 * n + i + 1, :]
            ref[...] = row[:, :64] + row[:, 64:]
        for p in range(2):
            shard = shards_ref[3 * per_x + p]
            q_ref[:, p * two : (p + 1) * two] = shard[:, :two]
            kv_ref[:, 0, p * PAIR : (p + 1) * PAIR] = shard[:, two : two + PAIR]
            kv_ref[:, 1, p * PAIR : (p + 1) * PAIR] = shard[:, two + PAIR : 2 * two]
            o_ref[:, p * two : (p + 1) * two] = shard[:, 2 * two :]


def finish(base, y_recv, ga_own, ga_recv, x, gres, gain, shards, gains):
    rows, width = x.shape
    n_chunks, block, _ = shards.shape
    hidden = (n_chunks - 2) // 3 * CHUNK
    per_x = hidden // CHUNK
    row = pl.BlockSpec((rows // (per_x + 1), width), lambda i: (i, 0))
    fixed = lambda shape: pl.BlockSpec(shape, lambda i: (0,) * len(shape))
    m = width // PAIR
    shapes = [(block, SPLIT), (block, 2, SPLIT // 2), (block, SPLIT), (m, PAIR), (m, PAIR), (1, 64), (1, 64)]
    shapes += [(block, 2, hidden), (block, hidden)]
    piece = lambda i: jnp.minimum(i, per_x - 1)
    return pl.pallas_call(
        finish_kernel,
        grid=(per_x + 1,),
        in_specs=[row] * 6 + [fixed((1, width)), fixed(shards.shape), fixed(gains.shape)],
        out_specs=[row, row]
        + [fixed(shape) for shape in shapes[:7]]
        + [
            pl.BlockSpec((block, 2, CHUNK), lambda i: (0, 0, piece(i))),
            pl.BlockSpec((block, CHUNK), lambda i: (0, piece(i))),
        ],
        out_shape=[jax.ShapeDtypeStruct((rows, width), BF16), jax.ShapeDtypeStruct((rows, width), F32)]
        + [jax.ShapeDtypeStruct(shape, F32) for shape in shapes],
        compiler_params=pltpu.CompilerParams(vmem_limit_bytes=VMEM_LIMIT),
        cost_estimate=cost(6e-6),
        name="finish",
    )(base, y_recv, ga_own, ga_recv, x, gres, gain, shards, gains)


def swap(value, axis, size, bit):
    return lax.ppermute(value, axis, [(i, i ^ bit) for i in range(size)])


def after(value, *others):
    return lax.optimization_barrier((value,) + others)[0]


def paired(
    n_dp, tokens, doc_ids, gain_attn, w_q, w_kv, q_gain, k_gain, w_o, gain_ffn, w_gu, w_down, cotangent
):
    rows, width = tokens.shape
    head_dim = q_gain.shape[0]
    hidden = w_down.shape[0]
    seq = doc_ids.shape[1]
    t = lax.axis_index("tensor")
    over = functools.partial(swap, axis="tensor", size=2, bit=1)

    tokens_oth = over(tokens)

    segment = doc_ids[0]
    segment = jnp.where(t == 0, segment, jnp.roll(segment, rows))
    lanes = jnp.arange(PAIR, dtype=jnp.int32)[None, :]
    match = lanes == segment[:, None]
    marker = lanes == 8
    segk = (match | marker).astype(BF16)
    segq = (jnp.where(match, SAME, 0.0) - jnp.where(marker, SAME, 0.0)).astype(BF16)
    half_dim = head_dim // 2
    frequency = jnp.exp(-math.log(THETA) * 2.0 * jnp.arange(half_dim, dtype=F32) / head_dim)
    position = (jnp.arange(seq, dtype=jnp.int32) + t * rows) % seq
    angles = position.astype(F32)[:, None] * frequency[None, :]
    cos, sin = jnp.cos(angles), jnp.sin(angles)
    cosine = jnp.concatenate([cos] * 4, axis=1)
    sine = jnp.concatenate([-sin, sin] * 2, axis=1)
    gain1, gain2 = gain_attn.reshape(1, width), gain_ffn.reshape(1, width)
    qg = jnp.concatenate([q_gain, q_gain]).reshape(1, PAIR)
    kg = jnp.concatenate([k_gain, k_gain]).reshape(1, PAIR)
    w_kv = w_kv.reshape(width, -1)
    w_gu = w_gu.reshape(width, 2 * hidden)
    tables = dict(segq=segq, segk=segk, cos=cosine, sin=sine, gain1=gain1, gain2=gain2, qg=qg, kg=kg)

    attn_own, q_own, kd_own, vd_own, qraw_own, kraw_own = qkv(
        tokens, gain1, w_q, w_kv, qg, kg, cosine, sine, 0
    )
    values = dict(
        tok_own=tokens, tok_oth=tokens_oth, cot_own=cotangent, w_q=w_q, w_kv=w_kv, w_o=w_o, w_gu=w_gu, w_down=w_down,
        attn_own=attn_own, q_own=q_own, kd_own=kd_own, vd_own=vd_own, qraw_own=qraw_own, kraw_own=kraw_own,
    )
    values.update(front(values, tables))
    tables.update(gain_ffn=values["gain_ffn"])
    ga_own, ga_recv, shards, gains, y_recv = back(n_dp, values, tables)
    output, grad_tokens, grad_q, grad_kv, grad_o, sum_1, sum_2, sum_q, sum_k, grad_gu, grad_down = finish(
        values["base"], y_recv, ga_own, ga_recv, tokens, values["branch"], gain1, shards, gains
    )
    return (
        output,
        grad_tokens,
        sum_1.reshape(width),
        grad_q,
        grad_kv,
        sum_q.reshape(head_dim),
        sum_k.reshape(head_dim),
        grad_o.T,
        sum_2.reshape(width),
        grad_gu,
        grad_down.T,
    )


def normalize(values):
    inverse = lax.rsqrt(jnp.mean(values * values, axis=-1, keepdims=True) + EPS)
    return (values * inverse, inverse)


def norm_back(grad_normed, normed, inverse):
    return inverse * (grad_normed - normed * jnp.mean(grad_normed * normed, axis=-1, keepdims=True))


def rotate(values, cosine_table, sine_table):
    half_dim = values.shape[-1] // 2
    first_half = values[..., :half_dim]
    second_half = values[..., half_dim:]
    return jnp.concatenate(
        [
            first_half * cosine_table - second_half * sine_table,
            second_half * cosine_table + first_half * sine_table,
        ],
        -1,
    )


def shards(
    tokens, doc_ids, gain_attn, w_q, w_kv, q_gain, k_gain, w_o, gain_ffn, w_gu, w_down, cotangent
):
    f32 = jnp.float32
    bf16 = jnp.bfloat16
    rows_dev, model_width = tokens.shape
    head_dim = q_gain.shape[0]
    q_cols = w_q.shape[1]
    q_heads = q_cols // head_dim
    kv_cols = w_kv.shape[2]
    kv_heads = kv_cols // head_dim
    group_size = q_heads // kv_heads
    hidden = w_gu.shape[2]
    seq_len = doc_ids.shape[1]
    segment = doc_ids[0]
    block_rows = min(512, seq_len)
    blocks = seq_len // block_rows
    score_scale = head_dim ** (-0.5)
    w_kv_flat = w_kv.reshape(model_width, 2 * kv_cols)
    w_gu_flat = w_gu.reshape(model_width, 2 * hidden)
    half_dim = head_dim // 2
    frequency = jnp.exp(-math.log(THETA) * 2.0 * jnp.arange(half_dim, dtype=f32) / head_dim)
    angles = jnp.arange(seq_len, dtype=f32)[:, None] * frequency[None, :]
    cosine_table = jnp.cos(angles)[:, None, :]
    sine_table = jnp.sin(angles)[:, None, :]
    key_pos = jnp.arange(seq_len, dtype=jnp.int32)
    x_float = tokens.astype(f32)
    normed1, inverse1 = normalize(x_float)
    attn_in = (normed1 * gain_attn).astype(bf16)
    attn_all = lax.all_gather(attn_in, "tensor", axis=0, tiled=True)
    q_raw = jnp.dot(attn_all, w_q, preferred_element_type=f32).reshape(seq_len, q_heads, head_dim)
    kv_raw = jnp.dot(attn_all, w_kv_flat, preferred_element_type=f32).reshape(
        seq_len, 2, kv_heads, head_dim
    )
    q_normed, q_inverse = normalize(q_raw)
    k_normed, k_inverse = normalize(kv_raw[:, 0])
    queries = rotate(q_normed * q_gain, cosine_table, sine_table).astype(bf16)
    queries = queries.reshape(seq_len, kv_heads, group_size, head_dim)
    keys = rotate(k_normed * k_gain, cosine_table, sine_table).astype(bf16)
    values_low = kv_raw[:, 1].astype(bf16)

    def scores_of(first_row):
        q_block = lax.dynamic_slice_in_dim(queries, first_row, block_rows, 0)
        seg_block = lax.dynamic_slice_in_dim(segment, first_row, block_rows, 0)
        raw_scores = (
            jnp.einsum("qhgd,thd->hgqt", q_block, keys, preferred_element_type=f32) * score_scale
        )
        query_pos = first_row + jnp.arange(block_rows, dtype=jnp.int32)
        allowed = (key_pos[None, :] <= query_pos[:, None]) & (
            seg_block[:, None] == segment[None, :]
        )
        return (jnp.where(allowed, raw_scores, -1e30), q_block)

    def attend(first_row):
        masked, q_block = scores_of(first_row)
        row_max = jnp.max(masked, axis=-1, keepdims=True)
        exponent = jnp.exp(masked - row_max)
        denominator = jnp.sum(exponent, axis=-1, keepdims=True)
        probs = (exponent / denominator).astype(bf16)
        attended_block = jnp.einsum("hgqt,thd->qhgd", probs, values_low, preferred_element_type=f32)
        return (attended_block, (row_max + jnp.log(denominator))[..., 0])

    starts = jnp.arange(blocks, dtype=jnp.int32) * block_rows
    attended, log_sums = lax.map(attend, starts)
    attended_low = attended.reshape(seq_len, q_cols).astype(bf16)
    resid = x_float + lax.psum_scatter(
        jnp.dot(attended_low, w_o, preferred_element_type=f32),
        "tensor",
        scatter_dimension=0,
        tiled=True,
    )
    normed2, inverse2 = normalize(resid)
    ffn_in = (normed2 * gain_ffn).astype(bf16)
    ffn_all = lax.all_gather(ffn_in, "tensor", axis=0, tiled=True)
    gate_up = jnp.dot(ffn_all, w_gu_flat, preferred_element_type=f32)
    gate_part = gate_up[:, :hidden]
    up_part = gate_up[:, hidden:]
    sigmoid_gate = jax.nn.sigmoid(gate_part)
    silu_gate = gate_part * sigmoid_gate
    mixed = (silu_gate * up_part).astype(bf16)
    result = resid + lax.psum_scatter(
        jnp.dot(mixed, w_down, preferred_element_type=f32).astype(jnp.bfloat16),
        "tensor",
        scatter_dimension=0,
        tiled=True,
    ).astype(jnp.float32)
    output = result.astype(bf16)
    grad_all = lax.all_gather(cotangent, "tensor", axis=0, tiled=True)
    grad_down = jnp.einsum("sf,sd->fd", mixed, grad_all, preferred_element_type=f32)
    grad_mixed = jnp.einsum("sd,fd->sf", grad_all, w_down, preferred_element_type=f32)
    grad_gate = grad_mixed * up_part * sigmoid_gate * (1.0 + gate_part * (1.0 - sigmoid_gate))
    grad_up = grad_mixed * silu_gate
    grad_gu = jnp.concatenate([grad_gate, grad_up], 1).astype(bf16)
    grad_w_gu = jnp.einsum("sd,sf->df", ffn_all, grad_gu, preferred_element_type=f32).reshape(
        model_width, 2, hidden
    )
    grad_ffn_in = lax.psum_scatter(
        jnp.einsum("sf,df->sd", grad_gu, w_gu_flat, preferred_element_type=f32).astype(
            jnp.bfloat16
        ),
        "tensor",
        scatter_dimension=0,
        tiled=True,
    ).astype(jnp.float32)
    gain_ffn_part = jnp.sum(grad_ffn_in * normed2, axis=0)
    grad_resid = cotangent.astype(f32) + norm_back(grad_ffn_in * gain_ffn, normed2, inverse2)
    branch_all = lax.all_gather(grad_resid.astype(bf16), "tensor", axis=0, tiled=True)
    grad_w_o = jnp.einsum("sc,sd->cd", attended_low, branch_all, preferred_element_type=f32)
    grad_attended = jnp.einsum("sd,cd->sc", branch_all, w_o, preferred_element_type=f32).astype(
        bf16
    )
    grad_attended = grad_attended.reshape(seq_len, kv_heads, group_size, head_dim)

    def attend_back(carried, scanned):
        first_row, lse_block = scanned
        masked, q_block = scores_of(first_row)
        probs = jnp.exp(masked - lse_block[..., None])
        go_block = lax.dynamic_slice_in_dim(grad_attended, first_row, block_rows, 0)
        grad_probs = jnp.einsum("qhgd,thd->hgqt", go_block, values_low, preferred_element_type=f32)
        grad_scores = (
            probs * (grad_probs - jnp.sum(probs * grad_probs, axis=-1, keepdims=True))
        ).astype(bf16)
        keys_next = carried[0] + score_scale * jnp.einsum(
            "hgqt,qhgd->thd", grad_scores, q_block, preferred_element_type=f32
        )
        values_next = carried[1] + jnp.einsum(
            "hgqt,qhgd->thd", probs.astype(bf16), go_block, preferred_element_type=f32
        )
        grad_q_block = score_scale * jnp.einsum(
            "hgqt,thd->qhgd", grad_scores, keys, preferred_element_type=f32
        )
        return ((keys_next, values_next), grad_q_block)

    zero_kv = jnp.zeros((seq_len, kv_heads, head_dim), f32)
    (grad_keys, grad_values), grad_queries = lax.scan(
        attend_back, (zero_kv, zero_kv), (starts, log_sums)
    )
    grad_q_normed = rotate(
        grad_queries.reshape(seq_len, q_heads, head_dim), cosine_table, -sine_table
    )
    q_gain_part = jnp.sum(grad_q_normed * q_normed, axis=(0, 1))
    grad_q_raw = (
        norm_back(grad_q_normed * q_gain, q_normed, q_inverse).astype(bf16).reshape(seq_len, q_cols)
    )
    grad_k_normed = rotate(grad_keys, cosine_table, -sine_table)
    k_gain_part = jnp.sum(grad_k_normed * k_normed, axis=(0, 1))
    grad_k_raw = (
        norm_back(grad_k_normed * k_gain, k_normed, k_inverse)
        .astype(bf16)
        .reshape(seq_len, kv_cols)
    )
    grad_kv = jnp.concatenate([grad_k_raw, grad_values.astype(bf16).reshape(seq_len, kv_cols)], 1)
    grad_w_q = jnp.einsum("sd,sc->dc", attn_all, grad_q_raw, preferred_element_type=f32)
    grad_w_kv = jnp.einsum("sd,sc->dc", attn_all, grad_kv, preferred_element_type=f32).reshape(
        model_width, 2, kv_cols
    )
    grad_attn_in = lax.psum_scatter(
        (
            jnp.einsum("sc,dc->sd", grad_q_raw, w_q, preferred_element_type=f32)
            + jnp.einsum("sc,dc->sd", grad_kv, w_kv_flat, preferred_element_type=f32)
        ).astype(jnp.bfloat16),
        "tensor",
        scatter_dimension=0,
        tiled=True,
    ).astype(jnp.float32)
    gain_attn_part = jnp.sum(grad_attn_in * normed1, axis=0)
    grad_tokens = grad_resid + norm_back(grad_attn_in * gain_attn, normed1, inverse1)
    gain_sums = lax.psum(
        (gain_attn_part, gain_ffn_part, q_gain_part, k_gain_part), ("dp", "tensor")
    )
    shard_q, shard_kv, shard_o, shard_gu, shard_down = (
        lax.psum_scatter(
            grad_w_q.astype(jnp.bfloat16), "dp", scatter_dimension=0, tiled=True
        ).astype(jnp.float32),
        lax.psum_scatter(
            grad_w_kv.astype(jnp.bfloat16), "dp", scatter_dimension=0, tiled=True
        ).astype(jnp.float32),
        lax.psum_scatter(
            grad_w_o.astype(jnp.bfloat16), "dp", scatter_dimension=1, tiled=True
        ).astype(jnp.float32),
        lax.psum_scatter(
            grad_w_gu.astype(jnp.bfloat16), "dp", scatter_dimension=0, tiled=True
        ).astype(jnp.float32),
        lax.psum_scatter(
            grad_down.astype(jnp.bfloat16), "dp", scatter_dimension=1, tiled=True
        ).astype(jnp.float32),
    )
    return (
        output,
        grad_tokens,
        gain_sums[0],
        shard_q,
        shard_kv,
        gain_sums[2],
        gain_sums[3],
        shard_o,
        gain_sums[1],
        shard_gu,
        shard_down,
    )


def solution(mesh):
    in_specs = (
        P(("dp", "tensor"), None),
        P("dp", None),
        P(),
        P(None, "tensor"),
        P(None, None, "tensor"),
        P(),
        P(),
        P("tensor", None),
        P(),
        P(None, None, "tensor"),
        P("tensor", None),
        P(("dp", "tensor"), None),
    )
    out_specs = (
        P(("dp", "tensor"), None),
        P(("dp", "tensor"), None),
        P(),
        P("dp", "tensor"),
        P("dp", None, "tensor"),
        P(),
        P(),
        P("tensor", "dp"),
        P(),
        P("dp", None, "tensor"),
        P("tensor", "dp"),
    )
    paired_axes = mesh.shape["tensor"] == 2 and mesh.shape["dp"] == 16
    body = functools.partial(paired, mesh.shape["dp"]) if paired_axes else shards
    return jax.shard_map(body, mesh=mesh, in_specs=in_specs, out_specs=out_specs, check_vma=False)
```

```python
import functools
import math

import jax
import jax.numpy as jnp
from jax import lax
from jax.experimental import pallas as pl
from jax.experimental.pallas import tpu as pltpu
from jax.sharding import PartitionSpec as P

EPS = 1e-06
THETA = 1000000.0
LOG2E = 1.4426950408889634
LN2 = 0.6931471805599453
BLOCK = 256
PAIR = 128
SAME = 256.0
F32 = jnp.float32
BF16 = jnp.bfloat16
COST_RATE = 1.0e13
VMEM_LIMIT = 56 * 1024 * 1024
BACK_VMEM = 61 * 1024 * 1024


def dot_nn(a, b):
    return lax.dot_general(a, b, (((1,), (0,)), ((), ())), preferred_element_type=F32)


def dot_nt(a, b):
    return lax.dot_general(a, b, (((1,), (1,)), ((), ())), preferred_element_type=F32)


def cost(seconds):
    return pl.CostEstimate(flops=int(seconds * COST_RATE), bytes_accessed=0, transcendentals=0)


def lane_of(shape):
    return lax.broadcasted_iota(jnp.int32, shape, len(shape) - 1)


def head_mean(values):
    high = values.astype(BF16)
    low = (values - high.astype(F32)).astype(BF16)
    row = lax.broadcasted_iota(jnp.int32, (PAIR, PAIR), 0) // 64
    col = lax.broadcasted_iota(jnp.int32, (PAIR, PAIR), 1) // 64
    mean = jnp.where(row == col, 1.0 / 64.0, 0.0).astype(BF16)
    return dot_nn(high, mean) + dot_nn(low, mean)


def swap_halves(values):
    first = lane_of(values.shape) % 64 < 32
    return jnp.where(first, pltpu.roll(values, 96, 1), pltpu.roll(values, 32, 1))


def rope(values, cosine, sine):
    return values * cosine + swap_halves(values) * sine


def row_norm(x):
    return lax.rsqrt(jnp.mean(x * x, axis=-1, keepdims=True) + EPS)


def qkv_kernel(
    x_ref, gain_ref, wq_ref, wk_ref, wv_ref, qg_ref, kg_ref, cos_ref, sin_ref,
    attn_ref, q_ref, kd_ref, vd_ref, qraw_ref, kraw_ref,
):
    x = x_ref[...].astype(F32)
    attn = (x * row_norm(x) * gain_ref[...]).astype(BF16)
    attn_ref[...] = attn
    q = dot_nn(attn, wq_ref[...])
    k = dot_nn(attn, wk_ref[...])
    v = dot_nn(attn, wv_ref[...])
    qraw_ref[...] = q.astype(BF16)
    kraw_ref[...] = k.astype(BF16)
    cosine, sine = cos_ref[...], sin_ref[...]
    for g in range(q.shape[1] // PAIR):
        at = slice(g * PAIR, (g + 1) * PAIR)
        u = q[:, at]
        n = u * lax.rsqrt(head_mean(u * u) + EPS)
        q_ref[:, at] = (rope(n * qg_ref[...], cosine, sine) * (LOG2E / 8.0)).astype(BF16)
    low = lane_of((x.shape[0], PAIR)) < 64
    for p in range(k.shape[1] // PAIR):
        at = slice(p * PAIR, (p + 1) * PAIR)
        u = k[:, at]
        n = u * lax.rsqrt(head_mean(u * u) + EPS)
        roped = rope(n * kg_ref[...], cosine, sine)
        for src, dst in ((roped, kd_ref), (v[:, at], vd_ref)):
            turned = pltpu.roll(src, 64, 1)
            dst[:, 2 * p * PAIR : (2 * p + 1) * PAIR] = jnp.where(low, src, turned).astype(BF16)
            dst[:, (2 * p + 1) * PAIR : (2 * p + 2) * PAIR] = jnp.where(low, turned, src).astype(BF16)


def qkv(x, gain, w_q, w_kv, qg, kg, cosine, sine, half):
    rows, width = x.shape
    qc, kc = w_q.shape[1], w_kv.shape[1] // 2
    nb = rows // BLOCK
    whole = lambda shape, *at: pl.BlockSpec(shape, lambda i: at)
    row = lambda cols: pl.BlockSpec((BLOCK, cols), lambda i: (i, 0))
    table = pl.BlockSpec((BLOCK, PAIR), lambda i: (i + half * nb, 0))
    return pl.pallas_call(
        qkv_kernel,
        grid=(nb,),
        in_specs=[
            row(width), whole((1, width), 0, 0), whole((width, qc), 0, 0),
            whole((width, kc), 0, 0), whole((width, kc), 0, 1),
            whole((1, PAIR), 0, 0), whole((1, PAIR), 0, 0), table, table,
        ],
        out_specs=[row(width), row(qc), row(2 * kc), row(2 * kc), row(qc), row(kc)],
        out_shape=[
            jax.ShapeDtypeStruct((rows, c), BF16) for c in (width, qc, 2 * kc, 2 * kc, qc, kc)
        ],
        compiler_params=pltpu.CompilerParams(vmem_limit_bytes=VMEM_LIMIT),
        cost_estimate=cost(5e-6),
        name="qkv",
    )(x, gain, w_q, w_kv, w_kv, qg, kg, cosine, sine)


MESH = pl.DeviceIdType.MESH
CHUNK = 768
SPLIT = 512
DEPTH = 2


def dot_tn(a, b):
    return lax.dot_general(a, b, (((0,), (0,)), ((), ())), preferred_element_type=F32)


def pack_columns(dst, first, ref):
    rows, width = ref.shape
    low = lane_of((rows, PAIR)) < 64
    for k in range(width // (2 * PAIR)):
        a = ref[:, 2 * k * PAIR : (2 * k + 1) * PAIR].astype(F32)
        b = ref[:, (2 * k + 1) * PAIR : (2 * k + 2) * PAIR].astype(F32)
        lanes = slice(k * PAIR, (k + 1) * PAIR)
        dst[0, first : first + rows, lanes] = jnp.where(low, a, pltpu.roll(b, 64, 1)).astype(BF16)
        dst[1, first : first + rows, lanes] = jnp.where(low, pltpu.roll(a, 64, 1), b).astype(BF16)


BACK_INPUTS = (
    "h", "cot_pack", "ffn_pack", "attn_pack", "tok_own", "tok_oth", "y_send", "branch", "do_own", "do_send",
    "w_q", "w_kv", "q_own", "q_oth", "kd_own", "kd_oth", "vd_own", "vd_oth", "o_own", "o_oth", "linv_own", "linv_oth",
    "qraw_own", "qraw_oth", "kraw_own", "kraw_oth",
)
BACK_TABLES = ("segq", "segk", "cos", "sin", "gain_ffn", "qg", "kg")
BACK_OUTPUTS = ("ga_out", "ga_recv", "shards", "gains", "y_recv")


class Names:
    def __init__(self, names, refs):
        self.__dict__.update(zip(names, refs))


def back_kernel(n_dp, scratch_names, *refs):
    m = Names(BACK_INPUTS + BACK_TABLES + BACK_OUTPUTS + scratch_names, refs)
    rows, width = m.tok_own.shape
    hidden = m.h.shape[3]
    per_x = hidden // CHUNK
    n_wide = 3 * per_x
    n_chunks = n_wide + 2
    nb = 2 * rows // BLOCK
    t = lax.axis_index("tensor")
    d = lax.axis_index("dp")
    core = lax.rem(d, 2)
    x = lax.rem(d // 2, 2)
    zl = lax.rem(d // 4, 2)
    zh = d // 8
    over_t = {"tensor": 1 - t}
    over_core = {"dp": d + 1 - 2 * core}
    over_x = {"dp": d + 2 - 4 * x}
    over_zl = {"dp": d + 4 - 8 * zl}
    over_zh = {"dp": d + 8 - 16 * zh}
    partners = (over_t, over_core, over_x, over_zl, over_zh)
    low = lane_of((rows, PAIR)) < 64
    own_rows, oth_rows = pl.ds(0, rows), pl.ds(rows, rows)

    barrier = pltpu.get_barrier_semaphore()
    for p in partners:
        pl.semaphore_signal(barrier, inc=1, device_id=p, device_id_type=MESH)
    pl.semaphore_wait(barrier, len(partners))

    def tensor_copy(i, src, dst):
        return pltpu.make_async_remote_copy(
            src_ref=src, dst_ref=dst, send_sem=m.t_send.at[i], recv_sem=m.t_recv.at[i],
            device_id=over_t, device_id_type=MESH,
        )

    do_copy = tensor_copy(1, m.do_send, m.do_recv)
    branch_copy = tensor_copy(2, m.branch_v, m.branch_recv)
    y_copy = tensor_copy(3, m.y_send, m.y_recv)
    ga_copy = tensor_copy(4, m.branch_v, m.ga_recv)

    def rs_copy(stage, c, src, dst, device):
        return pltpu.make_async_remote_copy(
            src_ref=src, dst_ref=dst, send_sem=m.rs_send.at[stage, c], recv_sem=m.rs_recv.at[stage, c],
            device_id=device, device_id_type=MESH,
        )

    left, right = pl.ds(0, SPLIT), pl.ds(SPLIT, CHUNK - SPLIT)
    every = pl.ds(0, 2)
    block_rows = m.sums.shape[4]
    full_rows = pl.ds(0, block_rows)

    def core_copy(c):
        return rs_copy(0, c, m.core_send.at[lax.rem(c, 2)], m.sums.at[c], over_core)

    def first_copies(c):
        return (
            rs_copy(1, c, m.sums.at[c, every, every, 1 - x, full_rows, left], m.r1a.at[c], over_x),
            rs_copy(2, c, m.sums.at[c, every, 1 - zl, every, full_rows, right], m.r1b.at[c], over_zl),
        )

    def second_copies(c):
        return (
            rs_copy(3, c, m.sums.at[c, every, 1 - zl, x, full_rows, left], m.r2a.at[c], over_zl),
            rs_copy(4, c, m.sums.at[c, every, zl, 1 - x, full_rows, right], m.r2b.at[c], over_x),
        )

    def third_copy(c):
        return rs_copy(5, c, m.sums.at[c, 1 - zh, zl, x], m.r3.at[c], over_zh)

    def local(i, src, dst):
        return pltpu.make_async_copy(src, dst, m.l_sem.at[i])

    def both(i, src_own, src_oth, dst):
        return (local(i, src_own, dst.at[own_rows]), local(i + 1, src_oth, dst.at[oth_rows]))

    def start(copies):
        for copy in copies:
            copy.start()

    def wait(copies):
        for copy in copies:
            copy.wait()

    def add_core(c):
        core_copy(c).wait_recv()
        for a in range(2):
            for b in range(2):
                for e in range(2):
                    m.sums[c, a, b, e] = (
                        m.sums[c, a, b, e].astype(F32) + m.kept[lax.rem(c, 2), a, b, e].astype(F32)
                    ).astype(BF16)

    def total_copy(c):
        slot = lax.rem(c, 2)
        return pltpu.make_async_copy(m.totals.at[slot], m.shards.at[c], m.s_sem.at[slot])

    def tick(i):
        @pl.when(i < n_chunks)
        def _():
            a_copy, b_copy = first_copies(i)
            a_copy.wait_recv()
            b_copy.wait_recv()
            for a in range(2):
                for b in range(2):
                    m.sums[i, a, b, x, :, :SPLIT] = (
                        m.sums[i, a, b, x, :, :SPLIT].astype(F32) + m.r1a[i, a, b].astype(F32)
                    ).astype(BF16)
                    m.sums[i, a, zl, b, :, SPLIT:] = (
                        m.sums[i, a, zl, b, :, SPLIT:].astype(F32) + m.r1b[i, a, b].astype(F32)
                    ).astype(BF16)
            start(second_copies(i))

        @pl.when(i + DEPTH < n_chunks - 1)
        def _():
            start(first_copies(i + DEPTH))

        @pl.when((i >= 1) & (i < n_chunks + 1))
        def _():
            c = i - 1
            a_copy, b_copy = second_copies(c)
            a_copy.wait_recv()
            b_copy.wait_recv()
            for a in range(2):
                m.sums[c, a, zl, x, :, :SPLIT] = (
                    m.sums[c, a, zl, x, :, :SPLIT].astype(F32) + m.r2a[c, a].astype(F32)
                ).astype(BF16)
                m.sums[c, a, zl, x, :, SPLIT:] = (
                    m.sums[c, a, zl, x, :, SPLIT:].astype(F32) + m.r2b[c, a].astype(F32)
                ).astype(BF16)
            third_copy(c).start()

        @pl.when((i >= 2) & (i < n_chunks + 2))
        def _():
            c = i - 2
            third_copy(c).wait_recv()

            @pl.when(c >= 2)
            def _():
                total_copy(c - 2).wait()

            m.totals[lax.rem(c, 2)] = m.sums[c, zh, zl, x].astype(F32) + m.r3[c].astype(F32)
            total_copy(c).start()

    def put(ref, slot, lanes, value):
        for a in range(2):
            for b in range(2):
                for e in range(2):
                    k = ((a * 2 + b) * 2 + e) * block_rows
                    ref[slot, a, b, e, :, lanes] = value[k : k + block_rows].astype(BF16)

    do_copy.start()
    packs = [local(i, src, m.packed.at[i]) for i, src in enumerate((m.cot_pack, m.ffn_pack))]
    attn_load = local(0, m.attn_pack, m.packed.at[0])
    start(packs)
    loads = [
        local(2, m.branch, m.branch_v), local(3, m.do_own, m.do_v), local(7, m.w_q, m.wq_v), local(8, m.w_kv, m.wkv_v),
        *both(9, m.o_own, m.o_oth, m.o_v), *both(11, m.kraw_own, m.kraw_oth, m.kraw_v),
    ]

    def tiles(g):
        slot = lax.rem(g, 2)
        lanes = pl.ds(pl.multiple_of(g * PAIR, PAIR), PAIR)
        out = []
        for j, (own, oth, dst) in enumerate((
            (m.q_own, m.q_oth, m.q_v), (m.kd_own, m.kd_oth, m.kd_v), (m.vd_own, m.vd_oth, m.vd_v),
            (m.qraw_own, m.qraw_oth, m.qraw_v), (m.linv_own, m.linv_oth, m.linv_v),
        )):
            out.append(pltpu.make_async_copy(own.at[:, lanes], dst.at[slot, own_rows], m.g_sem.at[slot, 2 * j]))
            out.append(pltpu.make_async_copy(oth.at[:, lanes], dst.at[slot, oth_rows], m.g_sem.at[slot, 2 * j + 1]))
        return out

    def wide_phase(y_v):
        def fetch(c):
            slot = lax.rem(c, 2)
            cols = pl.ds(pl.multiple_of(lax.rem(c, per_x) * CHUNK, CHUNK), CHUNK)
            return [
                pltpu.make_async_copy(
                    m.h.at[j, c // per_x, :, cols], y_v.at[slot, at], m.h_sem.at[slot, j]
                )
                for j, at in enumerate((own_rows, oth_rows))
            ]

        start(fetch(0))
        start(loads)
        packs[0].wait()
        loads[0].wait()

        def chunk(c, carry):
            slot = lax.rem(c, 2)
            which = jnp.minimum(c // per_x, 1)
            wait(fetch(c))

            @pl.when(c == per_x)
            def _():
                packs[1].wait()
                attn_load.start()

            @pl.when(c + 1 < n_wide)
            def _():
                start(fetch(c + 1))

            @pl.when(c >= 2)
            def _():
                core_copy(c - 2).wait_send()

            put(m.core_send, slot, slice(None), dot_tn(m.packed[which, 1 - core], y_v[slot]))
            core_copy(c).start()
            put(m.kept, slot, slice(None), dot_tn(m.packed[which, core], y_v[slot]))

            @pl.when(c >= 1)
            def _():
                add_core(c - 1)

            @pl.when((c >= 1) & (c <= DEPTH))
            def _():
                start(first_copies(c - 1))

            @pl.when(c == n_wide - 4)
            def _():
                do_copy.wait_recv()
                branch_copy.start()

            @pl.when((c == n_wide - 4) | (c == n_wide - 2))
            def _():
                tick((c - n_wide + 4) // 2)

            return carry

        lax.fori_loop(0, n_wide, chunk, 0)
        add_core(n_wide - 1)
        tick(2)

    pl.run_scoped(wide_phase, pltpu.VMEM((2, 2 * rows, CHUNK), BF16))
    start(tiles(0))

    wait(loads[1:])
    attn_load.wait()
    y_copy.start()

    def narrow_chunk(p):
        c = n_wide + p
        slot = lax.rem(c, 2)
        core_copy(c - 2).wait_send()
        cols = pl.ds(pl.multiple_of(p * SPLIT, SPLIT), SPLIT)
        o_cols = pl.ds(pl.multiple_of(p * (CHUNK - SPLIT), CHUNK - SPLIT), CHUNK - SPLIT)
        for which, dst in ((1 - core, m.core_send), (core, m.kept)):
            put(dst, slot, slice(0, SPLIT), dot_tn(m.packed[0, which], m.g_v[:, cols]))
            put(dst, slot, slice(SPLIT, CHUNK), dot_tn(m.packed[1, which], m.o_v[:, o_cols]))
        core_copy(c).start()

    def place(block):
        return pl.ds(pl.multiple_of(lax.rem(block + t * (nb // 2), nb) * BLOCK, BLOCK), BLOCK)

    m.qgain[...] = jnp.zeros_like(m.qgain)
    m.kgain[...] = jnp.zeros_like(m.kgain)

    def attention_phase(qx, dox, kx0, kx1, vx0, vx1, kt, dqt, dk0, dk1, dv0, dv1, dks, dvs):
        all_low = lane_of((2 * rows, PAIR)) < 64
        one = jnp.ones((2 * rows, PAIR), F32)
        zero = jnp.zeros((2 * rows, PAIR), BF16)
        qx[:, PAIR:] = m.segq[...]
        kx0[:, PAIR:] = m.segk[...]
        kx1[:, PAIR:] = m.segk[...]
        vx0[:, PAIR:] = jnp.where(all_low, -one, 0.0).astype(BF16)
        vx1[:, PAIR:] = jnp.where(all_low, 0.0, -one).astype(BF16)

        def step(qb, kb, diagonal):
            qs, ks = place(qb), place(kb)
            q, do = qx[qs, :], dox[qs, :]
            for h, (kx, vx, dk, dv) in enumerate(((kx0, vx0, dk0, dv0), (kx1, vx1, dk1, dv1))):
                s = dot_nt(kx[ks, :], q)
                if diagonal:
                    r = lax.broadcasted_iota(jnp.int32, s.shape, 0)
                    s = jnp.where(r <= lane_of(s.shape), s, -1e30)
                e = jnp.exp2(s)
                ds = (e * dot_nt(vx[ks, :], do)).astype(BF16)
                dv[ks, :] += dot_nn(e.astype(BF16), do[:, :PAIR])
                dk[ks, :] += dot_nn(ds, q[:, :PAIR])
                dqt[h * 64 : (h + 1) * 64, qs] += dot_nn(kt[:, ks], ds)

        def group(g, carry):
            slot = lax.rem(g, 2)
            lanes = pl.ds(pl.multiple_of(g * PAIR, PAIR), PAIR)
            p = g // 2
            wait(tiles(g))

            @pl.when(g + 1 < 4)
            def _():
                start(tiles(g + 1))

            qx[:, :PAIR] = m.q_v[slot]
            k, v = m.kd_v[slot], m.vd_v[slot]
            kx0[:, :PAIR] = jnp.where(all_low, k, zero)
            kx1[:, :PAIR] = jnp.where(all_low, zero, k)
            vx0[:, :PAIR] = jnp.where(all_low, v, zero)
            vx1[:, :PAIR] = jnp.where(all_low, zero, v)
            kt[...] = jnp.transpose(k.astype(F32))[:64, :].astype(BF16)
            for at, do_ref in ((own_rows, m.do_v), (oth_rows, m.do_recv)):
                scaled = do_ref[:, lanes].astype(F32) * m.linv_v[slot, at, :]
                dox[at, :PAIR] = scaled.astype(BF16)
                dox[at, PAIR:] = (scaled * m.o_v[at, lanes].astype(F32)).astype(BF16)
            for ref in (dqt, dk0, dk1, dv0, dv1):
                ref[...] = jnp.zeros_like(ref)

            def q_body(qb, c):
                step(qb, qb, True)

                def k_body(kb, cc):
                    step(qb, kb, False)
                    return cc

                lax.fori_loop(jnp.maximum(qb - 2, 0), qb, k_body, 0)
                return c

            lax.fori_loop(0, nb, q_body, 0)

            @pl.when(g == 1)
            def _():
                tick(4)

            g_lanes = pl.ds(pl.multiple_of(p * SPLIT + slot * PAIR, PAIR), PAIR)
            for at in (own_rows, oth_rows):
                dq = jnp.transpose(dqt[:, at]) * 0.125
                normed_grad = rope(dq, m.cos[at, :], -m.sin[at, :])
                raw = m.qraw_v[slot, at, :].astype(F32)
                inverse = lax.rsqrt(head_mean(raw * raw) + EPS)
                u = raw * inverse
                m.qgain[...] += jnp.sum(normed_grad * u, axis=0, keepdims=True)
                w = normed_grad * m.qg[...]
                m.g_v[at, g_lanes] = (inverse * (w - u * head_mean(w * u))).astype(BF16)

            def gathered(a, b, at):
                joined = jnp.where(low, a[at, :], b[at, :])
                return joined + pltpu.roll(joined, 64, 1)

            @pl.when(slot == 0)
            def _():
                for at in (own_rows, oth_rows):
                    dks[at, :] = gathered(dk0, dk1, at)
                    dvs[at, :] = gathered(dv0, dv1, at)

            @pl.when(slot == 1)
            def _():
                k_lanes = pl.ds(pl.multiple_of(p * SPLIT + 2 * PAIR, PAIR), PAIR)
                v_lanes = pl.ds(pl.multiple_of(p * SPLIT + 3 * PAIR, PAIR), PAIR)
                raw_lanes = pl.ds(pl.multiple_of(p * PAIR, PAIR), PAIR)
                for at in (own_rows, oth_rows):
                    dk = jnp.where(low, dks[at, :], gathered(dk0, dk1, at)) * LN2
                    dv = jnp.where(low, dvs[at, :], gathered(dv0, dv1, at))
                    normed_grad = rope(dk, m.cos[at, :], -m.sin[at, :])
                    raw = m.kraw_v[at, raw_lanes].astype(F32)
                    inverse = lax.rsqrt(head_mean(raw * raw) + EPS)
                    u = raw * inverse
                    m.kgain[...] += jnp.sum(normed_grad * u, axis=0, keepdims=True)
                    w = normed_grad * m.kg[...]
                    m.g_v[at, k_lanes] = (inverse * (w - u * head_mean(w * u))).astype(BF16)
                    m.g_v[at, v_lanes] = dv.astype(BF16)

                @pl.when(p == 0)
                def _():
                    branch_copy.wait_recv()
                    pack_columns(m.packed.at[1], 0, m.branch_v)
                    pack_columns(m.packed.at[1], rows, m.branch_recv)

                narrow_chunk(p)

            @pl.when(g == 2)
            def _():
                add_core(n_wide)

            tick(3 + g + jnp.minimum(g, 1))
            return carry

        lax.fori_loop(0, 4, group, 0)

    pl.run_scoped(
        attention_phase,
        *[pltpu.VMEM((2 * rows, 2 * PAIR), BF16)] * 6,
        pltpu.VMEM((64, 2 * rows), BF16), pltpu.VMEM((PAIR, 2 * rows), F32),
        *[pltpu.VMEM((2 * rows, PAIR), F32)] * 6,
    )

    def attn_in_grad(at):
        out = None
        qc, kc = m.wq_v.shape[1], m.wkv_v.shape[1] // 2
        for p in range(2):
            for ref, base, begin, size in (
                (m.wq_v, 0, 0, 2 * PAIR), (m.wkv_v, 0, 2 * PAIR, PAIR), (m.wkv_v, kc, 3 * PAIR, PAIR)
            ):
                term = dot_nt(
                    m.g_v[at, p * SPLIT + begin : p * SPLIT + begin + size],
                    ref[:, base + p * size : base + (p + 1) * size],
                )
                out = term if out is None else out + term
        return out

    def end_phase(ga_own, tok_v):
        start(both(0, m.tok_own, m.tok_oth, tok_v))
        wait(both(0, m.tok_own, m.tok_oth, tok_v))

        def grad_and_gain(at):
            grad = attn_in_grad(at)
            tokens = tok_v[at, :].astype(F32)
            return grad, jnp.sum(grad * (tokens * row_norm(tokens)), axis=0, keepdims=True)

        branch_copy.wait_send()
        total = jnp.zeros((1, width), F32)
        for i in range(rows // BLOCK):
            grad, part = grad_and_gain(pl.ds(rows + i * BLOCK, BLOCK))
            m.branch_v[i * BLOCK : (i + 1) * BLOCK, :] = grad.astype(BF16)
            total += part
        ga_copy.start()
        add_core(n_chunks - 1)
        start(first_copies(n_chunks - 1))
        tick(n_chunks - 3)
        for i in range(rows // BLOCK):
            grad, part = grad_and_gain(pl.ds(i * BLOCK, BLOCK))
            ga_own[i * BLOCK : (i + 1) * BLOCK, :] = grad.astype(BF16)
            total += part
        ga_out_copy = local(3, ga_own, m.ga_out)
        ga_out_copy.start()
        for r in range(width // PAIR):
            m.mine[r : r + 1, :] = total[:, r * PAIR : (r + 1) * PAIR]
            at = slice(width // PAIR + r, width // PAIR + r + 1)
            m.mine[at, :] = m.gain_ffn[:, r * PAIR : (r + 1) * PAIR]
        last = 2 * width // PAIR
        m.mine[last : last + 1, :] = m.qgain[...]
        m.mine[last + 1 : last + 2, :] = m.kgain[...]
        m.mine[last + 2 :, :] = jnp.zeros((m.mine.shape[0] - last - 2, PAIR), F32)

        def gain_copy(i, device):
            return pltpu.make_async_remote_copy(
                src_ref=m.gain_out.at[i], dst_ref=m.gain_in.at[i], send_sem=m.gain_sem.at[0, i],
                recv_sem=m.gain_sem.at[1, i], device_id=device, device_id_type=MESH,
            )

        for i, device in enumerate(partners):
            m.gain_out[i] = m.mine[...]
            gain_copy(i, device).start()
            if i >= 1:
                tick(n_chunks - 3 + i)
            gain_copy(i, device).wait_recv()
            m.mine[...] += m.gain_in[i]
        m.gains[...] = m.mine[...]
        y_copy.wait_recv()
        ga_copy.wait_recv()
        for copy in (do_copy, y_copy, ga_copy):
            copy.wait_send()
        for i, device in enumerate(partners):
            gain_copy(i, device).wait_send()
        for c in (n_chunks - 2, n_chunks - 1):
            core_copy(c).wait_send()

        def drain(c, carry):
            for copy in (*first_copies(c), *second_copies(c), third_copy(c)):
                copy.wait_send()
            return carry

        lax.fori_loop(0, n_chunks, drain, 0)
        for c in (n_chunks - 2, n_chunks - 1):
            total_copy(c).wait()
        ga_out_copy.wait()

    pl.run_scoped(end_phase, pltpu.VMEM((rows, width), BF16), pltpu.VMEM((2 * rows, width), BF16))


def back(n_dp, values, tables):
    rows, width = values["tok_own"].shape
    hidden = values["h"].shape[3]
    seq = 2 * rows
    qc = values["w_q"].shape[1]
    n_chunks = 3 * hidden // CHUNK + 2
    block = width // n_dp
    vm = pltpu.VMEM
    dma = pltpu.SemaphoreType.DMA
    scratch = dict(
        packed=vm((2, 2, seq, width // 2), BF16),
        core_send=vm((2, 2, 2, 2, block, CHUNK), BF16), kept=vm((2, 2, 2, 2, block, CHUNK), BF16),
        sums=vm((n_chunks, 2, 2, 2, block, CHUNK), BF16),
        r1a=vm((n_chunks, 2, 2, block, SPLIT), BF16), r1b=vm((n_chunks, 2, 2, block, CHUNK - SPLIT), BF16),
        r2a=vm((n_chunks, 2, block, SPLIT), BF16), r2b=vm((n_chunks, 2, block, CHUNK - SPLIT), BF16),
        r3=vm((n_chunks, block, CHUNK), BF16), totals=vm((2, block, CHUNK), F32),
        wq_v=vm((width, qc), BF16), wkv_v=vm((width, qc), BF16),
        o_v=vm((seq, qc), BF16), kraw_v=vm((seq, qc // 2), BF16),
        q_v=vm((2, seq, PAIR), BF16), kd_v=vm((2, seq, PAIR), BF16), vd_v=vm((2, seq, PAIR), BF16),
        qraw_v=vm((2, seq, PAIR), BF16), linv_v=vm((2, seq, PAIR), F32),
        g_v=vm((seq, 2 * SPLIT), BF16), do_v=vm((rows, qc), BF16),
        do_recv=vm((rows, qc), BF16),
        branch_v=vm((rows, width), BF16), branch_recv=vm((rows, width), BF16),
        qgain=vm((1, PAIR), F32), kgain=vm((1, PAIR), F32), mine=vm((24, PAIR), F32),
        gain_out=vm((5, 24, PAIR), F32), gain_in=vm((5, 24, PAIR), F32),
        t_send=dma((5,)), t_recv=dma((5,)), rs_send=dma((6, n_chunks)), rs_recv=dma((6, n_chunks)),
        l_sem=dma((14,)), g_sem=dma((2, 10)), h_sem=dma((2, 2)), s_sem=dma((2,)), gain_sem=dma((2, 5)),
    )
    anywhere = pl.BlockSpec(memory_space=pl.ANY)
    vmem = pl.BlockSpec(memory_space=pltpu.VMEM)
    return pl.pallas_call(
        functools.partial(back_kernel, n_dp, tuple(scratch)),
        in_specs=[anywhere] * len(BACK_INPUTS) + [vmem] * len(BACK_TABLES),
        out_specs=[anywhere, anywhere, anywhere, vmem, anywhere],
        out_shape=[
            jax.ShapeDtypeStruct((rows, width), BF16),
            jax.ShapeDtypeStruct((rows, width), BF16),
            jax.ShapeDtypeStruct((n_chunks, block, CHUNK), F32), jax.ShapeDtypeStruct((24, PAIR), F32),
            jax.ShapeDtypeStruct((rows, width), BF16),
        ],
        scratch_shapes=list(scratch.values()),
        compiler_params=pltpu.CompilerParams(
            vmem_limit_bytes=BACK_VMEM, collective_id=0, has_side_effects=True
        ),
        cost_estimate=cost(100e-6),
        name="back",
    )(*[values[k] for k in BACK_INPUTS], *[tables[k] for k in BACK_TABLES])


FRONT_INPUTS = (
    "tok_own", "tok_oth", "cot_own", "w_q", "w_kv", "w_o", "w_gu", "w_down",
    "q_own", "kd_own", "vd_own", "attn_own",
)
FRONT_TABLES = ("segq", "segk", "cos", "sin", "gain1", "gain2", "qg", "kg")
FRONT_OUTPUTS = (
    "q_oth", "kd_oth", "vd_oth", "qraw_oth", "kraw_oth", "o_own", "o_oth", "linv_own", "linv_oth",
    "cot_pack", "ffn_pack", "attn_pack", "h", "base", "y_send", "branch", "do_own", "do_send",
    "gain_ffn",
)
PIECES = 4


def front_kernel(scratch_names, *refs):
    m = Names(FRONT_INPUTS + FRONT_TABLES + FRONT_OUTPUTS + scratch_names, refs)
    rows, width = m.tok_own.shape
    hidden = m.w_down.shape[0]
    qc = m.w_q.shape[1]
    kc = m.w_kv.shape[1] // 2
    nb = 2 * rows // BLOCK
    t = lax.axis_index("tensor")
    d = lax.axis_index("dp")
    core = lax.rem(d, 2)
    x_at = lax.rem(d // 2, 2)
    over_x = {"dp": d + 2 - 4 * x_at}
    over_t = {"tensor": 1 - t}
    over_core = {"dp": d + 1 - 2 * core}

    barrier = pltpu.get_barrier_semaphore()
    for p in (over_t, over_core, over_x):
        pl.semaphore_signal(barrier, inc=1, device_id=p, device_id_type=MESH)
    pl.semaphore_wait(barrier, 3)

    def remote(i, src, dst, device):
        return pltpu.make_async_remote_copy(
            src_ref=src, dst_ref=dst, send_sem=m.r_send.at[i], recv_sem=m.r_recv.at[i],
            device_id=device, device_id_type=MESH,
        )

    pieces = [pl.ds(i * (rows // PIECES), rows // PIECES) for i in range(PIECES)]
    halves = [pl.ds(i * BLOCK, BLOCK) for i in range(rows // BLOCK)]
    cot_copies = [remote(i, m.cot_own.at[at], m.cot_v.at[1, at], over_t) for i, at in enumerate(pieces)]
    part_o = qc // 4

    def wo_part(x_of, core_of):
        return pl.ds(pl.multiple_of((2 * x_of + core_of) * part_o, part_o), part_o)

    mine_o, core_o = wo_part(x_at, core), wo_part(x_at, 1 - core)
    wo_copy = remote(4, m.w_o.at[mine_o], m.wot_v.at[mine_o], over_t)
    wo_core = remote(5, m.wot_v.at[mine_o], m.wot_v.at[mine_o], over_core)
    wo_x = (
        remote(11, m.wot_v.at[mine_o], m.wot_v.at[mine_o], over_x),
        remote(12, m.wot_v.at[core_o], m.wot_v.at[core_o], over_x),
    )
    o_copy = remote(6, m.o_v.at[1], m.theirs, over_t)
    ffn_copies = [remote(7 + i, m.ffn_v.at[0, at], m.ffn_v.at[1, at], over_t) for i, at in enumerate(halves)]
    gf_copies = [remote(9 + i, m.gf_send.at[at], m.gf_in.at[at], over_t) for i, at in enumerate(halves)]

    def local(i, src, dst):
        return pltpu.make_async_copy(src, dst, m.l_sem.at[i])

    loads = [
        local(i, src, dst)
        for i, (src, dst) in enumerate((
            (m.tok_oth, m.tok_v.at[1]), (m.w_q, m.wq_v), (m.w_kv, m.wkv_v), (m.q_own, m.q_v.at[0]),
            (m.kd_own, m.kd_v.at[0]), (m.vd_own, m.vd_v.at[0]), (m.w_o, m.wom_v), (m.tok_own, m.tok_v.at[0]),
            (m.attn_own, m.attn_v.at[0]), (m.cot_own, m.cot_v.at[0]), (m.w_gu, m.wgu_v), (m.w_down, m.wd_v),
        ))
    ]
    out_sem = [0]
    stores = []

    def store(src, dst):
        copy = pltpu.make_async_copy(src, dst, m.o_sem.at[out_sem[0]])
        out_sem[0] += 1
        copy.start()
        stores.append(copy)

    wo_copy.start()
    for copy in cot_copies[:3]:
        copy.start()
    for copy in loads:
        copy.start()
    for copy in loads[:6]:
        copy.wait()

    for at in halves:
        table = pl.ds(rows + at.start, BLOCK)
        qkv_kernel(
            m.tok_v.at[1, at], m.gain1, m.wq_v, m.wkv_v.at[:, pl.ds(0, kc)], m.wkv_v.at[:, pl.ds(kc, kc)],
            m.qg, m.kg, m.cos.at[table], m.sin.at[table],
            m.attn_v.at[1, at], m.q_v.at[1, at], m.kd_v.at[1, at], m.vd_v.at[1, at], m.qraw_v.at[at], m.kraw_v.at[at],
        )
    for src, dst in (
        (m.q_v.at[1], m.q_oth), (m.kd_v.at[1], m.kd_oth), (m.vd_v.at[1], m.vd_oth),
        (m.qraw_v, m.qraw_oth), (m.kraw_v, m.kraw_oth),
    ):
        store(src, dst)
    wo_copy.wait_recv()
    wo_core.start()
    wo_x[0].start()

    def place(block):
        return pl.ds(pl.multiple_of(lax.rem(block + t * (nb // 2), nb) * BLOCK, BLOCK), BLOCK)

    def attention_phase(kx0, kx1, vx0, vx1, acc):
        both = lane_of((2 * rows, PAIR)) < 64
        one = jnp.ones((2 * rows, PAIR), F32)
        low = lane_of((rows, PAIR)) < 64
        zero = jnp.zeros((rows, PAIR), BF16)
        kx0[:, PAIR:] = m.segk[...]
        kx1[:, PAIR:] = m.segk[...]
        vx0[:, PAIR:] = jnp.where(both, one, 0.0).astype(BF16)
        vx1[:, PAIR:] = jnp.where(both, 0.0, one).astype(BF16)

        def half(which, carry):
            part = 1 - which
            first = lax.rem(part + t, 2) * (nb // 2)

            def group(g, carry):
                lanes = pl.ds(pl.multiple_of(g * PAIR, PAIR), PAIR)
                for i in range(2):
                    at = pl.ds(i * rows, rows)
                    k, v = m.kd_v[i, :, lanes], m.vd_v[i, :, lanes]
                    kx0[at, :PAIR] = jnp.where(low, k, zero)
                    kx1[at, :PAIR] = jnp.where(low, zero, k)
                    vx0[at, :PAIR] = jnp.where(low, v, zero)
                    vx1[at, :PAIR] = jnp.where(low, zero, v)

                def q_block(i, c):
                    at = pl.ds(pl.multiple_of(i * BLOCK, BLOCK), BLOCK)
                    seg_at = pl.ds(pl.multiple_of(part * rows + i * BLOCK, BLOCK), BLOCK)
                    q = jnp.concatenate([m.q_v[part, at, lanes], m.segq[seg_at, :]], axis=1)
                    block = first + i

                    def step(kb, diagonal):
                        here = place(kb)
                        total = None
                        for kx, vx in ((kx0, vx0), (kx1, vx1)):
                            s = dot_nt(q, kx[here, :])
                            if diagonal:
                                r = lax.broadcasted_iota(jnp.int32, s.shape, 0)
                                s = jnp.where(lane_of(s.shape) <= r, s, -1e30)
                            term = dot_nn(jnp.exp2(s).astype(BF16), vx[here, :])
                            total = term if total is None else total + term
                        return total

                    acc[...] = step(block, True)

                    def body(kb, c):
                        acc[...] += step(kb, False)
                        return c

                    lax.fori_loop(jnp.maximum(block - 2, 0), block, body, 0)
                    inverse = 1.0 / acc[:, PAIR:]
                    m.o_v[part, at, lanes] = (acc[:, :PAIR] * inverse).astype(BF16)
                    m.linv_v[part, at, lanes] = inverse
                    return c

                lax.fori_loop(0, rows // BLOCK, q_block, 0)
                return carry

            lax.fori_loop(0, qc // PAIR, group, 0)

            @pl.when(which == 0)
            def _():
                o_copy.start()
                wo_core.wait_recv()
                wo_x[1].start()
                cot_copies[3].start()

            return carry

        lax.fori_loop(0, 2, half, 0)

    pl.run_scoped(
        attention_phase, *[pltpu.VMEM((2 * rows, 2 * PAIR), BF16)] * 4, pltpu.VMEM((BLOCK, 2 * PAIR), F32)
    )
    for src, dst in (
        (m.o_v.at[0], m.o_own), (m.o_v.at[1], m.o_oth), (m.linv_v.at[0], m.linv_own), (m.linv_v.at[1], m.linv_oth)
    ):
        store(src, dst)

    for copy in loads[6:9]:
        copy.wait()
    pack_columns(m.ffn_pack_v, 0, m.attn_v.at[0])
    pack_columns(m.ffn_pack_v, rows, m.attn_v.at[1])
    attn_store = local(12, m.ffn_pack_v, m.attn_pack)
    attn_store.start()
    for copy in wo_x:
        copy.wait_recv()
    o_copy.wait_recv()
    for i, at in enumerate(halves):
        resid = (
            m.tok_v[0, at, :].astype(F32) + dot_nn(m.o_v[0, at, :], m.wom_v[...]) + dot_nn(m.theirs[at, :], m.wot_v[...])
        )
        m.resid_v[at, :] = resid
        m.ffn_v[0, at, :] = (resid * row_norm(resid) * m.gain2[...]).astype(BF16)
        ffn_copies[i].start()

    for copy in loads[9:]:
        copy.wait()
    n_tiles = hidden // CHUNK
    cot_store = local(13, m.cot_pack_v, m.cot_pack)

    def h_copy(slot, part, at, f):
        cols = pl.ds(pl.multiple_of(f * CHUNK, CHUNK), CHUNK)
        return pltpu.make_async_copy(m.h_v.at[slot], m.h.at[part, :, at, cols], m.h_sem.at[slot])

    def piece(n, carry):
        part = lax.rem((n + 1) // 2, 2)
        at = pl.ds(pl.multiple_of((n // 2) * BLOCK, BLOCK), BLOCK)
        to = pl.ds(pl.multiple_of((2 * part + (1 - part) * (n // 3)) * BLOCK, BLOCK), BLOCK)
        for i in range(2):
            @pl.when(n == 1 + i)
            def _():
                ffn_copies[i].wait_recv()
                if i == 0:
                    for copy in cot_copies[:2]:
                        copy.wait_recv()

        def tile(f, c):
            slot = lax.rem(n * n_tiles + f, 2)
            cols = pl.ds(pl.multiple_of(f * CHUNK, CHUNK), CHUNK)
            up_cols = pl.ds(pl.multiple_of(hidden + f * CHUNK, CHUNK), CHUNK)
            x = m.ffn_v[part, at, :]
            gate = dot_nn(x, m.wgu_v[:, cols])
            up = dot_nn(x, m.wgu_v[:, up_cols])
            grad = dot_nt(m.cot_v[part, at, :], m.wd_v[cols, :])

            @pl.when(n * n_tiles + f >= 2)
            def _():
                h_copy(slot, part, at, f).wait()

            sig = 0.5 * jnp.tanh(0.5 * gate) + 0.5
            silu = gate * sig
            mixed = (silu * up).astype(BF16)
            gg = (grad * up * (sig + silu * (1.0 - sig))).astype(BF16)
            gu = (grad * silu).astype(BF16)
            for i, value in enumerate((mixed, gg, gu)):
                m.h_v[slot, i] = value
            h_copy(slot, part, at, f).start()
            y = dot_nn(mixed, m.wd_v[cols, :])
            gf = dot_nt(gg, m.wgu_v[:, cols]) + dot_nt(gu, m.wgu_v[:, up_cols])

            @pl.when(f == 0)
            def _():
                m.y_v[to, :] = y
                m.gf_v[to, :] = gf

            @pl.when(f > 0)
            def _():
                m.y_v[to, :] += y
                m.gf_v[to, :] += gf

            return c

        lax.fori_loop(0, n_tiles, tile, 0)

        @pl.when(n == 0)
        def _():
            pack_columns(m.cot_pack_v, 0, m.cot_v.at[0])
            attn_store.wait()
            pack_columns(m.ffn_pack_v, 0, m.ffn_v.at[0])

        for i in range(2):
            @pl.when(n == 1 + i)
            def _():
                m.gf_send[halves[i], :] = m.gf_v[2 * BLOCK :, :].astype(BF16)
                gf_copies[i].start()
                m.attn_v[1, halves[i], :] = m.y_v[2 * BLOCK :, :].astype(BF16)
                if i == 0:
                    for copy in cot_copies[2:]:
                        copy.wait_recv()
                    pack_columns(m.cot_pack_v, rows, m.cot_v.at[1])
                    cot_store.start()

        return carry

    lax.fori_loop(0, 4, piece, 0)
    store(m.attn_v.at[1], m.y_send)
    pack_columns(m.ffn_pack_v, rows, m.ffn_v.at[1])
    store(m.ffn_pack_v, m.ffn_pack)

    total = jnp.zeros((1, width), F32)
    for i, at in enumerate(halves):
        gf_copies[i].wait_recv()
        grad = m.gf_v[at, :] + m.gf_in[at, :].astype(F32)
        resid = m.resid_v[at, :]
        inverse = row_norm(resid)
        normed = resid * inverse
        total += jnp.sum(grad * normed, axis=0, keepdims=True)
        w = grad * m.gain2[...]
        gres = m.cot_v[0, at, :].astype(F32) + inverse * (
            w - normed * jnp.mean(w * normed, axis=-1, keepdims=True)
        )
        branch = gres.astype(BF16)
        m.attn_v[0, at, :] = branch
        m.do_v[0, at, :] = dot_nt(branch, m.wom_v[...]).astype(BF16)
        m.do_v[1, at, :] = dot_nt(branch, m.wot_v[...]).astype(BF16)
        m.tok_v[0, at, :] = (m.y_v[at, :] + resid).astype(BF16)
    for src, dst in (
        (m.do_v.at[1], m.do_send), (m.do_v.at[0], m.do_own), (m.attn_v.at[0], m.branch),
        (m.tok_v.at[0], m.base),
    ):
        store(src, dst)
    m.gain_ffn[...] = total
    for copy in (*cot_copies, wo_copy, wo_core, *wo_x, o_copy, *ffn_copies, *gf_copies):
        copy.wait_send()
    for slot in range(2):
        pltpu.make_async_copy(m.h_v.at[slot], m.h.at[0, :, halves[1], pl.ds(0, CHUNK)], m.h_sem.at[slot]).wait()
    cot_store.wait()
    for copy in stores:
        copy.wait()


def front(values, tables):
    rows, width = values["tok_own"].shape
    hidden = values["w_down"].shape[0]
    qc = values["w_q"].shape[1]
    seq = 2 * rows
    vm = pltpu.VMEM
    dma = pltpu.SemaphoreType.DMA
    scratch = dict(
        tok_v=vm((2, rows, width), BF16), cot_v=vm((2, rows, width), BF16),
        wq_v=vm((width, qc), BF16), wkv_v=vm((width, qc), BF16), wom_v=vm((qc, width), BF16), wot_v=vm((qc, width), BF16),
        wgu_v=vm((width, 2 * hidden), BF16), wd_v=vm((hidden, width), BF16),
        q_v=vm((2, rows, qc), BF16), kd_v=vm((2, rows, qc), BF16), vd_v=vm((2, rows, qc), BF16),
        attn_v=vm((2, rows, width), BF16), qraw_v=vm((rows, qc), BF16), kraw_v=vm((rows, qc // 2), BF16),
        o_v=vm((2, rows, qc), BF16), linv_v=vm((2, rows, qc), F32), theirs=vm((rows, qc), BF16),
        resid_v=vm((rows, width), F32), ffn_v=vm((2, rows, width), BF16),
        h_v=vm((2, 3, BLOCK, CHUNK), BF16), y_v=vm((3 * BLOCK, width), F32), gf_v=vm((3 * BLOCK, width), F32),
        gf_send=vm((rows, width), BF16), gf_in=vm((rows, width), BF16),
        cot_pack_v=vm((2, seq, width // 2), BF16),
        ffn_pack_v=vm((2, seq, width // 2), BF16), do_v=vm((2, rows, qc), BF16),
        r_send=dma((13,)), r_recv=dma((13,)), l_sem=dma((14,)), o_sem=dma((20,)), h_sem=dma((2,)),
    )
    anywhere = pl.BlockSpec(memory_space=pl.ANY)
    vmem = pl.BlockSpec(memory_space=pltpu.VMEM)
    low, full = (lambda *shape: jax.ShapeDtypeStruct(shape, BF16)), (lambda *shape: jax.ShapeDtypeStruct(shape, F32))
    shapes = dict(
        q_oth=low(rows, qc), kd_oth=low(rows, qc), vd_oth=low(rows, qc),
        qraw_oth=low(rows, qc), kraw_oth=low(rows, qc // 2), o_own=low(rows, qc), o_oth=low(rows, qc),
        linv_own=full(rows, qc), linv_oth=full(rows, qc),
        cot_pack=low(2, seq, width // 2), ffn_pack=low(2, seq, width // 2), attn_pack=low(2, seq, width // 2),
        h=low(2, 3, rows, hidden), base=low(rows, width), y_send=low(rows, width),
        branch=low(rows, width), do_own=low(rows, qc), do_send=low(rows, qc),
        gain_ffn=full(1, width),
    )
    outs = pl.pallas_call(
        functools.partial(front_kernel, tuple(scratch)),
        in_specs=[anywhere] * len(FRONT_INPUTS) + [vmem] * len(FRONT_TABLES),
        out_specs=[anywhere] * (len(FRONT_OUTPUTS) - 1) + [vmem],
        out_shape=[shapes[k] for k in FRONT_OUTPUTS],
        scratch_shapes=list(scratch.values()),
        compiler_params=pltpu.CompilerParams(
            vmem_limit_bytes=BACK_VMEM, collective_id=1, has_side_effects=True
        ),
        cost_estimate=cost(100e-6),
        name="front",
    )(*[values[k] for k in FRONT_INPUTS], *[tables[k] for k in FRONT_TABLES])
    return dict(zip(FRONT_OUTPUTS, outs))


def finish_kernel(
    base_ref, yr_ref, ga_ref, gr_ref, x_ref, gres_ref, gain_ref, shards_ref, gains_ref,
    out_ref, gt_ref, q_ref, kv_ref, o_ref, g1_ref, g2_ref, gq_ref, gk_ref, gu_ref, down_ref,
):
    out_ref[...] = (base_ref[...].astype(F32) + yr_ref[...].astype(F32)).astype(BF16)
    x = x_ref[...].astype(F32)
    inverse = row_norm(x)
    normed = x * inverse
    w = (ga_ref[...].astype(F32) + gr_ref[...].astype(F32)) * gain_ref[...]
    gt_ref[...] = gres_ref[...].astype(F32) + inverse * (w - normed * jnp.mean(w * normed, axis=-1, keepdims=True))
    n_chunks = shards_ref.shape[0]
    per_x = (n_chunks - 2) // 3
    two = 2 * PAIR
    step = pl.program_id(0)

    @pl.when(step < per_x)
    def _():
        down_ref[...] = shards_ref[step]
        gu_ref[:, 0, :] = shards_ref[per_x + step]
        gu_ref[:, 1, :] = shards_ref[2 * per_x + step]

    @pl.when(step == per_x)
    def _():
        n = g1_ref.shape[0]
        g1_ref[...] = gains_ref[:n, :]
        g2_ref[...] = gains_ref[n : 2 * n, :]
        for i, ref in enumerate((gq_ref, gk_ref)):
            row = gains_ref[2 * n + i : 2 * n + i + 1, :]
            ref[...] = row[:, :64] + row[:, 64:]
        for p in range(2):
            shard = shards_ref[3 * per_x + p]
            q_ref[:, p * two : (p + 1) * two] = shard[:, :two]
            kv_ref[:, 0, p * PAIR : (p + 1) * PAIR] = shard[:, two : two + PAIR]
            kv_ref[:, 1, p * PAIR : (p + 1) * PAIR] = shard[:, two + PAIR : 2 * two]
            o_ref[:, p * two : (p + 1) * two] = shard[:, 2 * two :]


def finish(base, y_recv, ga_own, ga_recv, x, gres, gain, shards, gains):
    rows, width = x.shape
    n_chunks, block, _ = shards.shape
    hidden = (n_chunks - 2) // 3 * CHUNK
    per_x = hidden // CHUNK
    row = pl.BlockSpec((rows // (per_x + 1), width), lambda i: (i, 0))
    fixed = lambda shape: pl.BlockSpec(shape, lambda i: (0,) * len(shape))
    m = width // PAIR
    shapes = [(block, SPLIT), (block, 2, SPLIT // 2), (block, SPLIT), (m, PAIR), (m, PAIR), (1, 64), (1, 64)]
    shapes += [(block, 2, hidden), (block, hidden)]
    piece = lambda i: jnp.minimum(i, per_x - 1)
    return pl.pallas_call(
        finish_kernel,
        grid=(per_x + 1,),
        in_specs=[row] * 6 + [fixed((1, width)), fixed(shards.shape), fixed(gains.shape)],
        out_specs=[row, row]
        + [fixed(shape) for shape in shapes[:7]]
        + [
            pl.BlockSpec((block, 2, CHUNK), lambda i: (0, 0, piece(i))),
            pl.BlockSpec((block, CHUNK), lambda i: (0, piece(i))),
        ],
        out_shape=[jax.ShapeDtypeStruct((rows, width), BF16), jax.ShapeDtypeStruct((rows, width), F32)]
        + [jax.ShapeDtypeStruct(shape, F32) for shape in shapes],
        compiler_params=pltpu.CompilerParams(vmem_limit_bytes=VMEM_LIMIT),
        cost_estimate=cost(6e-6),
        name="finish",
    )(base, y_recv, ga_own, ga_recv, x, gres, gain, shards, gains)


def swap(value, axis, size, bit):
    return lax.ppermute(value, axis, [(i, i ^ bit) for i in range(size)])


def after(value, *others):
    return lax.optimization_barrier((value,) + others)[0]


def paired(
    n_dp, tokens, doc_ids, gain_attn, w_q, w_kv, q_gain, k_gain, w_o, gain_ffn, w_gu, w_down, cotangent
):
    rows, width = tokens.shape
    head_dim = q_gain.shape[0]
    hidden = w_down.shape[0]
    seq = doc_ids.shape[1]
    t = lax.axis_index("tensor")
    over = functools.partial(swap, axis="tensor", size=2, bit=1)

    tokens_oth = over(tokens)

    segment = doc_ids[0]
    segment = jnp.where(t == 0, segment, jnp.roll(segment, rows))
    lanes = jnp.arange(PAIR, dtype=jnp.int32)[None, :]
    match = lanes == segment[:, None]
    marker = lanes == 8
    segk = (match | marker).astype(BF16)
    segq = (jnp.where(match, SAME, 0.0) - jnp.where(marker, SAME, 0.0)).astype(BF16)
    half_dim = head_dim // 2
    frequency = jnp.exp(-math.log(THETA) * 2.0 * jnp.arange(half_dim, dtype=F32) / head_dim)
    position = (jnp.arange(seq, dtype=jnp.int32) + t * rows) % seq
    angles = position.astype(F32)[:, None] * frequency[None, :]
    cos, sin = jnp.cos(angles), jnp.sin(angles)
    cosine = jnp.concatenate([cos] * 4, axis=1)
    sine = jnp.concatenate([-sin, sin] * 2, axis=1)
    gain1, gain2 = gain_attn.reshape(1, width), gain_ffn.reshape(1, width)
    qg = jnp.concatenate([q_gain, q_gain]).reshape(1, PAIR)
    kg = jnp.concatenate([k_gain, k_gain]).reshape(1, PAIR)
    w_kv = w_kv.reshape(width, -1)
    w_gu = w_gu.reshape(width, 2 * hidden)
    tables = dict(segq=segq, segk=segk, cos=cosine, sin=sine, gain1=gain1, gain2=gain2, qg=qg, kg=kg)

    attn_own, q_own, kd_own, vd_own, qraw_own, kraw_own = qkv(
        tokens, gain1, w_q, w_kv, qg, kg, cosine, sine, 0
    )
    values = dict(
        tok_own=tokens, tok_oth=tokens_oth, cot_own=cotangent, w_q=w_q, w_kv=w_kv, w_o=w_o, w_gu=w_gu, w_down=w_down,
        attn_own=attn_own, q_own=q_own, kd_own=kd_own, vd_own=vd_own, qraw_own=qraw_own, kraw_own=kraw_own,
    )
    values.update(front(values, tables))
    tables.update(gain_ffn=values["gain_ffn"])
    ga_own, ga_recv, shards, gains, y_recv = back(n_dp, values, tables)
    output, grad_tokens, grad_q, grad_kv, grad_o, sum_1, sum_2, sum_q, sum_k, grad_gu, grad_down = finish(
        values["base"], y_recv, ga_own, ga_recv, tokens, values["branch"], gain1, shards, gains
    )
    return (
        output,
        grad_tokens,
        sum_1.reshape(width),
        grad_q,
        grad_kv,
        sum_q.reshape(head_dim),
        sum_k.reshape(head_dim),
        grad_o.T,
        sum_2.reshape(width),
        grad_gu,
        grad_down.T,
    )


def normalize(values):
    inverse = lax.rsqrt(jnp.mean(values * values, axis=-1, keepdims=True) + EPS)
    return (values * inverse, inverse)


def norm_back(grad_normed, normed, inverse):
    return inverse * (grad_normed - normed * jnp.mean(grad_normed * normed, axis=-1, keepdims=True))


def rotate(values, cosine_table, sine_table):
    half_dim = values.shape[-1] // 2
    first_half = values[..., :half_dim]
    second_half = values[..., half_dim:]
    return jnp.concatenate(
        [
            first_half * cosine_table - second_half * sine_table,
            second_half * cosine_table + first_half * sine_table,
        ],
        -1,
    )


def shards(
    tokens, doc_ids, gain_attn, w_q, w_kv, q_gain, k_gain, w_o, gain_ffn, w_gu, w_down, cotangent
):
    f32 = jnp.float32
    bf16 = jnp.bfloat16
    rows_dev, model_width = tokens.shape
    head_dim = q_gain.shape[0]
    q_cols = w_q.shape[1]
    q_heads = q_cols // head_dim
    kv_cols = w_kv.shape[2]
    kv_heads = kv_cols // head_dim
    group_size = q_heads // kv_heads
    hidden = w_gu.shape[2]
    seq_len = doc_ids.shape[1]
    segment = doc_ids[0]
    block_rows = min(512, seq_len)
    blocks = seq_len // block_rows
    score_scale = head_dim ** (-0.5)
    w_kv_flat = w_kv.reshape(model_width, 2 * kv_cols)
    w_gu_flat = w_gu.reshape(model_width, 2 * hidden)
    half_dim = head_dim // 2
    frequency = jnp.exp(-math.log(THETA) * 2.0 * jnp.arange(half_dim, dtype=f32) / head_dim)
    angles = jnp.arange(seq_len, dtype=f32)[:, None] * frequency[None, :]
    cosine_table = jnp.cos(angles)[:, None, :]
    sine_table = jnp.sin(angles)[:, None, :]
    key_pos = jnp.arange(seq_len, dtype=jnp.int32)
    x_float = tokens.astype(f32)
    normed1, inverse1 = normalize(x_float)
    attn_in = (normed1 * gain_attn).astype(bf16)
    attn_all = lax.all_gather(attn_in, "tensor", axis=0, tiled=True)
    q_raw = jnp.dot(attn_all, w_q, preferred_element_type=f32).reshape(seq_len, q_heads, head_dim)
    kv_raw = jnp.dot(attn_all, w_kv_flat, preferred_element_type=f32).reshape(
        seq_len, 2, kv_heads, head_dim
    )
    q_normed, q_inverse = normalize(q_raw)
    k_normed, k_inverse = normalize(kv_raw[:, 0])
    queries = rotate(q_normed * q_gain, cosine_table, sine_table).astype(bf16)
    queries = queries.reshape(seq_len, kv_heads, group_size, head_dim)
    keys = rotate(k_normed * k_gain, cosine_table, sine_table).astype(bf16)
    values_low = kv_raw[:, 1].astype(bf16)

    def scores_of(first_row):
        q_block = lax.dynamic_slice_in_dim(queries, first_row, block_rows, 0)
        seg_block = lax.dynamic_slice_in_dim(segment, first_row, block_rows, 0)
        raw_scores = (
            jnp.einsum("qhgd,thd->hgqt", q_block, keys, preferred_element_type=f32) * score_scale
        )
        query_pos = first_row + jnp.arange(block_rows, dtype=jnp.int32)
        allowed = (key_pos[None, :] <= query_pos[:, None]) & (
            seg_block[:, None] == segment[None, :]
        )
        return (jnp.where(allowed, raw_scores, -1e30), q_block)

    def attend(first_row):
        masked, q_block = scores_of(first_row)
        row_max = jnp.max(masked, axis=-1, keepdims=True)
        exponent = jnp.exp(masked - row_max)
        denominator = jnp.sum(exponent, axis=-1, keepdims=True)
        probs = (exponent / denominator).astype(bf16)
        attended_block = jnp.einsum("hgqt,thd->qhgd", probs, values_low, preferred_element_type=f32)
        return (attended_block, (row_max + jnp.log(denominator))[..., 0])

    starts = jnp.arange(blocks, dtype=jnp.int32) * block_rows
    attended, log_sums = lax.map(attend, starts)
    attended_low = attended.reshape(seq_len, q_cols).astype(bf16)
    resid = x_float + lax.psum_scatter(
        jnp.dot(attended_low, w_o, preferred_element_type=f32),
        "tensor",
        scatter_dimension=0,
        tiled=True,
    )
    normed2, inverse2 = normalize(resid)
    ffn_in = (normed2 * gain_ffn).astype(bf16)
    ffn_all = lax.all_gather(ffn_in, "tensor", axis=0, tiled=True)
    gate_up = jnp.dot(ffn_all, w_gu_flat, preferred_element_type=f32)
    gate_part = gate_up[:, :hidden]
    up_part = gate_up[:, hidden:]
    sigmoid_gate = jax.nn.sigmoid(gate_part)
    silu_gate = gate_part * sigmoid_gate
    mixed = (silu_gate * up_part).astype(bf16)
    result = resid + lax.psum_scatter(
        jnp.dot(mixed, w_down, preferred_element_type=f32).astype(jnp.bfloat16),
        "tensor",
        scatter_dimension=0,
        tiled=True,
    ).astype(jnp.float32)
    output = result.astype(bf16)
    grad_all = lax.all_gather(cotangent, "tensor", axis=0, tiled=True)
    grad_down = jnp.einsum("sf,sd->fd", mixed, grad_all, preferred_element_type=f32)
    grad_mixed = jnp.einsum("sd,fd->sf", grad_all, w_down, preferred_element_type=f32)
    grad_gate = grad_mixed * up_part * sigmoid_gate * (1.0 + gate_part * (1.0 - sigmoid_gate))
    grad_up = grad_mixed * silu_gate
    grad_gu = jnp.concatenate([grad_gate, grad_up], 1).astype(bf16)
    grad_w_gu = jnp.einsum("sd,sf->df", ffn_all, grad_gu, preferred_element_type=f32).reshape(
        model_width, 2, hidden
    )
    grad_ffn_in = lax.psum_scatter(
        jnp.einsum("sf,df->sd", grad_gu, w_gu_flat, preferred_element_type=f32).astype(
            jnp.bfloat16
        ),
        "tensor",
        scatter_dimension=0,
        tiled=True,
    ).astype(jnp.float32)
    gain_ffn_part = jnp.sum(grad_ffn_in * normed2, axis=0)
    grad_resid = cotangent.astype(f32) + norm_back(grad_ffn_in * gain_ffn, normed2, inverse2)
    branch_all = lax.all_gather(grad_resid.astype(bf16), "tensor", axis=0, tiled=True)
    grad_w_o = jnp.einsum("sc,sd->cd", attended_low, branch_all, preferred_element_type=f32)
    grad_attended = jnp.einsum("sd,cd->sc", branch_all, w_o, preferred_element_type=f32).astype(
        bf16
    )
    grad_attended = grad_attended.reshape(seq_len, kv_heads, group_size, head_dim)

    def attend_back(carried, scanned):
        first_row, lse_block = scanned
        masked, q_block = scores_of(first_row)
        probs = jnp.exp(masked - lse_block[..., None])
        go_block = lax.dynamic_slice_in_dim(grad_attended, first_row, block_rows, 0)
        grad_probs = jnp.einsum("qhgd,thd->hgqt", go_block, values_low, preferred_element_type=f32)
        grad_scores = (
            probs * (grad_probs - jnp.sum(probs * grad_probs, axis=-1, keepdims=True))
        ).astype(bf16)
        keys_next = carried[0] + score_scale * jnp.einsum(
            "hgqt,qhgd->thd", grad_scores, q_block, preferred_element_type=f32
        )
        values_next = carried[1] + jnp.einsum(
            "hgqt,qhgd->thd", probs.astype(bf16), go_block, preferred_element_type=f32
        )
        grad_q_block = score_scale * jnp.einsum(
            "hgqt,thd->qhgd", grad_scores, keys, preferred_element_type=f32
        )
        return ((keys_next, values_next), grad_q_block)

    zero_kv = jnp.zeros((seq_len, kv_heads, head_dim), f32)
    (grad_keys, grad_values), grad_queries = lax.scan(
        attend_back, (zero_kv, zero_kv), (starts, log_sums)
    )
    grad_q_normed = rotate(
        grad_queries.reshape(seq_len, q_heads, head_dim), cosine_table, -sine_table
    )
    q_gain_part = jnp.sum(grad_q_normed * q_normed, axis=(0, 1))
    grad_q_raw = (
        norm_back(grad_q_normed * q_gain, q_normed, q_inverse).astype(bf16).reshape(seq_len, q_cols)
    )
    grad_k_normed = rotate(grad_keys, cosine_table, -sine_table)
    k_gain_part = jnp.sum(grad_k_normed * k_normed, axis=(0, 1))
    grad_k_raw = (
        norm_back(grad_k_normed * k_gain, k_normed, k_inverse)
        .astype(bf16)
        .reshape(seq_len, kv_cols)
    )
    grad_kv = jnp.concatenate([grad_k_raw, grad_values.astype(bf16).reshape(seq_len, kv_cols)], 1)
    grad_w_q = jnp.einsum("sd,sc->dc", attn_all, grad_q_raw, preferred_element_type=f32)
    grad_w_kv = jnp.einsum("sd,sc->dc", attn_all, grad_kv, preferred_element_type=f32).reshape(
        model_width, 2, kv_cols
    )
    grad_attn_in = lax.psum_scatter(
        (
            jnp.einsum("sc,dc->sd", grad_q_raw, w_q, preferred_element_type=f32)
            + jnp.einsum("sc,dc->sd", grad_kv, w_kv_flat, preferred_element_type=f32)
        ).astype(jnp.bfloat16),
        "tensor",
        scatter_dimension=0,
        tiled=True,
    ).astype(jnp.float32)
    gain_attn_part = jnp.sum(grad_attn_in * normed1, axis=0)
    grad_tokens = grad_resid + norm_back(grad_attn_in * gain_attn, normed1, inverse1)
    gain_sums = lax.psum(
        (gain_attn_part, gain_ffn_part, q_gain_part, k_gain_part), ("dp", "tensor")
    )
    shard_q, shard_kv, shard_o, shard_gu, shard_down = (
        lax.psum_scatter(
            grad_w_q.astype(jnp.bfloat16), "dp", scatter_dimension=0, tiled=True
        ).astype(jnp.float32),
        lax.psum_scatter(
            grad_w_kv.astype(jnp.bfloat16), "dp", scatter_dimension=0, tiled=True
        ).astype(jnp.float32),
        lax.psum_scatter(
            grad_w_o.astype(jnp.bfloat16), "dp", scatter_dimension=1, tiled=True
        ).astype(jnp.float32),
        lax.psum_scatter(
            grad_w_gu.astype(jnp.bfloat16), "dp", scatter_dimension=0, tiled=True
        ).astype(jnp.float32),
        lax.psum_scatter(
            grad_down.astype(jnp.bfloat16), "dp", scatter_dimension=1, tiled=True
        ).astype(jnp.float32),
    )
    return (
        output,
        grad_tokens,
        gain_sums[0],
        shard_q,
        shard_kv,
        gain_sums[2],
        gain_sums[3],
        shard_o,
        gain_sums[1],
        shard_gu,
        shard_down,
    )


def solution(mesh):
    in_specs = (
        P(("dp", "tensor"), None),
        P("dp", None),
        P(),
        P(None, "tensor"),
        P(None, None, "tensor"),
        P(),
        P(),
        P("tensor", None),
        P(),
        P(None, None, "tensor"),
        P("tensor", None),
        P(("dp", "tensor"), None),
    )
    out_specs = (
        P(("dp", "tensor"), None),
        P(("dp", "tensor"), None),
        P(),
        P("dp", "tensor"),
        P("dp", None, "tensor"),
        P(),
        P(),
        P("tensor", "dp"),
        P(),
        P("dp", None, "tensor"),
        P("tensor", "dp"),
    )
    paired_axes = mesh.shape["tensor"] == 2 and mesh.shape["dp"] == 16
    body = functools.partial(paired, mesh.shape["dp"]) if paired_axes else shards
    return jax.shard_map(body, mesh=mesh, in_specs=in_specs, out_specs=out_specs, check_vma=False)
```
